32 devices in a mesh: batch: 8 (over y, x, core), head: 4 (over z).
Axes of the slice: x: 2, y: 2, z: 4, core: 2. Of those that a mesh axis runs over, the one named last changes fastest.
Arguments:
- layer_input: bfloat16 [16384, 768], P(('batch', 'head')), may hold values from -6 to 6
- memory_flags: int32 [32], P('batch'), may hold values 0 or 1
- document_start: int32 [32], P('batch'), may hold values from 1 to 511
- memory_coefficients: bfloat16 [32, 256, 768], P('batch'), may hold values from -6 to 6
- first_gain: bfloat16 [768], replicated, may hold values from 0.5 to 1.5
- first_shift: bfloat16 [768], replicated, may hold values from -1 to 1
- query_weight: bfloat16 [768, 768], P(None, 'head'), may hold values from -0.3125 to 0.3125
- query_bias: bfloat16 [768], P('head'), may hold values from -1 to 1
- key_matrix: bfloat16 [768, 768], P(None, 'head'), may hold values from -0.21875 to 0.21875
- value_matrix: bfloat16 [768, 768], P(None, 'head'), may hold values from -0.21875 to 0.21875
- value_offset_bias: bfloat16 [768], P('head'), may hold values from -1 to 1
- out_weight: bfloat16 [768, 768], P('head'), may hold values from -0.875 to 0.875
- out_bias: bfloat16 [768], replicated, may hold values from -1 to 1
- second_gain: bfloat16 [768], replicated, may hold values from 0.5 to 1.5
- second_shift: bfloat16 [768], replicated, may hold values from -1 to 1
- up_weight: bfloat16 [768, 3072], P(None, 'head'), may hold values from -0.21875 to 0.21875
- up_bias: bfloat16 [3072], P('head'), may hold values from -1 to 1
- down_weight: bfloat16 [3072, 768], P('head'), may hold values from -0.109375 to 0.109375
- down_bias: bfloat16 [768], replicated, may hold values from -1 to 1
- centre_weight: float32 [12, 256], P('head'), may hold values from -0.375 to 0.375
- width_weight: float32 [12, 256], P('head'), may hold values from -0.375 to 0.375
- grad_output: bfloat16 [16384, 768], P(('batch', 'head')), may hold values from -6 to 6
Outputs:
- layer_output: bfloat16 [16384, 768], P(('batch', 'head'))
- input_grad: bfloat16 [16384, 768], P(('batch', 'head'))
- first_gain_grad: float32 [768], replicated
- first_shift_grad: float32 [768], replicated
- query_weight_grad: float32 [768, 768], P(None, 'head')
- query_bias_grad: float32 [768], P('head')
- key_weight_grad: float32 [768, 768], P(None, 'head')
- value_weight_grad: float32 [768, 768], P(None, 'head')
- value_bias_grad: float32 [768], P('head')
- out_weight_grad: float32 [768, 768], P('head')
- out_bias_grad: float32 [768], replicated
- second_gain_grad: float32 [768], replicated
- second_shift_grad: float32 [768], replicated
- up_weight_grad: float32 [768, 3072], P(None, 'head')
- up_bias_grad: float32 [3072], P('head')
- down_weight_grad: float32 [3072, 768], P('head')
- down_bias_grad: float32 [768], replicated
- centre_weight_grad: float32 [12, 256], P('head')
- width_weight_grad: float32 [12, 256], P('head')
The draws below stay inside these ranges and needn't reach their ends.
Inputs may be any that keep to these rules, and one draw needn't show every extreme that they name: `memory_flags`: 1 marks a segment with memory.
All inputs are finite; a program needn't handle non-finite values. No bound on the sum of `memory_flags` on one device may be relied on, other than what follows from the above.
Results may differ from the reference program's by a relative error of at most 0.018.
The reference program's roundings to bfloat16 on the way count: a program that leaves them out, or rounds other values in their place, can miss the bound.
Values may be sent and summed in bfloat16 or wider, within the bound.
A program may use at most 128 MiB of HBM per device.

```python
import math
from functools import partial
import jax
import jax.numpy as jnp
from jax import lax

D = 768
HEADS = 12
FF = 3072
BASIS = 256
SEQ = 512
SEG_DEV = 4
SEGS = 32
TOKENS = 16384
N_HEAD = 4


def touch_ends(entries, key, least, top_value):
    extent = entries.shape
    index_at = [jax.random.randint(jax.random.fold_in(key, axis), (), 0, extent[axis]) for axis in range(len(extent))]
    entries = entries.at[tuple(index_at)].set(least)
    longest = extent.index(max(extent))
    index_at[longest] = (index_at[longest] + 1) % extent[longest]
    return entries.at[tuple(index_at)].set(top_value)


def level_of(own_key, extent, shards, smallest, largest):
    loudness = 1.0
    for dim, shards_of in shards:
        steps = jax.random.uniform(jax.random.fold_in(jax.random.fold_in(own_key, 6), dim), (shards_of,), jnp.float32, smallest / len(shards), largest / len(shards))
        loudness = loudness * jnp.repeat(jnp.exp(steps), extent[dim] // shards_of).reshape((-1,) + (1,) * (len(extent) - 1 - dim))
    return loudness


def scatter_about(key, shape, scale, most, cuts=(), kind=jnp.bfloat16):
    result = jax.random.normal(key, shape, jnp.float32) * scale
    if len(cuts) > 0:
        result = level_of(key, shape, cuts, -0.22, 0.18) * result
    return jnp.clip(result, min=-most, max=most).astype(kind)


def setup_inputs(seed: int = 0) -> dict:
    keys = jax.random.split(jax.random.key(seed), 23)
    layer_input = scatter_about(keys[0], (TOKENS, D), 1.0, 6.0, ((0, 32),))
    memory_flags = touch_ends((jax.random.randint(keys[1], (SEGS,), 0, 2) < 1).astype(jnp.int32), jax.random.fold_in(keys[1], 1), 0, 1)
    document_start = touch_ends(jax.random.randint(keys[2], (SEGS,), 1, SEQ), jax.random.fold_in(keys[2], 1), 1, SEQ - 1).astype(jnp.int32)
    memory_coefficients = scatter_about(keys[3], (SEGS, BASIS, D), 1.0, 6.0, ((0, 8),))
    first_gain = jnp.clip(1.0 + 0.1 * jax.random.normal(keys[4], (D,), jnp.float32), 0.5, 1.5).astype(jnp.bfloat16)
    first_shift = scatter_about(keys[5], (D,), 0.2, 1.0)
    query_weight = scatter_about(keys[6], (D, D), (D // 2) ** -0.5, 0.3125, ((1, 4),))
    query_bias = scatter_about(keys[7], (D,), 0.2, 1.0, ((0, 4),))
    key_matrix = scatter_about(keys[8], (D, D), D ** -0.5, 0.21875, ((1, 4),))
    value_matrix = scatter_about(keys[9], (D, D), D ** -0.5, 0.21875, ((1, 4),))
    value_offset_bias = scatter_about(keys[10], (D,), 0.2, 1.0, ((0, 4),))
    out_weight = scatter_about(keys[11], (D, D), (D // 16) ** -0.5, 0.875, ((0, 4),))
    out_bias = scatter_about(keys[12], (D,), 0.2, 1.0)
    second_gain = jnp.clip(1.0 + 0.1 * jax.random.normal(keys[13], (D,), jnp.float32), 0.5, 1.5).astype(jnp.bfloat16)
    second_shift = scatter_about(keys[14], (D,), 0.2, 1.0)
    up_weight = scatter_about(keys[15], (D, FF), D ** -0.5, 0.21875, ((1, 4),))
    up_bias = scatter_about(keys[16], (FF,), 0.2, 1.0, ((0, 4),))
    down_weight = scatter_about(keys[17], (FF, D), FF ** -0.5, 0.109375, ((0, 4),))
    down_bias = scatter_about(keys[18], (D,), 0.2, 1.0)
    centre_weight = scatter_about(keys[19], (HEADS, BASIS), BASIS ** -0.5, 0.375, ((0, 4),), jnp.float32)
    width_weight = scatter_about(keys[20], (HEADS, BASIS), BASIS ** -0.5, 0.375, ((0, 4),), jnp.float32)
    grad_output = scatter_about(keys[21], (TOKENS, D), 1.0, 6.0, ((0, 32),))
    return dict(layer_input=layer_input, memory_flags=memory_flags, document_start=document_start, memory_coefficients=memory_coefficients, first_gain=first_gain, first_shift=first_shift, query_weight=query_weight, query_bias=query_bias, key_matrix=key_matrix, value_matrix=value_matrix, value_offset_bias=value_offset_bias, out_weight=out_weight, out_bias=out_bias, second_gain=second_gain, second_shift=second_shift, up_weight=up_weight, up_bias=up_bias, down_weight=down_weight, down_bias=down_bias, centre_weight=centre_weight, width_weight=width_weight, grad_output=grad_output)


@jax.custom_vjp
def low(v):
    return lax.optimization_barrier(v.astype(jnp.bfloat16)).astype(jnp.float32)

@jax.custom_vjp
def low_back(v):
    return v

def low_keep(v):
    return (low(v), None)

def low_pass(kept, grad):
    return (grad,)

def back_keep(v):
    return (v, None)

def back_low(kept, grad):
    return (low(grad),)
low.defvjp(low_keep, low_pass)
low_back.defvjp(back_keep, back_low)
maximum_precision = lax.Precision.HIGHEST

def forward_and_backward(values_in):
    return low(low_back(values_in))

def matmul(left, right):
    return jnp.dot(left, right, precision=maximum_precision, preferred_element_type=jnp.float32)

def layer_norm(values_in, gain, shift):
    center = values_in - lax.optimization_barrier(jnp.mean(values_in, axis=-1, keepdims=True))
    scaled = center * lax.rsqrt(lax.optimization_barrier(jnp.mean(center * center, axis=-1, keepdims=True)) + 1e-05)
    return scaled * gain + shift

def segment_mix(queries, keys_low, values, memory_keys, memory_values, flag, bound, centre_weight, width_weight):
    length = queries.shape[0]
    factor = queries.shape[-1] ** (-0.5)
    row_ids = jnp.arange(length, dtype=jnp.int32)[:, None]
    col_ids = jnp.arange(length, dtype=jnp.int32)[None, :]
    allowed = (col_ids <= row_ids) & ((col_ids >= bound) | (row_ids < bound))
    scores = jnp.einsum('qhd,khd->hqk', queries, keys_low, precision=maximum_precision) * factor
    scores = low_back(jnp.where(allowed[None], scores, -1000000000.0))
    attn_probs = low(jax.nn.softmax(scores, axis=-1))
    local_mix = jnp.einsum('hqk,khd->qhd', attn_probs, values, precision=maximum_precision)
    mem_scores = low_back(jnp.einsum('qhd,nhd->hqn', queries, memory_keys, precision=maximum_precision) * factor)
    centre = jax.nn.sigmoid(jnp.einsum('hqn,hn->hq', mem_scores, centre_weight, precision=maximum_precision))
    spread = 0.02 * jax.nn.softplus(jnp.einsum('hqn,hn->hq', mem_scores, width_weight, precision=maximum_precision)) + 0.01
    basis_count = memory_keys.shape[0]
    centres = (jnp.arange(basis_count, dtype=jnp.float32) + 0.5) / basis_count
    offset = centre[..., None] - centres
    recall = jnp.exp(-offset * offset / (2.0 * spread[..., None])) * lax.rsqrt(2.0 * math.pi * spread[..., None]) / basis_count
    recall = low(recall)
    recalled = jnp.einsum('hqn,nhd->qhd', recall, memory_values, precision=maximum_precision)
    return local_mix + flag * recalled

def block_forward(params, inputs, memory_signal, flags, bounds):
    first_gain, first_shift, query_weight, query_bias, key_matrix, value_matrix, value_offset_bias, out_weight, out_bias, second_gain, second_shift, up_weight, up_bias, down_weight, down_bias, centre_weight, width_weight = params
    segments = memory_signal.shape[0]
    length = inputs.shape[0] // segments
    heads = centre_weight.shape[0]
    head_size = query_weight.shape[1] // heads
    group_cols = query_weight.shape[1] // N_HEAD
    group_heads = heads // N_HEAD
    group_units = up_weight.shape[1] // N_HEAD
    normed = low(layer_norm(inputs, first_gain, first_shift))
    attn_sum = jnp.zeros_like(inputs)
    for group_idx in range(N_HEAD):
        column_span = slice(group_idx * group_cols, (group_idx + 1) * group_cols)
        head_range = slice(group_idx * group_heads, (group_idx + 1) * group_heads)
        shared = low_back(normed)
        tile_shape = (segments, length, group_heads, head_size)
        basis_dimensions = (segments, memory_signal.shape[1], group_heads, head_size)
        queries = forward_and_backward(matmul(shared, query_weight[:, column_span]) + query_bias[column_span]).reshape(tile_shape)
        keys_low = forward_and_backward(matmul(shared, key_matrix[:, column_span])).reshape(tile_shape)
        values = forward_and_backward(matmul(shared, value_matrix[:, column_span]) + value_offset_bias[column_span]).reshape(tile_shape)
        memory_keys = forward_and_backward(jnp.einsum('wmr,rq->wmq', memory_signal, key_matrix[:, column_span], precision=maximum_precision)).reshape(basis_dimensions)
        memory_values = forward_and_backward(jnp.einsum('wmr,rq->wmq', memory_signal, value_matrix[:, column_span], precision=maximum_precision) + value_offset_bias[column_span]).reshape(basis_dimensions)
        mixer = jax.checkpoint(partial(segment_mix, centre_weight=centre_weight[head_range], width_weight=width_weight[head_range]))
        mixed = lax.map(lambda segment_item: mixer(*segment_item), (queries, keys_low, values, memory_keys, memory_values, flags, bounds))
        context = forward_and_backward(mixed.reshape(segments * length, group_cols))
        attn_sum = attn_sum + low(matmul(context, out_weight[column_span, :]))
    hidden = inputs + low_back(attn_sum + out_bias)
    normed_two = low(layer_norm(hidden, second_gain, second_shift))
    mlp_sum = jnp.zeros_like(inputs)
    for group_idx in range(N_HEAD):
        unit_range = slice(group_idx * group_units, (group_idx + 1) * group_units)
        shared_two = low_back(normed_two)
        up_pre = low_back(matmul(shared_two, up_weight[:, unit_range]) + up_bias[unit_range])
        up_act = low(jax.nn.gelu(up_pre, approximate=True))
        mlp_sum = mlp_sum + low(matmul(up_act, down_weight[unit_range, :]))
    return hidden + low_back(mlp_sum + down_bias)

def reference(layer_input, memory_flags, document_start, memory_coefficients, first_gain, first_shift, query_weight, query_bias, key_matrix, value_matrix, value_offset_bias, out_weight, out_bias, second_gain, second_shift, up_weight, up_bias, down_weight, down_bias, centre_weight, width_weight, grad_output):
    params = tuple((item.astype(jnp.float32) for item in (first_gain, first_shift, query_weight, query_bias, key_matrix, value_matrix, value_offset_bias, out_weight, out_bias, second_gain, second_shift, up_weight, up_bias, down_weight, down_bias, centre_weight, width_weight)))
    groups = memory_flags.shape[0] // SEG_DEV
    width = layer_input.shape[1]
    row_count = layer_input.shape[0] // groups
    scanned = (layer_input.astype(jnp.float32).reshape(groups, row_count, width), memory_coefficients.astype(jnp.float32).reshape(groups, SEG_DEV, memory_coefficients.shape[1], width), memory_flags.astype(jnp.float32).reshape(groups, SEG_DEV), document_start.astype(jnp.int32).reshape(groups, SEG_DEV), grad_output.astype(jnp.float32).reshape(groups, row_count, width))

    def one_group(totals, segment_item):
        block_in, block_memory, block_flags, block_bounds, block_grad = segment_item
        output_block, pullback = jax.vjp(lambda values_in, weights_in: block_forward(weights_in, values_in, block_memory, block_flags, block_bounds), block_in, params)
        grad_in, grad_params = pullback(block_grad)
        totals = jax.tree.map(lambda left, right: left + right, totals, grad_params)
        return (totals, (output_block.astype(jnp.bfloat16), grad_in.astype(jnp.bfloat16)))
    zero_grads = jax.tree.map(jnp.zeros_like, params)
    totals, (outputs, grads_in) = lax.scan(one_group, zero_grads, scanned)
    return (outputs.reshape(-1, width), grads_in.reshape(-1, width), totals[0], totals[1], totals[2], totals[3], totals[4], totals[5], totals[6], totals[7], totals[8], totals[9], totals[10], totals[11], totals[12], totals[13], totals[14], totals[15], totals[16])
```

```python
import math

import jax
import jax.numpy as jnp
from jax import lax
from jax.experimental import pallas as pl
from jax.experimental.pallas import tpu as pltpu
from jax.sharding import PartitionSpec as P

F32 = jnp.float32
BF16 = jnp.bfloat16
EPS = 1e-05
ROOT = math.sqrt(2.0 / math.pi)
CUBE = 0.044715
ROW_TILE = 32


def mm(left, right):
    return lax.dot_general(left, right, (((1,), (0,)), ((), ())), preferred_element_type=F32)


def mm_nt(left, right):
    return lax.dot_general(left, right, (((1,), (1,)), ((), ())), preferred_element_type=F32)


def mm_tn(left, right):
    return lax.dot_general(left, right, (((0,), (0,)), ((), ())), preferred_element_type=F32)


def three_parts(value):
    high = value.astype(BF16)
    rest = value - high.astype(F32)
    middle = rest.astype(BF16)
    low = (rest - middle.astype(F32)).astype(BF16)
    return high, middle, low


def lane_mean(value):
    return jnp.mean(value, axis=-1, keepdims=True)


def norm_rows(value):
    center = value - lane_mean(value)
    factor = lax.rsqrt(lane_mean(center * center) + EPS)
    return center * factor, factor


def fold8(value):
    return jnp.sum(value.reshape(value.shape[0] // 8, 8, value.shape[1]), axis=0)


def row_sum(value):
    return jnp.sum(value, axis=0, keepdims=True)


ATT, OUT, MLP = 0, 1, 2
KINDS = (ATT, OUT, MLP)
MESH = pl.DeviceIdType.MESH
SUB = 8


class Exchange:
    def __init__(self, n_batch, n_head, wa, wm, recv, fin, more, sems):
        self.n_head = n_head
        self.wa, self.wm = wa, wm
        self.recv, self.fin, self.more = recv, fin, more
        (self.ag_s, self.ag_r, self.rs_s, self.rs_r, self.fin_s, self.fin_r, self.ex_s, self.ex_r,
         self.sm_s, self.sm_r, self.ax_s, self.ax_r) = sems
        b, h = lax.axis_index("batch"), lax.axis_index("head")
        self.b, self.h = b, h
        core, x, y = lax.rem(b, 2), lax.rem(lax.div(b, 2), 2), lax.rem(lax.div(b, 4), 2)
        self.core = core
        across_x, across_y = b + 2 - 4 * x, b + 4 - 8 * y
        self.mate = b + 1 - 2 * core
        self.near = across_x + core * (across_y - across_x)
        self.far = across_y + core * (across_x - across_y)
        self.high = y + core * (x - y)
        self.low = x + core * (y - x)
        self.quarter = 2 * self.high + self.low
        self.other_quarter = 2 * self.high + 1 - self.low
        self.extra = []
        step = SUB
        while step < n_batch:
            bit = lax.rem(lax.div(b, step), 2)
            self.extra.append(b + step - 2 * step * bit)
            step *= 2
        self.half_width = wm.shape[-1] // 2
        self.rows = (wa.shape[1] // n_head, wa.shape[1] // n_head, wm.shape[2])
        self.pending = []

    def barrier(self):
        signal = pltpu.get_barrier_semaphore()
        peers = [(p, self.h) for p in [self.mate, self.near, self.far] + self.extra]
        peers += [(self.b, self.group(k)) for k in range(1, self.n_head)]
        for peer in peers:
            pl.semaphore_signal(signal, inc=1, device_id=peer, device_id_type=MESH)
        pl.semaphore_wait(signal, len(peers))

    def group(self, k):
        return lax.rem(self.h + k, self.n_head)

    def cols(self, which):
        return pl.ds(pl.multiple_of(which * self.half_width, 128), self.half_width)

    def view(self, kind, k, start, count, cols):
        g = self.group(k) if k else self.h
        if kind == MLP:
            return self.wm.at[g, :, pl.ds(pl.multiple_of(start, 16), count), cols]
        first, many = (0, 3) if kind == ATT else (3, 1)
        offset = pl.multiple_of(g * self.rows[kind] + start, 16)
        return self.wa.at[pl.ds(first, many), pl.ds(offset, count), cols]

    def part(self, kind, k, pieces, index, cols):
        count = self.rows[kind] // pieces
        return self.view(kind, k, index * count, count, cols)

    def copy(self, src, dst, send, recv, peer):
        return pltpu.make_async_remote_copy(
            src_ref=src, dst_ref=dst, send_sem=send, recv_sem=recv,
            device_id=peer, device_id_type=MESH,
        )

    def gather_start(self, kind):
        own = self.part(kind, 0, 4, self.quarter, self.cols(self.core))
        for j in range(self.n_head - 1, 0, -1):
            self.copy(
                own, own, self.ag_s.at[kind, j, 0], self.ag_r.at[kind, self.n_head - j, 0],
                (self.b, self.group(j)),
            ).start()

    def gather_step(self, kind, k, stage, receive=False):
        mine = self.cols(self.core)
        if stage == 0:
            ref = self.part(kind, k, 4, self.quarter, mine)
            peer = (self.b, self.group(k))
        elif stage == 1:
            which = self.other_quarter if receive else self.quarter
            ref = self.part(kind, k, 4, which, mine)
            peer = (self.near, self.h)
        elif stage == 2:
            ref = self.part(kind, k, 2, 1 - self.high if receive else self.high, mine)
            peer = (self.far, self.h)
        else:
            ref = self.part(kind, k, 1, 0, self.cols(1 - self.core) if receive else mine)
            peer = (self.mate, self.h)
        return self.copy(
            ref, ref, self.ag_s.at[kind, k, stage], self.ag_r.at[kind, k, stage], peer
        )

    def gather_pass(self, kind, k, stage):
        self.gather_step(kind, k, stage - 1, receive=True).wait_recv()
        if stage < 4:
            self.gather_step(kind, k, stage).start()

    def gather_sent(self, kind, k):
        if k == 0:
            own = self.part(kind, 0, 4, self.quarter, self.cols(self.core))
            for j in range(1, self.n_head):
                self.copy(
                    own, own, self.ag_s.at[kind, j, 0], self.ag_r.at[kind, j, 0],
                    (self.b, self.group(j)),
                ).wait_send()
        else:
            for stage in (1, 2, 3):
                self.gather_step(kind, k, stage).wait_send()

    def reduce_step(self, kind, k, stage):
        mine = self.cols(self.core)
        if stage == 0:
            src, peer = self.part(kind, k, 1, 0, self.cols(1 - self.core)), (self.mate, self.h)
        elif stage == 1:
            src, peer = self.part(kind, k, 2, 1 - self.high, mine), (self.far, self.h)
        elif stage == 2:
            src, peer = self.part(kind, k, 4, self.other_quarter, mine), (self.near, self.h)
        else:
            src, peer = self.part(kind, k, 4, self.quarter, mine), (self.b, self.group(k))
        return self.copy(
            src, self.recv[stage][kind].at[k], self.rs_s.at[kind, k, stage],
            self.rs_r.at[kind, k, stage], peer,
        )

    def add_rows(self, kind, k, start, count, received, out=None):
        mine = self.cols(self.core)
        own = self.view(kind, k, start, count, mine)
        target = own if out is None else out
        sources = [buf.at[k, :, pl.ds(pl.multiple_of(start - base, 16), count), :] for buf, base in received]
        kinds = own.shape[0]
        tile = 48

        for t in range(kinds):
            def step(i, state):
                span = pl.ds(pl.multiple_of(i * tile, 16), tile)
                total = own[t, span, :].astype(F32)
                for source in sources:
                    total = total + source[t, span, :].astype(F32)
                target[t, span, :] = total.astype(BF16)
                return state

            lax.fori_loop(0, count // tile, step, 0)

    def reduce_pass(self, kind, k, stage):
        rows = self.rows[kind]
        half, quarter = rows // 2, rows // 4
        first, second, third = (self.recv[s][kind] for s in range(3))
        if stage > 0:
            self.reduce_step(kind, k, stage - 1).wait_recv()
        kept = self.high * half
        if stage == 1:
            self.add_rows(kind, k, (1 - self.high) * half, half, [(first, 0)])
        elif stage == 2:
            self.add_rows(
                kind, k, self.other_quarter * quarter, quarter, [(first, 0), (second, kept)]
            )
        elif stage == 3:
            own = self.quarter * quarter
            self.add_rows(
                kind, k, own, quarter, [(first, 0), (second, kept), (third, own)]
            )
        if stage < 3 or k > 0:
            self.reduce_step(kind, k, stage).start()

    def fin_part(self, kind, pieces, index, cols):
        count = self.rows[kind] // pieces
        return self.fin[kind].at[:, pl.ds(pl.multiple_of(index * count, 16), count), cols]

    def final_step(self, kind, stage, receive=False):
        mine = self.cols(self.core)
        if stage == 0:
            which = self.other_quarter if receive else self.quarter
            ref, peer = self.fin_part(kind, 4, which, mine), (self.near, self.h)
        elif stage == 1:
            which = 1 - self.high if receive else self.high
            ref, peer = self.fin_part(kind, 2, which, mine), (self.far, self.h)
        else:
            ref = self.fin_part(kind, 1, 0, self.cols(1 - self.core) if receive else mine)
            peer = (self.mate, self.h)
        return self.copy(ref, ref, self.fin_s.at[kind, stage], self.fin_r.at[kind, stage], peer)

    def final_pass(self, kind, stage):
        if stage == 0:
            for k in range(1, self.n_head):
                self.reduce_step(kind, k, 3).wait_recv()
            quarter = self.rows[kind] // 4
            last = self.recv[3][kind]
            mine = self.cols(self.core)
            own = self.view(kind, 0, self.quarter * quarter, quarter, mine)
            target = self.fin_part(kind, 4, self.quarter, mine)
            tile = 48
            for t in range(own.shape[0]):
                def step(i, state):
                    span = pl.ds(pl.multiple_of(i * tile, 16), tile)
                    total = own[t, span, :].astype(F32)
                    for k in range(1, self.n_head):
                        total = total + last[k, t, span, :].astype(F32)
                    target[t, span, :] = total.astype(BF16)
                    return state

                lax.fori_loop(0, quarter // tile, step, 0)
            for e, peer in enumerate(self.extra):
                copy = self.copy(
                    target, self.more[kind].at[e], self.ex_s.at[kind, e], self.ex_r.at[kind, e],
                    (peer, self.h),
                )
                copy.start()
                copy.wait()
                for t in range(own.shape[0]):
                    total = target[t].astype(F32) + self.more[kind][e, t].astype(F32)
                    target[t] = total.astype(BF16)
        else:
            self.final_step(kind, stage - 1, receive=True).wait_recv()
        if stage < 3:
            self.final_step(kind, stage).start()

    def all_sent(self):
        for kind in KINDS:
            for k in range(self.n_head):
                for stage in range(4):
                    if stage < 3 or k > 0:
                        self.reduce_step(kind, k, stage).wait_send()
            for stage in range(3):
                self.final_step(kind, stage).wait_send()

    def aux_copy(self, aux, j):
        own = aux.at[self.h]
        return self.copy(
            own, own, self.ax_s.at[j], self.ax_r.at[self.n_head - j], (self.b, self.group(j))
        )

    def aux_wait(self, aux, k):
        own = aux.at[self.group(k)]
        self.copy(own, own, self.ax_s.at[k], self.ax_r.at[k], (self.b, self.group(k))).wait_recv()

    def small_sum(self, small, got, all_heads):
        for e, peer in enumerate([self.mate, self.near, self.far] + self.extra):
            copy = self.copy(small, got.at[e], self.sm_s.at[e], self.sm_r.at[e], (peer, self.h))
            copy.start()
            copy.wait()
            small[...] = small[...] + got[e]
        first = 3 + len(self.extra)
        copies = []
        for j in range(1, self.n_head):
            copy = self.copy(
                small, all_heads.at[self.h], self.sm_s.at[first + j],
                self.sm_r.at[first + j], (self.b, self.group(j)),
            )
            copy.start()
            copies.append(copy)
        all_heads[self.h] = small[...]
        for copy in copies:
            copy.wait()
        total = all_heads[0]
        for g in range(1, self.n_head):
            total = total + all_heads[g]
        small[...] = total


def schedule(n_head, gp, rp, fp):
    others = range(1, n_head)
    forward = {
        0: [(gp, OUT, k, 1) for k in others] + [(gp, MLP, 1, 1)],
        1: [(gp, OUT, k, 2) for k in others] + [(gp, MLP, 1, 2)],
        2: [(gp, OUT, k, 3) for k in others] + [(gp, MLP, 2, 1)],
        3: [(gp, MLP, 1, 3), (gp, MLP, 2, 2), (gp, MLP, 3, 1)],
        4: [(gp, MLP, 2, 3), (gp, MLP, 3, 2)],
        5: [(gp, MLP, 3, 3)],
    }
    units = {
        1: [(rp, MLP, 0, 1)],
        2: [(rp, MLP, 0, 2), (rp, MLP, 1, 1)],
        3: [(rp, MLP, 0, 3), (rp, MLP, 1, 2)],
    }
    backward = {
        0: [(rp, MLP, 2, 1), (rp, MLP, 1, 3)],
        1: [(rp, MLP, 2, 2), (rp, MLP, 3, 1)],
        2: [(rp, MLP, 2, 3)] + [(rp, OUT, k, 1) for k in range(n_head)],
        3: [(rp, MLP, 3, 2)] + [(rp, OUT, k, 2) for k in range(n_head)],
        4: [(rp, MLP, 3, 3)] + [(rp, OUT, k, 3) for k in range(n_head)],
        5: [(fp, MLP, 0), (fp, OUT, 0), (fp, MLP, 1), (fp, OUT, 1), (fp, MLP, 2), (fp, OUT, 2)],
    }
    return forward, units, backward


def layer_kernel(
    n_batch, n_head,
    flags, bounds, x_in, go_in, mc_in, att_in, up_in, down_in, aux_in, norm_in,
    y_out, dx_out, dqkv_out, dout_out, dmlp_out, small_out,
    xs, gos, mcs, wa, wm, aux, nrm,
    xl, qs, ks, vs, mks, mvs, ctx, prob_top, prob_low, hid, x2, acc, dx2,
    u_s, g_s, act_s, du_s, rt_s,
    cwm, um, cen, spr, wsg, isp, nrs, pg, small,
    got, all_heads, recv, fin, more, links, sems,
):
    gcs, dqs, dks, dvs, gmk, gmv = x2, acc, ks, vs, mks, mvs
    me = lax.axis_index("head")
    rows, width = xs.shape
    heads = prob_low.shape[0]
    blocks = 2
    blk = rows // blocks
    probs = (prob_top, prob_low)
    mask = dx2.at[:, 0:rows]
    s_s = g_s.at[blk:rows, 0:rows]
    ds_s = act_s.at[:, 0:rows]
    pairs = heads // 2
    basis = mcs.shape[0]
    gcols = width // n_head
    tiles = rows // ROW_TILE

    def load(src, dst, index):
        copy = pltpu.make_async_copy(src, dst, sems.at[index])
        copy.start()
        return copy

    net = Exchange(n_batch, n_head, wa, wm, recv, fin, more, links)
    att_copies = [load(att_in, wa.at[:, pl.ds(pl.multiple_of(me * gcols, 16), gcols), :], 5)]
    aux_own = load(aux_in, aux.at[me], 3)
    copies = [
        load(x_in, xs, 0),
        load(norm_in, nrm, 1),
        load(mc_in.at[me], mcs, 2),
        load(go_in, gos, 4),
    ]
    mlp_copies = [load(up_in, wm.at[me, 0], 6), load(down_in, wm.at[me, 1], 7)]
    net.barrier()
    for copy in att_copies:
        copy.wait()
    net.gather_start(ATT)
    aux_own.wait()
    for j in range(1, n_head):
        net.aux_copy(aux, j).start()
    net.gather_start(OUT)
    for copy in mlp_copies:
        copy.wait()
    net.gather_start(MLP)

    flag = flags[me].astype(F32)
    bound = bounds[me]

    def each_tile(body, carry=0):
        def step(i, state):
            return body(pl.ds(pl.multiple_of(i * ROW_TILE, ROW_TILE), ROW_TILE), state)

        return lax.fori_loop(0, tiles, step, carry)

    small[...] = jnp.zeros_like(small)
    zero_sum = jnp.zeros((8, width), F32)

    def mask_rows(span, state):
        row_ids = lax.broadcasted_iota(jnp.int32, (ROW_TILE, rows), 0) + span.start
        col_ids = lax.broadcasted_iota(jnp.int32, (ROW_TILE, rows), 1)
        least = jnp.where(row_ids < bound, 0, bound)
        allowed = (col_ids <= row_ids) & (col_ids >= least)
        mask[span, :] = jnp.where(allowed, 0.0, -jnp.inf).astype(F32)
        return state

    each_tile(mask_rows)
    for copy in copies:
        copy.wait()

    def first_norm(span, state):
        normed, _ = norm_rows(xs[span, :].astype(F32))
        xl[span, :] = (normed * nrm[0:1, :] + nrm[1:2, :]).astype(BF16)
        return state

    each_tile(first_norm)
    for stage in (1, 2, 3, 4):
        for k in range(1, n_head):
            net.gather_pass(ATT, k, stage)
    for k in range(1, n_head):
        net.aux_wait(aux, k)

    tile_n = 256
    for kind, out, mem_out, bias_row in ((0, qs, None, 0), (1, ks, mks, None), (2, vs, mvs, 1)):
        for n in range(0, width, tile_n):
            cols = slice(n, n + tile_n)
            weight = wa[kind, cols, :]
            value = mm_nt(xl[...], weight)
            if bias_row is not None:
                bias = aux[0, bias_row : bias_row + 1, cols]
                for g in range(1, n_head):
                    bias = bias + aux[g, bias_row : bias_row + 1, cols]
                value = value + bias
            out[:, cols] = value.astype(BF16)
            if mem_out is not None:
                value = mm_nt(mcs[...], weight)
                if bias_row is not None:
                    value = value + bias
                mem_out[:, cols] = value.astype(BF16)

    cwm[...] = jnp.zeros_like(cwm)
    per_group = heads // n_head
    for h in range(heads):
        g, k = divmod(h, per_group)
        cwm[h : h + 1, :] = aux[g, 3:4, k * basis : (k + 1) * basis]
        cwm[16 + h : 17 + h, :] = aux[g, 4:5, k * basis : (k + 1) * basis]
    head_width = width // heads
    own_lanes = (
        lax.broadcasted_iota(jnp.int32, (32, width), 0) % 16
        == lax.broadcasted_iota(jnp.int32, (32, width), 1) // head_width
    )
    scale = head_width ** (-0.5)
    parts = three_parts(cwm[...])
    maps = sum(mm(part, mks[...]) for part in reversed(parts))
    maps = jnp.where(own_lanes, maps * scale, 0.0)
    for index, part in enumerate(three_parts(maps)):
        um[32 * index : 32 * index + 32, :] = part
    pre = mm_nt(um[...], qs[...])
    pre = (pre[64:96] + pre[32:64]) + pre[0:32]
    centre = jax.nn.sigmoid(pre[0:16])
    width_pre = pre[16:32]
    spread = 0.02 * (jnp.maximum(width_pre, 0.0) + jnp.log1p(jnp.exp(-jnp.abs(width_pre)))) + 0.01
    cen[...] = centre
    spr[...] = spread
    wsg[...] = jax.nn.sigmoid(width_pre)
    isp[...] = -0.5 / spread
    nrs[...] = lax.rsqrt((2.0 * math.pi) * spread) / basis
    pg[...] = jnp.zeros_like(pg)

    lane = lax.broadcasted_iota(jnp.int32, (1, 2 * head_width), 1)
    half = [
        jnp.where((lane >= head_width) == bool(e), 1.0, 0.0).astype(BF16) for e in range(2)
    ]
    n_tile = 64
    sub = 64

    def recall_tile(head, start):
        ids = lax.broadcasted_iota(jnp.int32, (n_tile, rows), 0).astype(F32)
        offset = cen[pl.ds(head, 1), :] - (ids + (start + 0.5)) / basis
        value = jnp.exp(offset * offset * isp[pl.ds(head, 1), :]) * nrs[pl.ds(head, 1), :]
        return offset, value

    def at(index, slots):
        for value, events in slots.items():
            @pl.when(index == value)
            def _():
                for event, *rest in events:
                    event(*rest)

    gp, rp, fp = net.gather_pass, net.reduce_pass, net.final_pass
    forward_slots, unit_slots, backward_slots = schedule(n_head, gp, rp, fp)

    def forward_pair(p, state):
        at(p, forward_slots)
        lanes = pl.ds(pl.multiple_of(p * 2 * head_width, 2 * head_width), 2 * head_width)
        keys = ks[:, lanes]
        vals = vs[:, lanes]
        queries = qs[:, lanes] * jnp.asarray(scale, BF16)
        mem_vals = mvs[:, lanes] * flag.astype(BF16)
        for e in range(2):
            head = 2 * p + e
            masked_q = queries * half[e]
            masked_v = vals * half[e]
            for r in range(blocks):
                cols = (r + 1) * blk
                s_s[:, :cols] = mm_nt(masked_q[r * blk : (r + 1) * blk], keys[:cols])
                for t in range(0, blk, sub):
                    scores = s_s[t : t + sub, :cols] + mask[r * blk + t : r * blk + t + sub, :cols]
                    shifted = jnp.exp(scores - jnp.max(scores, axis=-1, keepdims=True))
                    inverse = 1.0 / jnp.sum(shifted, axis=-1, keepdims=True)
                    probs[r][head, t : t + sub, :] = (shifted * inverse).astype(BF16)
            for t in range(0, basis, n_tile):
                _, value = recall_tile(head, t)
                rt_s[t : t + n_tile, :] = value.astype(BF16)
            part = mm_tn(rt_s[...], mem_vals * half[e])
            for r in range(blocks):
                cols = (r + 1) * blk
                span = slice(r * blk, (r + 1) * blk)
                value = mm(probs[r][head], masked_v[:cols]) + part[span]
                if e == 0:
                    u_s[span, 0 : 2 * head_width] = value
                else:
                    ctx[span, lanes] = (value + u_s[span, 0 : 2 * head_width]).astype(BF16)
        return state

    lax.fori_loop(0, pairs, forward_pair, 0)

    for k in range(1, n_head):
        gp(OUT, k, 4)

    for n in range(0, width, tile_n):
        hid[:, n : n + tile_n] = mm(ctx[...], wa[3, :, n : n + tile_n])

    def second_norm(span, state):
        hidden = xs[span, :].astype(F32) + (hid[span, :] + nrm[2:3, :])
        hid[span, :] = hidden
        normed, _ = norm_rows(hidden)
        x2[span, :] = (normed * nrm[3:4, :] + nrm[4:5, :]).astype(BF16)
        acc[span, :] = jnp.zeros((ROW_TILE, width), F32)
        dx2[span, :] = jnp.zeros((ROW_TILE, width), F32)
        return state

    each_tile(second_norm)

    def units(k, state):
        g = lax.rem(me + k, n_head)
        at(k, {i: [(gp, MLP, i, 4)] for i in range(1, n_head)})
        for n in range(0, width, tile_n):
            cols = slice(n, n + tile_n)
            u_s[:, cols] = mm(x2[...], wm[g, 0, :, cols])
            g_s[:, cols] = mm_nt(gos[...], wm[g, 1, cols, :])
        bias = aux[g, 2:3, :]

        def activate(span, total):
            pre = u_s[span, :] + bias
            square = pre * pre
            tanh = jnp.tanh(ROOT * pre * (1.0 + CUBE * square))
            outer = 0.5 + 0.5 * tanh
            act_s[span, :] = (pre * outer).astype(BF16)
            slope = outer + (0.5 * ROOT) * pre * (1.0 - tanh * tanh) * (1.0 + (3 * CUBE) * square)
            low = (g_s[span, :] * slope).astype(BF16)
            du_s[span, :] = low
            return total + fold8(low.astype(F32))

        total = each_tile(activate, zero_sum)
        at(k, unit_slots)
        small[pl.ds(8 + g, 1), :] = row_sum(total)
        for n in range(0, width, tile_n):
            cols = slice(n, n + tile_n)
            acc[:, cols] += mm(act_s[...], wm[g, 1, :, cols])
            dx2[:, cols] += mm_nt(du_s[...], wm[g, 0, cols, :])
        at(k, {i: [(net.gather_sent, MLP, i)] for i in range(n_head)})
        for n in range(0, width, tile_n):
            cols = slice(n, n + tile_n)
            wm[g, 1, :, cols] = mm_tn(act_s[...], gos[:, cols]).astype(BF16)
            wm[g, 0, :, cols] = mm_tn(x2[...], du_s[:, cols]).astype(BF16)
        at(k, {i: [(rp, MLP, i, 0)] for i in range(n_head)})
        return state

    lax.fori_loop(0, n_head, units, 0)

    def second_back(span, sums):
        hidden = hid[span, :]
        normed, factor = norm_rows(hidden)
        grad = dx2[span, :]
        grad_out = gos[span, :].astype(F32)
        xl2 = hidden + (acc[span, :] + nrm[5:6, :])
        du_s[span, :] = xl2.astype(BF16)
        scaled = grad * nrm[3:4, :]
        total = grad_out + factor * (
            scaled - lane_mean(scaled) - normed * lane_mean(scaled * normed)
        )
        hid[span, :] = total
        low = total.astype(BF16)
        act_s[span, :] = low
        return (
            sums[0] + fold8(grad * normed),
            sums[1] + fold8(grad),
            sums[2] + fold8(low.astype(F32)),
            sums[3] + fold8(grad_out),
        )

    sums = each_tile(second_back, (zero_sum,) * 4)
    y_copy = load(du_s, y_out, 0)
    small[3:4, :] = row_sum(sums[0])
    small[4:5, :] = row_sum(sums[1])
    small[2:3, :] = row_sum(sums[2])
    small[5:6, :] = row_sum(sums[3])
    for n in range(0, width, tile_n):
        cols = slice(n, n + tile_n)
        gcs[:, cols] = mm_nt(act_s[...], wa[3, cols, :]).astype(BF16)
    for k in range(n_head):
        net.gather_sent(OUT, k)
    for n in range(0, width, tile_n):
        cols = slice(n, n + tile_n)
        wa[3, :, cols] = mm_tn(ctx[...], act_s[:, cols]).astype(BF16)
    for k in range(n_head):
        rp(OUT, k, 0)

    def backward_pair(p, state):
        at(p, backward_slots)
        lanes = pl.ds(pl.multiple_of(p * 2 * head_width, 2 * head_width), 2 * head_width)
        keys = ks[:, lanes]
        vals = vs[:, lanes]
        queries = qs[:, lanes] * jnp.asarray(scale, BF16)
        grads = gcs[:, lanes]
        mem_vals = mvs[:, lanes] * flag.astype(BF16)
        for e in range(2):
            head = 2 * p + e
            masked_g = grads * half[e]
            masked_q = queries * half[e]
            masked_k = keys * half[e]
            for r in range(blocks):
                cols = (r + 1) * blk
                span = slice(r * blk, (r + 1) * blk)
                s_s[:, :cols] = mm_nt(masked_g[span], vals[:cols])
                for t in range(0, blk, sub):
                    inner = slice(r * blk + t, r * blk + t + sub)
                    grad = s_s[t : t + sub, :cols]
                    prob = probs[r][head, t : t + sub, :].astype(F32)
                    total = jnp.sum(prob * grad, axis=-1, keepdims=True)
                    ds_s[inner, :cols] = (prob * (grad - total)).astype(BF16)
                value = mm(ds_s[span, :cols], masked_k[:cols])
                if e == 0:
                    dqs[span, lanes] = value
                else:
                    dqs[span, lanes] += value
            for c in range(blocks):
                span = slice(c * blk, (c + 1) * blk)
                key_part = mm_tn(ds_s[c * blk :, span], masked_q[c * blk :])
                val_part = mm_tn(prob_low[head, :, span], masked_g[blk:])
                if c == 0:
                    val_part = val_part + mm_tn(prob_top[head], masked_g[:blk])
                if e == 0:
                    u_s[span, 0:128] = key_part
                    u_s[span, 128:256] = val_part
                else:
                    dks[span, lanes] = (key_part + u_s[span, 0:128]).astype(BF16)
                    dvs[span, lanes] = (val_part + u_s[span, 128:256]).astype(BF16)
            g_s[0:basis, 0:rows] = mm_nt(mem_vals * half[e], grads)
            sum0 = jnp.zeros((8, rows), F32)
            sum1 = sum0
            sum2 = sum0
            for t in range(0, basis, n_tile):
                offset, value = recall_tile(head, t)
                rt_s[t : t + n_tile, :] = value.astype(BF16)
                weighted = g_s[t : t + n_tile, 0:rows] * value
                moment = weighted * offset
                sum0 = sum0 + fold8(weighted)
                sum1 = sum1 + fold8(moment)
                sum2 = sum2 + fold8(moment * offset)
            part = mm(rt_s[...], masked_g * flag.astype(BF16))
            if e == 0:
                u_s[0:basis, 256:384] = part
            else:
                gmv[:, lanes] = (part + u_s[0:basis, 256:384]).astype(BF16)
            one = pl.ds(head, 1)
            centre = cen[one, :]
            inverse = 1.0 / spr[one, :]
            grad_centre = -row_sum(sum1) * inverse
            grad_spread = (row_sum(sum2) * inverse - row_sum(sum0)) * (0.5 * inverse)
            pg[one, :] = grad_centre * centre * (1.0 - centre)
            pg[pl.ds(16 + head, 1), :] = 0.02 * grad_spread * wsg[one, :]
        return state

    lax.fori_loop(0, pairs, backward_pair, 0)
    y_copy.wait()

    slopes = three_parts(pg[...])
    moments = sum(mm(part, qs[...]) for part in reversed(slopes))
    moments = jnp.where(own_lanes, moments * scale, 0.0)
    pieces = three_parts(moments)
    weight_grads = sum(mm_nt(piece, mks[...]) for piece in reversed(pieces))
    for h in range(heads):
        g, k = divmod(h, per_group)
        small[12 + g : 13 + g, k * basis : (k + 1) * basis] = weight_grads[h : h + 1, :]
        small[16 + g : 17 + g, k * basis : (k + 1) * basis] = weight_grads[16 + h : 17 + h, :]
    gmk[...] = (
        (mm_tn(parts[1], pieces[0]) + mm_tn(parts[0], pieces[1])) + mm_tn(parts[0], pieces[0])
    ).astype(BF16)
    for n in range(0, width, tile_n):
        cols = slice(n, n + tile_n)
        high = um[0:32, cols]
        value = (mm_tn(slopes[1], high) + mm_tn(slopes[0], um[32:64, cols])) + mm_tn(
            slopes[0], high
        )
        act_s[:, cols] = (dqs[:, cols] * scale + value).astype(BF16)
    def bias_sums(span, sums):
        return (
            sums[0] + fold8(act_s[span, :].astype(F32)),
            sums[1] + fold8(dvs[span, :].astype(F32)),
        )

    sums = each_tile(bias_sums, (zero_sum,) * 2)
    small[6:7, :] = row_sum(sums[0])
    small[7:8, :] = row_sum(sums[1]) + row_sum(gmv[...].astype(F32))

    for n in range(0, width, tile_n):
        cols = slice(n, n + tile_n)
        dx2[:, cols] = (
            mm(act_s[...], wa[0, :, cols])
            + mm(dks[...], wa[1, :, cols])
            + mm(dvs[...], wa[2, :, cols])
        )
    for k in range(n_head):
        net.gather_sent(ATT, k)
    for n in range(0, width, tile_n):
        cols = slice(n, n + tile_n)
        wa[0, :, cols] = mm_tn(act_s[...], xl[:, cols]).astype(BF16)
        wa[1, :, cols] = (
            mm_tn(dks[...], xl[:, cols]) + mm_tn(gmk[...], mcs[:, cols])
        ).astype(BF16)
        wa[2, :, cols] = (
            mm_tn(dvs[...], xl[:, cols]) + mm_tn(gmv[...], mcs[:, cols])
        ).astype(BF16)

    for k in range(n_head):
        rp(ATT, k, 0)
    for k in range(n_head):
        rp(ATT, k, 1)

    def first_back(span, sums):
        normed, factor = norm_rows(xs[span, :].astype(F32))
        grad = dx2[span, :]
        scaled = grad * nrm[0:1, :]
        total = hid[span, :] + factor * (
            scaled - lane_mean(scaled) - normed * lane_mean(scaled * normed)
        )
        du_s[span, :] = total.astype(BF16)
        return (sums[0] + fold8(grad * normed), sums[1] + fold8(grad))

    sums = each_tile(first_back, (zero_sum,) * 2)
    small[0:1, :] = row_sum(sums[0])
    small[1:2, :] = row_sum(sums[1])
    outs = [load(du_s, dx_out, 0)]
    for k in range(n_head):
        rp(ATT, k, 2)
    net.small_sum(small, got, all_heads)
    outs += [load(small, small_out, 1)]
    for k in range(n_head):
        rp(ATT, k, 3)
    fp(MLP, 3)
    outs += [load(fin[MLP], dmlp_out, 2)]
    fp(OUT, 3)
    outs += [load(fin[OUT], dout_out, 3)]
    for stage in range(4):
        fp(ATT, stage)
    outs += [load(fin[ATT], dqkv_out, 4)]
    net.all_sent()
    for j in range(1, n_head):
        net.aux_copy(aux, j).wait_send()
    for copy in outs:
        copy.wait()


def per_device(
    n_batch, n_head,
    layer_input, memory_flags, document_start, memory_coefficients,
    first_gain, first_shift, query_weight, query_bias, key_matrix, value_matrix,
    value_offset_bias, out_weight, out_bias, second_gain, second_shift,
    up_weight, up_bias, down_weight, down_bias, centre_weight, width_weight, grad_output,
):
    rows, width = layer_input.shape
    basis = memory_coefficients.shape[1]
    gcols = query_weight.shape[1]
    heads = centre_weight.shape[0] * n_head
    me = lax.axis_index("head")
    att = jnp.stack([query_weight.T, key_matrix.T, value_matrix.T, out_weight])

    def spread(vector):
        return lax.dynamic_update_slice(jnp.zeros((width,), F32), vector.astype(F32), (me * gcols,))

    aux = jnp.stack(
        [spread(query_bias), spread(value_offset_bias), up_bias.astype(F32),
         centre_weight.reshape(width), width_weight.reshape(width)]
    )
    aux = jnp.pad(aux, ((0, 3), (0, 0)))
    norm = jnp.stack(
        [first_gain, first_shift, out_bias, second_gain, second_shift, down_bias]
    ).astype(F32)
    norm = jnp.pad(norm, ((0, 2), (0, 0)))
    extra = 0
    while SUB << extra < n_batch:
        extra += 1

    def vm(*shape, dtype=BF16):
        return pltpu.VMEM(shape, dtype)

    any_spec = pl.BlockSpec(memory_space=pl.ANY)
    smem = pl.BlockSpec(memory_space=pltpu.SMEM)
    dma = pltpu.SemaphoreType.DMA
    halves = ((3, gcols), (1, gcols), (2, width))
    recv = tuple(
        tuple(vm(n_head, t, r // pieces, width // 2) for t, r in halves) for pieces in (1, 2, 4, 4)
    )
    y, dx, dqkv, dout, dmlp, small = pl.pallas_call(
        lambda *refs: layer_kernel(n_batch, n_head, *refs),
        out_shape=(
            jax.ShapeDtypeStruct((rows, width), BF16),
            jax.ShapeDtypeStruct((rows, width), BF16),
            jax.ShapeDtypeStruct((3, gcols, width), BF16),
            jax.ShapeDtypeStruct((1, gcols, width), BF16),
            jax.ShapeDtypeStruct((2, width, width), BF16),
            jax.ShapeDtypeStruct((24, width), F32),
        ),
        in_specs=[smem, smem] + [any_spec] * 8,
        out_specs=[any_spec] * 6,
        scratch_shapes=[
            vm(rows, width), vm(rows, width), vm(basis, width),
            vm(4, width, width), vm(n_head, 2, width, width),
            vm(n_head, 8, width, dtype=F32), vm(8, width, dtype=F32),
            vm(rows, width), vm(rows, width), vm(rows, width), vm(rows, width),
            vm(basis, width), vm(basis, width), vm(rows, width),
            vm(heads, rows // 2, rows // 2), vm(heads, rows // 2, rows),
            vm(rows, width, dtype=F32), vm(rows, width),
            vm(rows, width, dtype=F32), vm(rows, width, dtype=F32),
            vm(rows, width, dtype=F32), vm(rows, width, dtype=F32),
            vm(rows, width), vm(rows, width), vm(basis, rows),
            vm(32, basis, dtype=F32), vm(96, width),
            vm(16, rows, dtype=F32), vm(16, rows, dtype=F32), vm(16, rows, dtype=F32),
            vm(16, rows, dtype=F32), vm(16, rows, dtype=F32), vm(32, rows, dtype=F32),
            vm(24, width, dtype=F32),
            vm(3 + extra, 24, width, dtype=F32), vm(n_head, 24, width, dtype=F32),
            recv,
            tuple(vm(t, r, width) for t, r in halves),
            tuple(vm(extra, t, r // 4, width // 2) for t, r in halves) if extra else (),
            (dma((3, n_head, 4)), dma((3, n_head, 4)), dma((3, n_head, 4)), dma((3, n_head, 4)),
             dma((3, 3)), dma((3, 3)), dma((3, max(extra, 1))), dma((3, max(extra, 1))),
             dma((3 + extra + n_head,)),
             dma((3 + extra + n_head,)), dma((n_head,)), dma((n_head,))),
            dma((8,)),
        ],
        compiler_params=pltpu.CompilerParams(
            collective_id=0, has_side_effects=True, vmem_limit_bytes=67043328
        ),
    )(memory_flags, document_start, layer_input, grad_output, memory_coefficients,
      att, up_weight, down_weight, aux, norm)
    per_group = heads // n_head
    mine = lambda row: lax.dynamic_slice(small[row], (me * gcols,), (gcols,))
    unit = lambda first: lax.dynamic_slice(small, (first + me, 0), (1, width))
    return (
        y, dx, small[0], small[1],
        dqkv[0].T.astype(F32), mine(6), dqkv[1].T.astype(F32), dqkv[2].T.astype(F32), mine(7),
        dout[0].astype(F32),
        small[2], small[3], small[4],
        dmlp[0].astype(F32), unit(8).reshape(width), dmlp[1].astype(F32), small[5],
        unit(12).reshape(per_group, basis), unit(16).reshape(per_group, basis),
    )


def solution(mesh):
    n_batch, n_head = mesh.shape["batch"], mesh.shape["head"]
    tokens = P(("batch", "head"), None)
    cols, rows, split, whole = P(None, "head"), P("head", None), P("head"), P()
    placed = (
        tokens, P("batch"), P("batch"), P("batch", None, None), whole, whole, cols, split, cols,
        cols, split, rows, whole, whole, whole, cols, split, rows, whole, rows, rows, tokens,
    )
    outs = (
        tokens, tokens, whole, whole, cols, split, cols, cols, split, rows, whole, whole, whole,
        cols, split, rows, whole, rows, rows,
    )
    return jax.shard_map(
        lambda *args: per_device(n_batch, n_head, *args),
        mesh=mesh, in_specs=placed, out_specs=outs, check_vma=False,
    )
```

```python
import math

import jax
import jax.numpy as jnp
from jax import lax
from jax.experimental import pallas as pl
from jax.experimental.pallas import tpu as pltpu
from jax.sharding import PartitionSpec as P

F32 = jnp.float32
BF16 = jnp.bfloat16
EPS = 1e-05
ROOT = math.sqrt(2.0 / math.pi)
CUBE = 0.044715
ROW_TILE = 128


def mm(left, right):
    return lax.dot_general(left, right, (((1,), (0,)), ((), ())), preferred_element_type=F32)


def mm_nt(left, right):
    return lax.dot_general(left, right, (((1,), (1,)), ((), ())), preferred_element_type=F32)


def mm_tn(left, right):
    return lax.dot_general(left, right, (((0,), (0,)), ((), ())), preferred_element_type=F32)


def three_parts(value):
    high = value.astype(BF16)
    rest = value - high.astype(F32)
    middle = rest.astype(BF16)
    low = (rest - middle.astype(F32)).astype(BF16)
    return high, middle, low


def lane_mean(value):
    return jnp.mean(value, axis=-1, keepdims=True)


def norm_rows(value):
    center = value - lane_mean(value)
    factor = lax.rsqrt(lane_mean(center * center) + EPS)
    return center * factor, factor


def fold8(value):
    return jnp.sum(value.reshape(value.shape[0] // 8, 8, value.shape[1]), axis=0)


def row_sum(value):
    return jnp.sum(value, axis=0, keepdims=True)


ATT, OUT, UP, DOWN = range(4)
KINDS = (ATT, OUT, UP, DOWN)
MESH = pl.DeviceIdType.MESH
SUB = 8


class Exchange:
    def __init__(self, n_batch, n_head, wa, wm, recv, fin, more, sems):
        self.n_head = n_head
        self.wa, self.wm = wa, wm
        self.recv, self.fin, self.more = recv, fin, more
        (self.ag_s, self.ag_r, self.rs_s, self.rs_r, self.fin_s, self.fin_r, self.ex_s, self.ex_r,
         self.sm_s, self.sm_r, self.ax_s, self.ax_r) = sems
        b, h = lax.axis_index("batch"), lax.axis_index("head")
        self.b, self.h = b, h
        core, x, y = lax.rem(b, 2), lax.rem(lax.div(b, 2), 2), lax.rem(lax.div(b, 4), 2)
        self.core = core
        across_x, across_y = b + 2 - 4 * x, b + 4 - 8 * y
        self.mate = b + 1 - 2 * core
        self.near = across_x + core * (across_y - across_x)
        self.far = across_y + core * (across_x - across_y)
        self.high = y + core * (x - y)
        self.low = x + core * (y - x)
        self.quarter = 2 * self.high + self.low
        self.other_quarter = 2 * self.high + 1 - self.low
        self.extra = []
        step = SUB
        while step < n_batch:
            bit = lax.rem(lax.div(b, step), 2)
            self.extra.append(b + step - 2 * step * bit)
            step *= 2
        self.half_width = wm.shape[-1] // 2
        self.rows = (wa.shape[1] // n_head,) * 2 + (wm.shape[2],) * 2
        self.pending = []

    def barrier(self):
        signal = pltpu.get_barrier_semaphore()
        peers = [(p, self.h) for p in [self.mate, self.near, self.far] + self.extra]
        peers += [(self.b, self.group(k)) for k in range(1, self.n_head)]
        for peer in peers:
            pl.semaphore_signal(signal, inc=1, device_id=peer, device_id_type=MESH)
        pl.semaphore_wait(signal, len(peers))

    def group(self, k):
        return lax.rem(self.h + k, self.n_head)

    def cols(self, which):
        return pl.ds(pl.multiple_of(which * self.half_width, 128), self.half_width)

    def view(self, kind, k, start, count, cols):
        g = self.group(k) if k else self.h
        if kind >= UP:
            return self.wm.at[g, pl.ds(kind - UP, 1), pl.ds(pl.multiple_of(start, 16), count), cols]
        first, many = (0, 3) if kind == ATT else (3, 1)
        offset = pl.multiple_of(g * self.rows[kind] + start, 16)
        return self.wa.at[pl.ds(first, many), pl.ds(offset, count), cols]

    def part(self, kind, k, pieces, index, cols):
        count = self.rows[kind] // pieces
        return self.view(kind, k, index * count, count, cols)

    def copy(self, src, dst, send, recv, peer):
        return pltpu.make_async_remote_copy(
            src_ref=src, dst_ref=dst, send_sem=send, recv_sem=recv,
            device_id=peer, device_id_type=MESH,
        )

    def gather_start(self, kind, k):
        own = self.part(kind, 0, 4, self.quarter, self.cols(self.core))
        j = self.n_head - k
        self.copy(
            own, own, self.ag_s.at[kind, j, 0], self.ag_r.at[kind, k, 0], (self.b, self.group(j))
        ).start()

    def gather_step(self, kind, k, stage, receive=False):
        mine = self.cols(self.core)
        if stage == 0:
            ref = self.part(kind, k, 4, self.quarter, mine)
            peer = (self.b, self.group(k))
        elif stage == 1:
            which = self.other_quarter if receive else self.quarter
            ref = self.part(kind, k, 4, which, mine)
            peer = (self.near, self.h)
        elif stage == 2:
            ref = self.part(kind, k, 2, 1 - self.high if receive else self.high, mine)
            peer = (self.far, self.h)
        else:
            ref = self.part(kind, k, 1, 0, self.cols(1 - self.core) if receive else mine)
            peer = (self.mate, self.h)
        return self.copy(
            ref, ref, self.ag_s.at[kind, k, stage], self.ag_r.at[kind, k, stage], peer
        )

    def gather_pass(self, kind, k, stage):
        self.gather_step(kind, k, stage - 1, receive=True).wait_recv()
        if stage < 4:
            self.gather_step(kind, k, stage).start()

    def gather_sent(self, kind, k):
        if k == 0:
            own = self.part(kind, 0, 4, self.quarter, self.cols(self.core))
            for j in range(1, self.n_head):
                self.copy(
                    own, own, self.ag_s.at[kind, j, 0], self.ag_r.at[kind, j, 0],
                    (self.b, self.group(j)),
                ).wait_send()
        else:
            for stage in (1, 2, 3):
                self.gather_step(kind, k, stage).wait_send()

    def reduce_step(self, kind, k, stage):
        mine = self.cols(self.core)
        if stage == 0:
            src, peer = self.part(kind, k, 1, 0, self.cols(1 - self.core)), (self.mate, self.h)
        elif stage == 1:
            src, peer = self.part(kind, k, 2, 1 - self.high, mine), (self.far, self.h)
        elif stage == 2:
            src, peer = self.part(kind, k, 4, self.other_quarter, mine), (self.near, self.h)
        else:
            src, peer = self.part(kind, k, 4, self.quarter, mine), (self.b, self.group(k))
        return self.copy(
            src, self.recv[stage][kind].at[k], self.rs_s.at[kind, k, stage],
            self.rs_r.at[kind, k, stage], peer,
        )

    def add_rows(self, kind, k, start, count, received, out=None):
        mine = self.cols(self.core)
        own = self.view(kind, k, start, count, mine)
        target = own if out is None else out
        sources = [buf.at[k, :, pl.ds(pl.multiple_of(start - base, 16), count), :] for buf, base in received]
        kinds = own.shape[0]
        tile = 48

        for t in range(kinds):
            def step(i, state):
                span = pl.ds(pl.multiple_of(i * tile, 16), tile)
                total = own[t, span, :].astype(F32)
                for source in sources:
                    total = total + source[t, span, :].astype(F32)
                target[t, span, :] = total.astype(BF16)
                return state

            lax.fori_loop(0, count // tile, step, 0)

    def reduce_pass(self, kind, k, stage):
        rows = self.rows[kind]
        half, quarter = rows // 2, rows // 4
        first, second, third = (self.recv[s][kind] for s in range(3))
        if stage > 0:
            self.reduce_step(kind, k, stage - 1).wait_recv()
        kept = self.high * half
        if stage == 1:
            self.add_rows(kind, k, (1 - self.high) * half, half, [(first, 0)])
        elif stage == 2:
            self.add_rows(
                kind, k, self.other_quarter * quarter, quarter, [(first, 0), (second, kept)]
            )
        elif stage == 3:
            own = self.quarter * quarter
            self.add_rows(
                kind, k, own, quarter, [(first, 0), (second, kept), (third, own)]
            )
        if stage < 3 or k > 0:
            self.reduce_step(kind, k, stage).start()

    def fin_part(self, kind, pieces, index, cols):
        count = self.rows[kind] // pieces
        return self.fin[kind].at[:, pl.ds(pl.multiple_of(index * count, 16), count), cols]

    def final_step(self, kind, stage, receive=False):
        mine = self.cols(self.core)
        if stage == 0:
            which = self.other_quarter if receive else self.quarter
            ref, peer = self.fin_part(kind, 4, which, mine), (self.near, self.h)
        elif stage == 1:
            which = 1 - self.high if receive else self.high
            ref, peer = self.fin_part(kind, 2, which, mine), (self.far, self.h)
        else:
            ref = self.fin_part(kind, 1, 0, self.cols(1 - self.core) if receive else mine)
            peer = (self.mate, self.h)
        return self.copy(ref, ref, self.fin_s.at[kind, stage], self.fin_r.at[kind, stage], peer)

    def final_pass(self, kind, stage):
        if stage == 0:
            for k in range(1, self.n_head):
                self.reduce_step(kind, k, 3).wait_recv()
            quarter = self.rows[kind] // 4
            last = self.recv[3][kind]
            mine = self.cols(self.core)
            own = self.view(kind, 0, self.quarter * quarter, quarter, mine)
            target = self.fin_part(kind, 4, self.quarter, mine)
            tile = 48
            for t in range(own.shape[0]):
                def step(i, state):
                    span = pl.ds(pl.multiple_of(i * tile, 16), tile)
                    total = own[t, span, :].astype(F32)
                    for k in range(1, self.n_head):
                        total = total + last[k, t, span, :].astype(F32)
                    target[t, span, :] = total.astype(BF16)
                    return state

                lax.fori_loop(0, quarter // tile, step, 0)
            for e, peer in enumerate(self.extra):
                copy = self.copy(
                    target, self.more[kind].at[e], self.ex_s.at[kind, e], self.ex_r.at[kind, e],
                    (peer, self.h),
                )
                copy.start()
                copy.wait()
                for t in range(own.shape[0]):
                    total = target[t].astype(F32) + self.more[kind][e, t].astype(F32)
                    target[t] = total.astype(BF16)
        else:
            self.final_step(kind, stage - 1, receive=True).wait_recv()
        if stage < 3:
            self.final_step(kind, stage).start()

    def all_sent(self):
        for kind in KINDS:
            for k in range(self.n_head):
                for stage in range(4):
                    if stage < 3 or k > 0:
                        self.reduce_step(kind, k, stage).wait_send()
            for stage in range(3):
                self.final_step(kind, stage).wait_send()

    def aux_copy(self, aux, j):
        own = aux.at[self.h]
        return self.copy(
            own, own, self.ax_s.at[j], self.ax_r.at[self.n_head - j], (self.b, self.group(j))
        )

    def aux_wait(self, aux, k):
        own = aux.at[self.group(k)]
        self.copy(own, own, self.ax_s.at[k], self.ax_r.at[k], (self.b, self.group(k))).wait_recv()

    def small_step(self, small, got, all_heads, stage, j=0):
        peers = [self.mate, self.near, self.far]
        if stage < 3:
            src, dst, peer, at = small, got.at[stage], (peers[stage], self.h), stage
        else:
            src, dst, peer, at = small, all_heads.at[self.h], (self.b, self.group(j)), 2 + j
        return self.copy(src, dst, self.sm_s.at[at], self.sm_r.at[at], peer)

    def small_pass(self, small, got, all_heads, stage):
        if stage == 0:
            self.small_step(small, got, all_heads, 0).start()
        elif stage <= 3:
            self.small_step(small, got, all_heads, stage - 1).wait()
            small[...] = small[...] + got[stage - 1]
            if stage < 3:
                self.small_step(small, got, all_heads, stage).start()
                return
            first = 2 + self.n_head
            for e, peer in enumerate(self.extra):
                copy = self.copy(
                    small, got.at[3 + e], self.sm_s.at[first + e], self.sm_r.at[first + e],
                    (peer, self.h),
                )
                copy.start()
                copy.wait()
                small[...] = small[...] + got[3 + e]
            for j in range(1, self.n_head):
                self.small_step(small, got, all_heads, 3, j).start()
            all_heads[self.h] = small[...]
        else:
            for j in range(1, self.n_head):
                self.small_step(small, got, all_heads, 3, j).wait()
            total = all_heads[0]
            for g in range(1, self.n_head):
                total = total + all_heads[g]
            small[...] = total


SCHEDULE = {
    "needA": (("g", 0, 1, 1), ("g", 0, 1, 2), ("g", 0, 2, 1), ("g", 0, 3, 1), ("g", 0, 1, 3), ("g", 1, 1, 1), ("g", 0, 2, 2), ("g", 1, 2, 1), ("g", 0, 1, 4), ("g", 0, 3, 2), ("g", 1, 3, 1), ("g", 1, 1, 2), ("g", 0, 2, 3), ("g", 1, 2, 2), ("g", 2, 1, 1), ("g", 0, 2, 4), ("g", 0, 3, 3), ("g", 1, 3, 2), ("g", 1, 1, 3), ("g", 0, 3, 4),),
    ("proj", 0): (("g", 1, 2, 3),),
    ("proj", 1): (("g", 3, 1, 1),),
    ("proj", 2): (("g", 2, 1, 2),),
    "maps": (("g", 1, 3, 3),),
    ("fwd", 1): (("g", 3, 1, 2),),
    ("fwd", 2): (("g", 2, 2, 1),),
    ("fwd", 4): (("g", 2, 1, 3),),
    ("fwd", 5): (("g", 3, 2, 1),),
    "needO": (("g", 1, 1, 4), ("g", 1, 2, 4), ("g", 1, 3, 4),),
    "ln2": (("g", 3, 1, 3),),
    ("mlp0", 0): (("g", 2, 2, 2),),
    ("mlp1", 0): (("g", 2, 3, 1), ("g", 3, 2, 2),),
    ("mlpU", 0): (("g", 3, 3, 1),),
    ("needU", 1): (("g", 2, 1, 4),),
    ("mlp0", 1): (("g", 2, 2, 3),),
    ("needD", 1): (("g", 3, 1, 4),),
    ("mlp1", 1): (("g", 2, 3, 2),),
    ("mlpD", 1): (("g", 3, 2, 3),),
    ("needU", 2): (("g", 2, 2, 4),),
    ("mlp0", 2): (("g", 3, 3, 2), ("r", 3, 0, 1), ("r", 2, 0, 1),),
    ("needD", 2): (("r", 3, 1, 1), ("g", 3, 2, 4),),
    ("mlp1", 2): (("g", 2, 3, 3), ("r", 2, 1, 1),),
    ("mlpU", 2): (("g", 3, 3, 3),),
    ("needU", 3): (("g", 2, 3, 4),),
    ("needD", 3): (("r", 3, 2, 1), ("r", 3, 0, 2), ("r", 2, 2, 1), ("g", 3, 3, 4),),
    ("mlp2", 3): (("r", 2, 0, 2),),
    "sb": (("r", 3, 1, 2),),
    "gctx": (("r", 3, 3, 1), ("r", 2, 3, 1),),
    ("bwd0", 0): (("r", 2, 1, 2),),
    ("bwd1", 0): (("r", 1, 0, 1), ("r", 1, 1, 1), ("r", 1, 2, 1), ("r", 1, 3, 1),),
    ("bwd0", 1): (("r", 3, 2, 2),),
    ("bwd1", 1): (("r", 3, 0, 3),),
    ("bwd0", 3): (("r", 2, 2, 2),),
    ("bwd1", 3): (("r", 2, 0, 3),),
    ("bwd0", 4): (("r", 3, 1, 3),),
    ("bwd1", 5): (("r", 3, 3, 2),),
    "dx": (("r", 2, 3, 2), ("r", 2, 1, 3),),
    "dwa": (("r", 1, 0, 2), ("r", 1, 1, 2), ("r", 1, 2, 2), ("r", 1, 3, 2),),
    "fb": (("r", 3, 2, 3),),
    "tail": (("r", 0, 0, 1), ("r", 0, 1, 1), ("r", 2, 2, 3), ("r", 0, 2, 1), ("r", 0, 3, 1), ("s", 1), ("r", 3, 3, 3), ("r", 2, 3, 3), ("r", 1, 0, 3), ("r", 1, 1, 3), ("r", 1, 2, 3), ("r", 1, 3, 3), ("r", 0, 0, 2), ("r", 0, 1, 2), ("r", 0, 2, 2), ("r", 0, 3, 2), ("f", 3, 0), ("s", 2), ("r", 0, 0, 3), ("r", 0, 1, 3), ("r", 0, 2, 3), ("f", 2, 0), ("r", 0, 3, 3), ("f", 3, 1), ("f", 1, 0), ("s", 3), ("f", 2, 1), ("f", 3, 2), ("f", 1, 1), ("f", 3, 3), ("f", 2, 2), ("f", 1, 2), ("f", 0, 0), ("f", 2, 3), ("f", 1, 3), ("f", 0, 1), ("s", 4), ("f", 0, 2), ("f", 0, 3),),
}

def layer_kernel(
    n_batch, n_head,
    flags, bounds, x_in, go_in, mc_in, att_in, up_in, down_in, aux_in, norm_in,
    y_out, dx_out, dqkv_out, dout_out, dmlp_out, small_out,
    xs, gos, mcs, wa, wm, aux, nrm,
    xl, qs, ks, vs, mks, mvs, ctx, prob_top, prob_low, hid, x2, acc, dx2,
    u_s, g_s, act_s, du_s, rt_s,
    cwm, um, cen, spr, wsg, isp, nrs, pg, small,
    got, all_heads, recv, fin, more, links, sems,
):
    gcs, dqs, dks, dvs, gmk, gmv = x2, acc, ks, vs, mks, mvs
    me = lax.axis_index("head")
    rows, width = xs.shape
    heads = prob_low.shape[0]
    blocks = 2
    blk = rows // blocks
    probs = (prob_top, prob_low)
    mask = dx2.at[:, 0:rows]
    s_s = g_s.at[blk:rows, 0:rows]
    ds_s = act_s.at[:, 0:rows]
    pairs = heads // 2
    basis = mcs.shape[0]
    gcols = width // n_head
    tiles = rows // ROW_TILE

    def load(src, dst, index):
        copy = pltpu.make_async_copy(src, dst, sems.at[index])
        copy.start()
        return copy

    others = range(1, n_head)
    net = Exchange(n_batch, n_head, wa, wm, recv, fin, more, links)
    att_copies = [load(att_in, wa.at[:, pl.ds(pl.multiple_of(me * gcols, 16), gcols), :], 5)]
    aux_own = load(aux_in, aux.at[me], 3)
    copies = [
        load(x_in, xs, 0),
        load(norm_in, nrm, 1),
        load(mc_in.at[me], mcs, 2),
        load(go_in, gos, 4),
    ]
    mlp_copies = [load(up_in, wm.at[me, 0], 6), load(down_in, wm.at[me, 1], 7)]
    net.barrier()
    for copy in att_copies:
        copy.wait()
    for k in others:
        net.gather_start(ATT, k)
    aux_own.wait()
    for j in range(1, n_head):
        net.aux_copy(aux, j).start()
    for k in others:
        net.gather_start(OUT, k)
    for copy in mlp_copies:
        copy.wait()
    for k in others:
        net.gather_start(UP, k)
        net.gather_start(DOWN, k)

    def event(op, first, *rest):
        if op == "g":
            net.gather_pass(first, *rest)
        elif op == "r":
            net.reduce_pass(first, *rest)
        elif op == "f":
            net.final_pass(first, *rest)
        else:
            net.small_pass(small, got, all_heads, first)

    def take(slot):
        for item in SCHEDULE.get(slot, ()):
            event(*item)

    def take_at(index, count, slot):
        for value in range(count):
            if (slot, value) in SCHEDULE:
                @pl.when(index == value)
                def _():
                    take((slot, value))


    flag = flags[me].astype(F32)
    bound = bounds[me]

    def each_tile(body, carry=0):
        def step(i, state):
            return body(pl.ds(pl.multiple_of(i * ROW_TILE, ROW_TILE), ROW_TILE), state)

        return lax.fori_loop(0, tiles, step, carry)

    small[...] = jnp.zeros_like(small)
    zero_sum = jnp.zeros((8, width), F32)

    def mask_rows(span, state):
        row_ids = lax.broadcasted_iota(jnp.int32, (ROW_TILE, rows), 0) + span.start
        col_ids = lax.broadcasted_iota(jnp.int32, (ROW_TILE, rows), 1)
        least = jnp.where(row_ids < bound, 0, bound)
        allowed = (col_ids <= row_ids) & (col_ids >= least)
        mask[span, :] = jnp.where(allowed, 0.0, -jnp.inf).astype(F32)
        return state

    each_tile(mask_rows)
    for copy in copies:
        copy.wait()

    def first_norm(span, state):
        normed, _ = norm_rows(xs[span, :].astype(F32))
        xl[span, :] = (normed * nrm[0:1, :] + nrm[1:2, :]).astype(BF16)
        return state

    each_tile(first_norm)
    take("ln1")
    take("needA")
    for k in others:
        net.aux_wait(aux, k)

    tile_n = 256
    for kind, out, mem_out, bias_row in ((0, qs, None, 0), (1, ks, mks, None), (2, vs, mvs, 1)):
        for n in range(0, width, tile_n):
            cols = slice(n, n + tile_n)
            weight = wa[kind, cols, :]
            value = mm_nt(xl[...], weight)
            if bias_row is not None:
                bias = aux[0, bias_row : bias_row + 1, cols]
                for g in range(1, n_head):
                    bias = bias + aux[g, bias_row : bias_row + 1, cols]
                value = value + bias
            out[:, cols] = value.astype(BF16)
            if mem_out is not None:
                value = mm_nt(mcs[...], weight)
                if bias_row is not None:
                    value = value + bias
                mem_out[:, cols] = value.astype(BF16)
        take(("proj", kind))

    cwm[...] = jnp.zeros_like(cwm)
    per_group = heads // n_head
    for h in range(heads):
        g, k = divmod(h, per_group)
        cwm[h : h + 1, :] = aux[g, 3:4, k * basis : (k + 1) * basis]
        cwm[16 + h : 17 + h, :] = aux[g, 4:5, k * basis : (k + 1) * basis]
    head_width = width // heads
    own_lanes = (
        lax.broadcasted_iota(jnp.int32, (32, width), 0) % 16
        == lax.broadcasted_iota(jnp.int32, (32, width), 1) // head_width
    )
    scale = head_width ** (-0.5)
    parts = three_parts(cwm[...])
    maps = sum(mm(part, mks[...]) for part in reversed(parts))
    maps = jnp.where(own_lanes, maps * scale, 0.0)
    for index, part in enumerate(three_parts(maps)):
        um[32 * index : 32 * index + 32, :] = part
    pre = mm_nt(um[...], qs[...])
    pre = (pre[64:96] + pre[32:64]) + pre[0:32]
    centre = jax.nn.sigmoid(pre[0:16])
    width_pre = pre[16:32]
    spread = 0.02 * (jnp.maximum(width_pre, 0.0) + jnp.log1p(jnp.exp(-jnp.abs(width_pre)))) + 0.01
    cen[...] = centre
    spr[...] = spread
    wsg[...] = jax.nn.sigmoid(width_pre)
    isp[...] = -0.5 / spread
    nrs[...] = lax.rsqrt((2.0 * math.pi) * spread) / basis
    pg[...] = jnp.zeros_like(pg)

    lane = lax.broadcasted_iota(jnp.int32, (1, 2 * head_width), 1)
    half = [
        jnp.where((lane >= head_width) == bool(e), 1.0, 0.0).astype(BF16) for e in range(2)
    ]
    n_tile = 64
    sub = 64

    def recall_tile(head, start):
        ids = lax.broadcasted_iota(jnp.int32, (n_tile, rows), 0).astype(F32)
        offset = cen[pl.ds(head, 1), :] - (ids + (start + 0.5)) / basis
        value = jnp.exp(offset * offset * isp[pl.ds(head, 1), :]) * nrs[pl.ds(head, 1), :]
        return offset, value

    take("maps")

    def forward_pair(p, state):
        lanes = pl.ds(pl.multiple_of(p * 2 * head_width, 2 * head_width), 2 * head_width)
        keys = ks[:, lanes]
        vals = vs[:, lanes]
        queries = qs[:, lanes] * jnp.asarray(scale, BF16)
        mem_vals = mvs[:, lanes] * flag.astype(BF16)
        for e in range(2):
            head = 2 * p + e
            masked_q = queries * half[e]
            masked_v = vals * half[e]
            for r in range(blocks):
                cols = (r + 1) * blk
                s_s[:, :cols] = mm_nt(masked_q[r * blk : (r + 1) * blk], keys[:cols])
                for t in range(0, blk, sub):
                    scores = s_s[t : t + sub, :cols] + mask[r * blk + t : r * blk + t + sub, :cols]
                    shifted = jnp.exp(scores - jnp.max(scores, axis=-1, keepdims=True))
                    inverse = 1.0 / jnp.sum(shifted, axis=-1, keepdims=True)
                    probs[r][head, t : t + sub, :] = (shifted * inverse).astype(BF16)
            for t in range(0, basis, n_tile):
                _, value = recall_tile(head, t)
                rt_s[t : t + n_tile, :] = value.astype(BF16)
            part = mm_tn(rt_s[...], mem_vals * half[e])
            for r in range(blocks):
                cols = (r + 1) * blk
                span = slice(r * blk, (r + 1) * blk)
                value = mm(probs[r][head], masked_v[:cols]) + part[span]
                if e == 0:
                    u_s[span, 0 : 2 * head_width] = value
                else:
                    ctx[span, lanes] = (value + u_s[span, 0 : 2 * head_width]).astype(BF16)
        take_at(p, pairs, "fwd")
        return state

    lax.fori_loop(0, pairs, forward_pair, 0)

    take("needO")

    for n in range(0, width, tile_n):
        hid[:, n : n + tile_n] = mm(ctx[...], wa[3, :, n : n + tile_n])

    take("out")

    def second_norm(span, state):
        hidden = xs[span, :].astype(F32) + (hid[span, :] + nrm[2:3, :])
        hid[span, :] = hidden
        normed, _ = norm_rows(hidden)
        x2[span, :] = (normed * nrm[3:4, :] + nrm[4:5, :]).astype(BF16)
        acc[span, :] = jnp.zeros((ROW_TILE, width), F32)
        dx2[span, :] = jnp.zeros((ROW_TILE, width), F32)
        return state

    each_tile(second_norm)
    take("ln2")

    def units(k, state):
        g = lax.rem(me + k, n_head)
        take_at(k, n_head, "needU")
        for n in range(0, width, tile_n):
            cols = slice(n, n + tile_n)
            u_s[:, cols] = mm(x2[...], wm[g, 0, :, cols])
        take_at(k, n_head, "mlp0")
        take_at(k, n_head, "needD")
        for n in range(0, width, tile_n):
            cols = slice(n, n + tile_n)
            g_s[:, cols] = mm_nt(gos[...], wm[g, 1, cols, :])
        bias = aux[g, 2:3, :]

        def activate(span, total):
            pre = u_s[span, :] + bias
            square = pre * pre
            tanh = jnp.tanh(ROOT * pre * (1.0 + CUBE * square))
            outer = 0.5 + 0.5 * tanh
            act_s[span, :] = (pre * outer).astype(BF16)
            slope = outer + (0.5 * ROOT) * pre * (1.0 - tanh * tanh) * (1.0 + (3 * CUBE) * square)
            low = (g_s[span, :] * slope).astype(BF16)
            du_s[span, :] = low
            return total + fold8(low.astype(F32))

        total = each_tile(activate, zero_sum)
        take_at(k, n_head, "mlp1")
        small[pl.ds(8 + g, 1), :] = row_sum(total)
        for n in range(0, width, tile_n):
            cols = slice(n, n + tile_n)
            acc[:, cols] += mm(act_s[...], wm[g, 1, :, cols])
            dx2[:, cols] += mm_nt(du_s[...], wm[g, 0, cols, :])
        take_at(k, n_head, "mlp2")

        def each_group(*calls):
            for value in range(n_head):
                @pl.when(k == value)
                def _():
                    for call, kind, *rest in calls:
                        call(kind, value, *rest)

        each_group((net.gather_sent, UP), (net.gather_sent, DOWN))
        for n in range(0, width, tile_n):
            cols = slice(n, n + tile_n)
            wm[g, 1, :, cols] = mm_tn(act_s[...], gos[:, cols]).astype(BF16)
        each_group((net.reduce_pass, DOWN, 0))
        take_at(k, n_head, "mlpD")
        for n in range(0, width, tile_n):
            cols = slice(n, n + tile_n)
            wm[g, 0, :, cols] = mm_tn(x2[...], du_s[:, cols]).astype(BF16)
        each_group((net.reduce_pass, UP, 0))
        take_at(k, n_head, "mlpU")
        return state

    lax.fori_loop(0, n_head, units, 0)

    def second_back(span, sums):
        hidden = hid[span, :]
        normed, factor = norm_rows(hidden)
        grad = dx2[span, :]
        grad_out = gos[span, :].astype(F32)
        xl2 = hidden + (acc[span, :] + nrm[5:6, :])
        du_s[span, :] = xl2.astype(BF16)
        scaled = grad * nrm[3:4, :]
        total = grad_out + factor * (
            scaled - lane_mean(scaled) - normed * lane_mean(scaled * normed)
        )
        hid[span, :] = total
        low = total.astype(BF16)
        act_s[span, :] = low
        return (
            sums[0] + fold8(grad * normed),
            sums[1] + fold8(grad),
            sums[2] + fold8(low.astype(F32)),
            sums[3] + fold8(grad_out),
        )

    sums = each_tile(second_back, (zero_sum,) * 4)
    y_copy = load(du_s, y_out, 0)
    small[3:4, :] = row_sum(sums[0])
    small[4:5, :] = row_sum(sums[1])
    small[2:3, :] = row_sum(sums[2])
    small[5:6, :] = row_sum(sums[3])
    take("sb")
    for n in range(0, width, tile_n):
        cols = slice(n, n + tile_n)
        gcs[:, cols] = mm_nt(act_s[...], wa[3, cols, :]).astype(BF16)
    take("gctx")
    for k in range(n_head):
        net.gather_sent(OUT, k)
    for n in range(0, width, tile_n):
        cols = slice(n, n + tile_n)
        wa[3, :, cols] = mm_tn(ctx[...], act_s[:, cols]).astype(BF16)
    for k in range(n_head):
        net.reduce_pass(OUT, k, 0)
    take("dwo")

    def backward_pair(p, state):
        lanes = pl.ds(pl.multiple_of(p * 2 * head_width, 2 * head_width), 2 * head_width)
        keys = ks[:, lanes]
        vals = vs[:, lanes]
        queries = qs[:, lanes] * jnp.asarray(scale, BF16)
        grads = gcs[:, lanes]
        mem_vals = mvs[:, lanes] * flag.astype(BF16)
        for e in range(2):
            head = 2 * p + e
            masked_g = grads * half[e]
            masked_q = queries * half[e]
            masked_k = keys * half[e]
            for r in range(blocks):
                cols = (r + 1) * blk
                span = slice(r * blk, (r + 1) * blk)
                s_s[:, :cols] = mm_nt(masked_g[span], vals[:cols])
                for t in range(0, blk, sub):
                    inner = slice(r * blk + t, r * blk + t + sub)
                    grad = s_s[t : t + sub, :cols]
                    prob = probs[r][head, t : t + sub, :].astype(F32)
                    total = jnp.sum(prob * grad, axis=-1, keepdims=True)
                    ds_s[inner, :cols] = (prob * (grad - total)).astype(BF16)
                value = mm(ds_s[span, :cols], masked_k[:cols])
                if e == 0:
                    dqs[span, lanes] = value
                else:
                    dqs[span, lanes] += value
            for c in range(blocks):
                span = slice(c * blk, (c + 1) * blk)
                key_part = mm_tn(ds_s[c * blk :, span], masked_q[c * blk :])
                val_part = mm_tn(prob_low[head, :, span], masked_g[blk:])
                if c == 0:
                    val_part = val_part + mm_tn(prob_top[head], masked_g[:blk])
                if e == 0:
                    u_s[span, 0:128] = key_part
                    u_s[span, 128:256] = val_part
                else:
                    dks[span, lanes] = (key_part + u_s[span, 0:128]).astype(BF16)
                    dvs[span, lanes] = (val_part + u_s[span, 128:256]).astype(BF16)
            g_s[0:basis, 0:rows] = mm_nt(mem_vals * half[e], grads)
            sum0 = jnp.zeros((8, rows), F32)
            sum1 = sum0
            sum2 = sum0
            for t in range(0, basis, n_tile):
                offset, value = recall_tile(head, t)
                rt_s[t : t + n_tile, :] = value.astype(BF16)
                weighted = g_s[t : t + n_tile, 0:rows] * value
                moment = weighted * offset
                sum0 = sum0 + fold8(weighted)
                sum1 = sum1 + fold8(moment)
                sum2 = sum2 + fold8(moment * offset)
            part = mm(rt_s[...], masked_g * flag.astype(BF16))
            if e == 0:
                u_s[0:basis, 256:384] = part
            else:
                gmv[:, lanes] = (part + u_s[0:basis, 256:384]).astype(BF16)
            one = pl.ds(head, 1)
            centre = cen[one, :]
            inverse = 1.0 / spr[one, :]
            grad_centre = -row_sum(sum1) * inverse
            grad_spread = (row_sum(sum2) * inverse - row_sum(sum0)) * (0.5 * inverse)
            pg[one, :] = grad_centre * centre * (1.0 - centre)
            pg[pl.ds(16 + head, 1), :] = 0.02 * grad_spread * wsg[one, :]
            take_at(p, pairs, ("bwd0", "bwd1")[e])
        return state

    lax.fori_loop(0, pairs, backward_pair, 0)
    y_copy.wait()

    slopes = three_parts(pg[...])
    moments = sum(mm(part, qs[...]) for part in reversed(slopes))
    moments = jnp.where(own_lanes, moments * scale, 0.0)
    pieces = three_parts(moments)
    weight_grads = sum(mm_nt(piece, mks[...]) for piece in reversed(pieces))
    for h in range(heads):
        g, k = divmod(h, per_group)
        small[12 + g : 13 + g, k * basis : (k + 1) * basis] = weight_grads[h : h + 1, :]
        small[16 + g : 17 + g, k * basis : (k + 1) * basis] = weight_grads[16 + h : 17 + h, :]
    gmk[...] = (
        (mm_tn(parts[1], pieces[0]) + mm_tn(parts[0], pieces[1])) + mm_tn(parts[0], pieces[0])
    ).astype(BF16)
    for n in range(0, width, tile_n):
        cols = slice(n, n + tile_n)
        high = um[0:32, cols]
        value = (mm_tn(slopes[1], high) + mm_tn(slopes[0], um[32:64, cols])) + mm_tn(
            slopes[0], high
        )
        act_s[:, cols] = (dqs[:, cols] * scale + value).astype(BF16)
    take("mem")

    def bias_sums(span, sums):
        return (
            sums[0] + fold8(act_s[span, :].astype(F32)),
            sums[1] + fold8(dvs[span, :].astype(F32)),
        )

    sums = each_tile(bias_sums, (zero_sum,) * 2)
    small[6:7, :] = row_sum(sums[0])
    small[7:8, :] = row_sum(sums[1]) + row_sum(gmv[...].astype(F32))
    take("bias")

    for n in range(0, width, tile_n):
        cols = slice(n, n + tile_n)
        dx2[:, cols] = (
            mm(act_s[...], wa[0, :, cols])
            + mm(dks[...], wa[1, :, cols])
            + mm(dvs[...], wa[2, :, cols])
        )
    take("dx")
    for k in range(n_head):
        net.gather_sent(ATT, k)
    for n in range(0, width, tile_n):
        cols = slice(n, n + tile_n)
        wa[0, :, cols] = mm_tn(act_s[...], xl[:, cols]).astype(BF16)
        wa[1, :, cols] = (
            mm_tn(dks[...], xl[:, cols]) + mm_tn(gmk[...], mcs[:, cols])
        ).astype(BF16)
        wa[2, :, cols] = (
            mm_tn(dvs[...], xl[:, cols]) + mm_tn(gmv[...], mcs[:, cols])
        ).astype(BF16)

    for k in range(n_head):
        net.reduce_pass(ATT, k, 0)
    take("dwa")

    def first_back(span, sums):
        normed, factor = norm_rows(xs[span, :].astype(F32))
        grad = dx2[span, :]
        scaled = grad * nrm[0:1, :]
        total = hid[span, :] + factor * (
            scaled - lane_mean(scaled) - normed * lane_mean(scaled * normed)
        )
        du_s[span, :] = total.astype(BF16)
        return (sums[0] + fold8(grad * normed), sums[1] + fold8(grad))

    sums = each_tile(first_back, (zero_sum,) * 2)
    small[0:1, :] = row_sum(sums[0])
    small[1:2, :] = row_sum(sums[1])
    event("s", 0)
    outs = [load(du_s, dx_out, 0)]
    take("fb")
    finished = {
        ("f", ATT, 3): (fin[ATT], dqkv_out, 1),
        ("f", OUT, 3): (fin[OUT], dout_out, 2),
        ("f", UP, 3): (fin[UP], dmlp_out.at[pl.ds(0, 1)], 3),
        ("f", DOWN, 3): (fin[DOWN], dmlp_out.at[pl.ds(1, 1)], 4),
        ("s", 4): (small, small_out, 5),
    }
    for item in SCHEDULE["tail"]:
        event(*item)
        if item in finished:
            outs.append(load(*finished[item]))
    net.all_sent()
    for j in range(1, n_head):
        net.aux_copy(aux, j).wait_send()
    for copy in outs:
        copy.wait()


def per_device(
    n_batch, n_head,
    layer_input, memory_flags, document_start, memory_coefficients,
    first_gain, first_shift, query_weight, query_bias, key_matrix, value_matrix,
    value_offset_bias, out_weight, out_bias, second_gain, second_shift,
    up_weight, up_bias, down_weight, down_bias, centre_weight, width_weight, grad_output,
):
    rows, width = layer_input.shape
    basis = memory_coefficients.shape[1]
    gcols = query_weight.shape[1]
    heads = centre_weight.shape[0] * n_head
    me = lax.axis_index("head")
    att = jnp.stack([query_weight.T, key_matrix.T, value_matrix.T, out_weight])

    def spread(vector):
        return lax.dynamic_update_slice(jnp.zeros((width,), F32), vector.astype(F32), (me * gcols,))

    aux = jnp.stack(
        [spread(query_bias), spread(value_offset_bias), up_bias.astype(F32),
         centre_weight.reshape(width), width_weight.reshape(width)]
    )
    aux = jnp.pad(aux, ((0, 3), (0, 0)))
    norm = jnp.stack(
        [first_gain, first_shift, out_bias, second_gain, second_shift, down_bias]
    ).astype(F32)
    norm = jnp.pad(norm, ((0, 2), (0, 0)))
    extra = 0
    while SUB << extra < n_batch:
        extra += 1

    def vm(*shape, dtype=BF16):
        return pltpu.VMEM(shape, dtype)

    any_spec = pl.BlockSpec(memory_space=pl.ANY)
    smem = pl.BlockSpec(memory_space=pltpu.SMEM)
    dma = pltpu.SemaphoreType.DMA
    halves = ((3, gcols), (1, gcols), (1, width), (1, width))
    recv = tuple(
        tuple(vm(n_head, t, r // pieces, width // 2) for t, r in halves) for pieces in (1, 2, 4, 4)
    )
    y, dx, dqkv, dout, dmlp, small = pl.pallas_call(
        lambda *refs: layer_kernel(n_batch, n_head, *refs),
        out_shape=(
            jax.ShapeDtypeStruct((rows, width), BF16),
            jax.ShapeDtypeStruct((rows, width), BF16),
            jax.ShapeDtypeStruct((3, gcols, width), BF16),
            jax.ShapeDtypeStruct((1, gcols, width), BF16),
            jax.ShapeDtypeStruct((2, width, width), BF16),
            jax.ShapeDtypeStruct((24, width), F32),
        ),
        in_specs=[smem, smem] + [any_spec] * 8,
        out_specs=[any_spec] * 6,
        scratch_shapes=[
            vm(rows, width), vm(rows, width), vm(basis, width),
            vm(4, width, width), vm(n_head, 2, width, width),
            vm(n_head, 8, width, dtype=F32), vm(8, width, dtype=F32),
            vm(rows, width), vm(rows, width), vm(rows, width), vm(rows, width),
            vm(basis, width), vm(basis, width), vm(rows, width),
            vm(heads, rows // 2, rows // 2), vm(heads, rows // 2, rows),
            vm(rows, width, dtype=F32), vm(rows, width),
            vm(rows, width, dtype=F32), vm(rows, width, dtype=F32),
            vm(rows, width, dtype=F32), vm(rows, width, dtype=F32),
            vm(rows, width), vm(rows, width), vm(basis, rows),
            vm(32, basis, dtype=F32), vm(96, width),
            vm(16, rows, dtype=F32), vm(16, rows, dtype=F32), vm(16, rows, dtype=F32),
            vm(16, rows, dtype=F32), vm(16, rows, dtype=F32), vm(32, rows, dtype=F32),
            vm(24, width, dtype=F32),
            vm(3 + extra, 24, width, dtype=F32), vm(n_head, 24, width, dtype=F32),
            recv,
            tuple(vm(t, r, width) for t, r in halves),
            tuple(vm(extra, t, r // 4, width // 2) for t, r in halves) if extra else (),
            (dma((4, n_head, 4)), dma((4, n_head, 4)), dma((4, n_head, 4)), dma((4, n_head, 4)),
             dma((4, 3)), dma((4, 3)), dma((4, max(extra, 1))), dma((4, max(extra, 1))),
             dma((3 + extra + n_head,)),
             dma((3 + extra + n_head,)), dma((n_head,)), dma((n_head,))),
            dma((8,)),
        ],
        compiler_params=pltpu.CompilerParams(
            collective_id=0, has_side_effects=True, vmem_limit_bytes=67043328
        ),
    )(memory_flags, document_start, layer_input, grad_output, memory_coefficients,
      att, up_weight, down_weight, aux, norm)
    per_group = heads // n_head
    mine = lambda row: lax.dynamic_slice(small[row], (me * gcols,), (gcols,))
    unit = lambda first: lax.dynamic_slice(small, (first + me, 0), (1, width))
    return (
        y, dx, small[0], small[1],
        dqkv[0].T.astype(F32), mine(6), dqkv[1].T.astype(F32), dqkv[2].T.astype(F32), mine(7),
        dout[0].astype(F32),
        small[2], small[3], small[4],
        dmlp[0].astype(F32), unit(8).reshape(width), dmlp[1].astype(F32), small[5],
        unit(12).reshape(per_group, basis), unit(16).reshape(per_group, basis),
    )


def solution(mesh):
    n_batch, n_head = mesh.shape["batch"], mesh.shape["head"]
    tokens = P(("batch", "head"), None)
    cols, rows, split, whole = P(None, "head"), P("head", None), P("head"), P()
    placed = (
        tokens, P("batch"), P("batch"), P("batch", None, None), whole, whole, cols, split, cols,
        cols, split, rows, whole, whole, whole, cols, split, rows, whole, rows, rows, tokens,
    )
    outs = (
        tokens, tokens, whole, whole, cols, split, cols, cols, split, rows, whole, whole, whole,
        cols, split, rows, whole, rows, rows,
    )
    return jax.shard_map(
        lambda *args: per_device(n_batch, n_head, *args),
        mesh=mesh, in_specs=placed, out_specs=outs, check_vma=False,
    )
```

```python
import math

import jax
import jax.numpy as jnp
from jax import lax
from jax.experimental import pallas as pl
from jax.experimental.pallas import tpu as pltpu
from jax.sharding import PartitionSpec as P

F32 = jnp.float32
BF16 = jnp.bfloat16
EPS = 1e-05
ROOT = math.sqrt(2.0 / math.pi)
CUBE = 0.044715
ROW_TILE = 128


def mm(left, right):
    return lax.dot_general(left, right, (((1,), (0,)), ((), ())), preferred_element_type=F32)


def mm_nt(left, right):
    return lax.dot_general(left, right, (((1,), (1,)), ((), ())), preferred_element_type=F32)


def mm_tn(left, right):
    return lax.dot_general(left, right, (((0,), (0,)), ((), ())), preferred_element_type=F32)


def three_parts(value):
    high = value.astype(BF16)
    rest = value - high.astype(F32)
    middle = rest.astype(BF16)
    low = (rest - middle.astype(F32)).astype(BF16)
    return high, middle, low


def lane_mean(value):
    return jnp.mean(value, axis=-1, keepdims=True)


def norm_rows(value):
    center = value - lane_mean(value)
    factor = lax.rsqrt(lane_mean(center * center) + EPS)
    return center * factor, factor


def fold8(value):
    return jnp.sum(value.reshape(value.shape[0] // 8, 8, value.shape[1]), axis=0)


def row_sum(value):
    return jnp.sum(value, axis=0, keepdims=True)


ATT, OUT, UP, DOWN = range(4)
KINDS = (ATT, OUT, UP, DOWN)
DIRECT = (ATT, OUT)
MESH = pl.DeviceIdType.MESH
SUB = 8


def nearest_first(place, count):
    return sorted(range(count), key=lambda other: (abs(other - place), other))


def pick(index, values):
    chosen = values[0]
    for at, value in enumerate(values[1:], 1):
        chosen = jnp.where(index == at, value, chosen)
    return chosen


class Exchange:
    def __init__(self, n_batch, n_head, wa, wm, recv, fin, more, smalls, sems):
        self.n_head, self.smalls = n_head, smalls
        self.wa, self.wm = wa, wm
        self.recv, self.fin, self.more = recv, fin, more
        (self.ag_s, self.ag_r, self.ag_o, self.rs_s, self.rs_r, self.fin_s, self.fin_r, self.ex_s, self.ex_r,
         self.sm_s, self.sm_r, self.ax_s, self.ax_r) = sems
        b, h = lax.axis_index("batch"), lax.axis_index("head")
        self.b, self.h = b, h
        core, x, y = lax.rem(b, 2), lax.rem(lax.div(b, 2), 2), lax.rem(lax.div(b, 4), 2)
        self.core = core
        across_x, across_y = b + 2 - 4 * x, b + 4 - 8 * y
        self.mate = b + 1 - 2 * core
        self.near = across_x + core * (across_y - across_x)
        self.far = across_y + core * (across_x - across_y)
        self.high = y + core * (x - y)
        self.low = x + core * (y - x)
        self.quarter = 2 * self.high + self.low
        self.other_quarter = 2 * self.high + 1 - self.low
        self.extra = []
        step = SUB
        while step < n_batch:
            bit = lax.rem(lax.div(b, step), 2)
            self.extra.append(b + step - 2 * step * bit)
            step *= 2
        orders = [nearest_first(place, n_head) for place in range(n_head)]
        self.groups = [
            h if k == 0 else pick(h, [order[k] for order in orders]) for k in range(n_head)
        ]
        self.half_width = wm.shape[-1] // 2
        self.rows = (wa.shape[1] // n_head,) * 2 + (wm.shape[2],) * 2
        self.pending = []

    def barrier(self):
        signal = pltpu.get_barrier_semaphore()
        peers = [(p, self.h) for p in [self.mate, self.near, self.far] + self.extra]
        peers += [(self.b, self.turn(k)) for k in range(1, self.n_head)]
        for peer in peers:
            pl.semaphore_signal(signal, inc=1, device_id=peer, device_id_type=MESH)
        pl.semaphore_wait(signal, len(peers))

    def group(self, k):
        return self.groups[k]

    def turn(self, j):
        return lax.rem(self.h + j, self.n_head)

    def cols(self, which):
        return pl.ds(pl.multiple_of(which * self.half_width, 128), self.half_width)

    def view(self, kind, k, start, count, cols):
        g = self.group(k)
        if kind >= UP:
            return self.wm.at[g, pl.ds(kind - UP, 1), pl.ds(pl.multiple_of(start, 16), count), cols]
        first, many = (0, 3) if kind == ATT else (3, 1)
        offset = pl.multiple_of(g * self.rows[kind] + start, 16)
        return self.wa.at[pl.ds(first, many), pl.ds(offset, count), cols]

    def part(self, kind, k, pieces, index, cols):
        count = self.rows[kind] // pieces
        return self.view(kind, k, index * count, count, cols)

    def copy(self, src, dst, send, recv, peer):
        return pltpu.make_async_remote_copy(
            src_ref=src, dst_ref=dst, send_sem=send, recv_sem=recv,
            device_id=peer, device_id_type=MESH,
        )

    def own_sends(self, kind):
        own = self.part(kind, 0, 4, self.quarter, self.cols(self.core))
        if kind in DIRECT:
            targets = [(self.group(k), None) for k in range(1, self.n_head)]
        else:
            targets = [(self.h + 1, self.h < self.n_head - 1), (self.h - 1, self.h > 0)]
        for at, (target, allowed) in enumerate(targets):
            copy = self.copy(
                own, own, self.ag_s.at[kind, at, 0], self.ag_r.at[kind, self.h, 0],
                (self.b, target),
            )
            yield copy, allowed

    def gather_start(self, kind):
        for copy, allowed in self.own_sends(kind):
            if allowed is None:
                copy.start()
            else:
                pl.when(allowed)(copy.start)

    def onward(self, kind, k):
        g = self.group(k)
        ref = self.part(kind, k, 4, self.quarter, self.cols(self.core))
        target = jnp.where(g < self.h, self.h + 1, self.h - 1)
        copy = self.copy(
            ref, ref, self.ag_o.at[kind, k], self.ag_r.at[kind, g, 0], (self.b, target)
        )
        return copy, (target >= 0) & (target < self.n_head)

    def gather_step(self, kind, k, stage, receive=False):
        mine = self.cols(self.core)
        if stage == 0:
            ref = self.part(kind, k, 4, self.quarter, mine)
            peer = (self.b, self.group(k))
        elif stage == 1:
            which = self.other_quarter if receive else self.quarter
            ref = self.part(kind, k, 4, which, mine)
            peer = (self.near, self.h)
        elif stage == 2:
            ref = self.part(kind, k, 2, 1 - self.high if receive else self.high, mine)
            peer = (self.far, self.h)
        else:
            ref = self.part(kind, k, 1, 0, self.cols(1 - self.core) if receive else mine)
            peer = (self.mate, self.h)
        at = self.group(k) if stage == 0 else k
        return self.copy(
            ref, ref, self.ag_s.at[kind, k, stage], self.ag_r.at[kind, at, stage], peer
        )

    def gather_pass(self, kind, k, stage):
        self.gather_step(kind, k, stage - 1, receive=True).wait_recv()
        if stage == 1 and kind not in DIRECT:
            copy, allowed = self.onward(kind, k)
            pl.when(allowed)(copy.start)
        if stage < 4:
            self.gather_step(kind, k, stage).start()

    def gather_sent(self, kind, k):
        if k == 0:
            for copy, allowed in self.own_sends(kind):
                if allowed is None:
                    copy.wait_send()
                else:
                    pl.when(allowed)(copy.wait_send)
            return
        for stage in (1, 2, 3):
            self.gather_step(kind, k, stage).wait_send()
        if kind not in DIRECT:
            copy, allowed = self.onward(kind, k)
            pl.when(allowed)(copy.wait_send)

    def reduce_step(self, kind, k, stage, receive=False):
        mine = self.cols(self.core)
        if stage == 0:
            src, peer = self.part(kind, k, 1, 0, self.cols(1 - self.core)), (self.mate, self.h)
        elif stage == 1:
            src, peer = self.part(kind, k, 2, 1 - self.high, mine), (self.far, self.h)
        elif stage == 2:
            src, peer = self.part(kind, k, 4, self.other_quarter, mine), (self.near, self.h)
        else:
            src, peer = self.part(kind, k, 4, self.quarter, mine), (self.b, self.group(k))
        at = k
        if stage == 3 and not receive:
            at = lax.rem(self.h - self.group(k) + self.n_head, self.n_head)
        return self.copy(
            src, self.recv[stage][kind].at[at], self.rs_s.at[kind, k, stage],
            self.rs_r.at[kind, at, stage], peer,
        )

    def add_rows(self, kind, k, start, count, received, out=None):
        mine = self.cols(self.core)
        own = self.view(kind, k, start, count, mine)
        target = own if out is None else out
        sources = [buf.at[k, :, pl.ds(pl.multiple_of(start - base, 16), count), :] for buf, base in received]
        kinds = own.shape[0]
        tile = min(count, 192)

        for t in range(kinds):
            def step(i, state):
                span = pl.ds(pl.multiple_of(i * tile, 16), tile)
                if len(sources) == 1:
                    target[t, span, :] = own[t, span, :] + sources[0][t, span, :]
                    return state
                total = own[t, span, :].astype(F32)
                for source in sources:
                    total = total + source[t, span, :].astype(F32)
                target[t, span, :] = total.astype(BF16)
                return state

            lax.fori_loop(0, count // tile, step, 0)

    def reduce_pass(self, kind, k, stage):
        rows = self.rows[kind]
        half, quarter = rows // 2, rows // 4
        first, second, third = (self.recv[s][kind] for s in range(3))
        if stage > 0:
            self.reduce_step(kind, k, stage - 1).wait_recv()
        kept = self.high * half
        if stage == 1:
            self.add_rows(kind, k, (1 - self.high) * half, half, [(first, 0)])
        elif stage == 2:
            self.add_rows(
                kind, k, self.other_quarter * quarter, quarter, [(first, 0), (second, kept)]
            )
        elif stage == 3:
            own = self.quarter * quarter
            self.add_rows(
                kind, k, own, quarter, [(first, 0), (second, kept), (third, own)]
            )
        if stage < 3 or k > 0:
            self.reduce_step(kind, k, stage).start()

    def fin_part(self, kind, pieces, index, cols):
        count = self.rows[kind] // pieces
        return self.fin[kind].at[:, pl.ds(pl.multiple_of(index * count, 16), count), cols]

    def final_step(self, kind, stage, receive=False):
        mine = self.cols(self.core)
        if stage == 0:
            which = self.other_quarter if receive else self.quarter
            ref, peer = self.fin_part(kind, 4, which, mine), (self.near, self.h)
        elif stage == 1:
            which = 1 - self.high if receive else self.high
            ref, peer = self.fin_part(kind, 2, which, mine), (self.far, self.h)
        else:
            ref = self.fin_part(kind, 1, 0, self.cols(1 - self.core) if receive else mine)
            peer = (self.mate, self.h)
        return self.copy(ref, ref, self.fin_s.at[kind, stage], self.fin_r.at[kind, stage], peer)

    def final_pass(self, kind, stage):
        if stage == 0:
            for k in range(1, self.n_head):
                self.reduce_step(kind, k, 3, receive=True).wait_recv()
            quarter = self.rows[kind] // 4
            last = self.recv[3][kind]
            mine = self.cols(self.core)
            own = self.view(kind, 0, self.quarter * quarter, quarter, mine)
            target = self.fin_part(kind, 4, self.quarter, mine)
            tile = min(quarter, 192)
            for t in range(own.shape[0]):
                def step(i, state):
                    span = pl.ds(pl.multiple_of(i * tile, 16), tile)
                    total = own[t, span, :].astype(F32)
                    for k in range(1, self.n_head):
                        total = total + last[k, t, span, :].astype(F32)
                    target[t, span, :] = total.astype(BF16)
                    return state

                lax.fori_loop(0, quarter // tile, step, 0)
            for e, peer in enumerate(self.extra):
                copy = self.copy(
                    target, self.more[kind].at[e], self.ex_s.at[kind, e], self.ex_r.at[kind, e],
                    (peer, self.h),
                )
                copy.start()
                copy.wait()
                for t in range(own.shape[0]):
                    total = target[t].astype(F32) + self.more[kind][e, t].astype(F32)
                    target[t] = total.astype(BF16)
        else:
            self.final_step(kind, stage - 1, receive=True).wait_recv()
        if stage < 3:
            self.final_step(kind, stage).start()

    def all_sent(self):
        for kind in KINDS:
            for k in range(self.n_head):
                for stage in range(4):
                    if stage < 3 or k > 0:
                        self.reduce_step(kind, k, stage).wait_send()
            for stage in range(3):
                self.final_step(kind, stage).wait_send()

    def aux_copy(self, aux, j):
        own = aux.at[self.h]
        return self.copy(
            own, own, self.ax_s.at[j], self.ax_r.at[self.n_head - j], (self.b, self.turn(j))
        )

    def aux_wait(self, aux, k):
        own = aux.at[self.turn(k)]
        self.copy(own, own, self.ax_s.at[k], self.ax_r.at[k], (self.b, self.turn(k))).wait_recv()

    def small_step(self, which, stage, j=0):
        value, got, all_heads = self.smalls[which]
        peers = [self.mate, self.near, self.far]
        if stage < 3:
            src, dst, peer, at = value, got.at[stage], (peers[stage], self.h), stage
        else:
            src, dst, peer, at = value, all_heads.at[self.h], (self.b, self.turn(j)), 2 + j
        return self.copy(src, dst, self.sm_s.at[which, at], self.sm_r.at[which, at], peer)

    def small_pass(self, which, stage):
        value, got, all_heads = self.smalls[which]
        if stage == 0:
            self.small_step(which, 0).start()
        elif stage <= 3:
            self.small_step(which, stage - 1).wait()
            value[...] = value[...] + got[stage - 1]
            if stage < 3:
                self.small_step(which, stage).start()
                return
            first = 2 + self.n_head
            for e, peer in enumerate(self.extra):
                copy = self.copy(
                    value, got.at[3 + e], self.sm_s.at[which, first + e],
                    self.sm_r.at[which, first + e], (peer, self.h),
                )
                copy.start()
                copy.wait()
                value[...] = value[...] + got[3 + e]
            for j in range(1, self.n_head):
                self.small_step(which, 3, j).start()
            all_heads[self.h] = value[...]
        else:
            for j in range(1, self.n_head):
                self.small_step(which, 3, j).wait()
            total = all_heads[0]
            for g in range(1, self.n_head):
                total = total + all_heads[g]
            value[...] = total


SCHEDULE = {
    "needA": (("g", 0, 1, 1), ("g", 0, 1, 2), ("g", 0, 2, 1), ("g", 1, 1, 1), ("g", 0, 3, 1), ("g", 1, 2, 1), ("g", 0, 1, 3), ("g", 0, 2, 2), ("g", 1, 1, 2), ("g", 0, 1, 4), ("g", 1, 3, 1), ("g", 0, 3, 2), ("g", 1, 2, 2), ("g", 2, 1, 1), ("g", 0, 2, 3), ("g", 1, 3, 2), ("g", 1, 1, 3), ("g", 0, 2, 4), ("g", 3, 1, 1), ("g", 2, 2, 1), ("g", 0, 3, 3), ("g", 2, 1, 2), ("g", 1, 2, 3), ("g", 0, 3, 4),),
    ("proj", 0): (("g", 3, 2, 1),),
    ("proj", 1): (("g", 1, 3, 3), ("g", 3, 1, 2),),
    ("fwd", 0): (("g", 2, 2, 2), ("g", 2, 3, 1),),
    ("fwd", 3): (("g", 2, 1, 3), ("g", 3, 2, 2), ("g", 3, 3, 1),),
    ("fwd", 5): (("g", 2, 3, 2),),
    "needO": (("g", 1, 1, 4), ("g", 1, 2, 4), ("g", 1, 3, 4),),
    ("mlp0", 0): (("g", 3, 1, 3), ("g", 3, 3, 2),),
    ("mlp2", 0): (("g", 2, 2, 3),),
    ("needU", 1): (("g", 2, 1, 4),),
    ("mlp0", 1): (("g", 3, 2, 3), ("r", 3, 0, 1),),
    ("needD", 1): (("g", 3, 1, 4),),
    ("mlp1", 1): (("g", 2, 3, 3), ("r", 2, 0, 1),),
    ("mlpU", 1): (("g", 3, 3, 3),),
    ("needU", 2): (("g", 2, 2, 4),),
    ("mlp0", 2): (("r", 3, 1, 1), ("r", 2, 1, 1),),
    ("needD", 2): (("g", 3, 2, 4),),
    ("mlp1", 2): (("r", 3, 0, 2),),
    ("mlp2", 2): (("r", 2, 0, 2),),
    ("needU", 3): (("g", 2, 3, 4),),
    ("mlp0", 3): (("r", 3, 2, 1), ("r", 2, 2, 1), ("r", 3, 0, 3),),
    ("needD", 3): (("g", 3, 3, 4),),
    ("mlp2", 3): (("r", 3, 1, 2), ("r", 2, 0, 3),),
    ("mlpU", 3): (("r", 2, 1, 2),),
    "sb": (("r", 3, 3, 1), ("r", 2, 3, 1),),
    "gctx": (("r", 3, 1, 3), ("s", 0, 1),),
    ("bwd0", 0): (("r", 3, 2, 2), ("r", 2, 1, 3), ("s", 0, 2), ("r", 1, 0, 1), ("r", 1, 1, 1), ("r", 1, 2, 1), ("r", 1, 3, 1),),
    ("bwd0", 2): (("r", 3, 2, 3), ("r", 2, 2, 2),),
    ("bwd1", 3): (("r", 3, 3, 2),),
    ("bwd1", 4): (("r", 2, 2, 3),),
    "mem": (("s", 0, 3), ("r", 1, 0, 2), ("r", 3, 3, 3), ("r", 1, 1, 2), ("r", 2, 3, 2),),
    "bias": (("r", 1, 2, 2),),
    "dx": (("s", 1, 1), ("r", 1, 3, 2), ("r", 1, 0, 3), ("r", 1, 1, 3),),
    "dwa": (("s", 1, 2), ("r", 1, 2, 3), ("r", 1, 3, 3), ("r", 0, 0, 1), ("r", 0, 1, 1), ("r", 0, 2, 1), ("r", 0, 3, 1), ("r", 2, 3, 3),),
    "fb": (("s", 1, 3), ("s", 2, 1),),
    "tail": (("s", 0, 4), ("r", 0, 0, 2), ("s", 2, 2), ("f", 3, 0), ("r", 0, 1, 2), ("r", 0, 0, 3), ("f", 1, 0), ("f", 3, 1), ("r", 0, 2, 2), ("r", 0, 1, 3), ("f", 1, 1), ("r", 0, 3, 2), ("f", 2, 0), ("r", 0, 2, 3), ("s", 2, 3), ("s", 1, 4), ("r", 0, 3, 3), ("f", 3, 2), ("f", 1, 2), ("f", 2, 1), ("f", 3, 3), ("f", 1, 3), ("f", 2, 2), ("s", 2, 4), ("f", 2, 3), ("f", 0, 0), ("f", 0, 1), ("f", 0, 2), ("f", 0, 3),),
}

def layer_kernel(
    n_batch, n_head,
    flags, bounds, norm_in, bias_in, map_in, x_in, go_in, mc_in, att_in, up_in, down_in,
    y_out, dx_out, dqkv_out, dout_out, dmlp_out, small_out, maps_out,
    xs, gos, mcs, wa, wm, aux, nrm,
    xl, qs, ks, vs, mks, mvs, ctx, prob_top, prob_low, hid, x2, acc, dx2,
    u_s, g_s, act_s, du_s, rt_s,
    cwm, um, cen, spr, wsg, isp, nrs, pg, small,
    maps_s, smalls, recv, fin, more, links, sems,
):
    gcs, dqs, dks, dvs, gmk, gmv = x2, acc, ks, vs, mks, mvs
    me = lax.axis_index("head")
    rows, width = xs.shape
    heads = prob_low.shape[0]
    blocks = 2
    blk = rows // blocks
    probs = (prob_top, prob_low)
    mask = dx2.at[:, 0:rows]
    s_s = g_s.at[blk:rows, 0:rows]
    ds_s = act_s.at[:, 0:rows]
    pairs = heads // 2
    basis = mcs.shape[0]
    gcols = width // n_head
    tiles = rows // ROW_TILE

    def load(src, dst, index):
        copy = pltpu.make_async_copy(src, dst, sems.at[index])
        copy.start()
        return copy

    others = range(1, n_head)
    net = Exchange(n_batch, n_head, wa, wm, recv, fin, more, smalls, links)
    att_copies = [load(att_in, wa.at[:, pl.ds(pl.multiple_of(me * gcols, 16), gcols), :], 5)]
    copies = [
        load(x_in, xs, 0),
        load(mc_in.at[me], mcs, 2),
        load(go_in, gos, 4),
    ]
    mlp_copies = [load(up_in, wm.at[me, 0], 6), load(down_in, wm.at[me, 1], 7)]
    for row, ref in enumerate(norm_in):
        nrm[row : row + 1, :] = ref[...].astype(F32).reshape(1, width)
    aux[me] = jnp.zeros((8, width), F32)
    for row, ref in enumerate(bias_in[:2]):
        aux[me, row : row + 1, 0:gcols] = ref[...].astype(F32).reshape(1, gcols)
    aux[me, 2:3, :] = bias_in[2][...].astype(F32).reshape(1, width)
    for row, ref in enumerate(map_in):
        for k in range(ref.shape[0]):
            aux[me, 3 + row : 4 + row, k * basis : (k + 1) * basis] = ref[k : k + 1, :]
    net.barrier()
    for copy in att_copies:
        copy.wait()
    net.gather_start(ATT)
    for j in range(1, n_head):
        net.aux_copy(aux, j).start()
    net.gather_start(OUT)
    for copy in mlp_copies:
        copy.wait()
    net.gather_start(UP)
    net.gather_start(DOWN)

    def event(op, first, *rest):
        if op == "g":
            net.gather_pass(first, *rest)
        elif op == "r":
            net.reduce_pass(first, *rest)
        elif op == "f":
            net.final_pass(first, *rest)
        else:
            net.small_pass(first, *rest)

    def take(slot):
        for item in SCHEDULE.get(slot, ()):
            event(*item)

    def take_at(index, count, slot):
        for value in range(count):
            if (slot, value) in SCHEDULE:
                @pl.when(index == value)
                def _():
                    take((slot, value))


    flag = flags[me].astype(F32)
    bound = bounds[me]

    def each_tile(body, carry=0):
        def step(i, state):
            return body(pl.ds(pl.multiple_of(i * ROW_TILE, ROW_TILE), ROW_TILE), state)

        return lax.fori_loop(0, tiles, step, carry)

    early, middle, late = (group[0] for group in smalls)
    for ref in (middle, late):
        ref[...] = jnp.zeros_like(ref)
    zero_sum = jnp.zeros((8, width), F32)

    def mask_rows(span, state):
        row_ids = lax.broadcasted_iota(jnp.int32, (ROW_TILE, rows), 0) + span.start
        col_ids = lax.broadcasted_iota(jnp.int32, (ROW_TILE, rows), 1)
        least = jnp.where(row_ids < bound, 0, bound)
        allowed = (col_ids <= row_ids) & (col_ids >= least)
        mask[span, :] = jnp.where(allowed, 0.0, -jnp.inf).astype(F32)
        return state

    each_tile(mask_rows)
    for copy in copies:
        copy.wait()

    def first_norm(span, state):
        normed, _ = norm_rows(xs[span, :].astype(F32))
        xl[span, :] = (normed * nrm[0:1, :] + nrm[1:2, :]).astype(BF16)
        return state

    each_tile(first_norm)
    take("ln1")
    take("needA")
    for k in others:
        net.aux_wait(aux, k)

    column = lax.broadcasted_iota(jnp.int32, (1, width), 1)
    biases = []
    for row in range(2):
        bias = jnp.zeros((1, width), F32)
        for g in range(n_head):
            moved = aux[g, row : row + 1, :]
            shift = g * gcols
            if shift:
                moved = pltpu.roll(moved, shift, 1)
            bias = bias + jnp.where(column // gcols == g, moved, 0.0)
        biases.append(bias)

    tile_n = 256
    for kind, out, mem_out, bias_row in ((0, qs, None, 0), (1, ks, mks, None), (2, vs, mvs, 1)):
        for n in range(0, width, tile_n):
            cols = slice(n, n + tile_n)
            weight = wa[kind, cols, :]
            value = mm_nt(xl[...], weight)
            if bias_row is not None:
                value = value + biases[bias_row][:, cols]
            out[:, cols] = value.astype(BF16)
            if mem_out is not None:
                value = mm_nt(mcs[...], weight)
                if bias_row is not None:
                    value = value + biases[bias_row][:, cols]
                mem_out[:, cols] = value.astype(BF16)
        take(("proj", kind))

    cwm[...] = jnp.zeros_like(cwm)
    per_group = heads // n_head
    for h in range(heads):
        g, k = divmod(h, per_group)
        cwm[h : h + 1, :] = aux[g, 3:4, k * basis : (k + 1) * basis]
        cwm[16 + h : 17 + h, :] = aux[g, 4:5, k * basis : (k + 1) * basis]
    head_width = width // heads
    own_lanes = (
        lax.broadcasted_iota(jnp.int32, (32, width), 0) % 16
        == lax.broadcasted_iota(jnp.int32, (32, width), 1) // head_width
    )
    scale = head_width ** (-0.5)
    parts = three_parts(cwm[...])
    maps = sum(mm(part, mks[...]) for part in reversed(parts))
    maps = jnp.where(own_lanes, maps * scale, 0.0)
    for index, part in enumerate(three_parts(maps)):
        um[32 * index : 32 * index + 32, :] = part
    pre = mm_nt(um[...], qs[...])
    pre = (pre[64:96] + pre[32:64]) + pre[0:32]
    centre = jax.nn.sigmoid(pre[0:16])
    width_pre = pre[16:32]
    spread = 0.02 * (jnp.maximum(width_pre, 0.0) + jnp.log1p(jnp.exp(-jnp.abs(width_pre)))) + 0.01
    cen[...] = centre
    spr[...] = spread
    wsg[...] = jax.nn.sigmoid(width_pre)
    isp[...] = -0.5 / spread
    nrs[...] = lax.rsqrt((2.0 * math.pi) * spread) / basis
    pg[...] = jnp.zeros_like(pg)

    lane = lax.broadcasted_iota(jnp.int32, (1, 2 * head_width), 1)
    half = [
        jnp.where((lane >= head_width) == bool(e), 1.0, 0.0).astype(BF16) for e in range(2)
    ]
    n_tile = 64
    sub = 64

    def recall_tile(head, start):
        ids = lax.broadcasted_iota(jnp.int32, (n_tile, rows), 0).astype(F32)
        offset = cen[pl.ds(head, 1), :] - (ids + (start + 0.5)) / basis
        value = jnp.exp(offset * offset * isp[pl.ds(head, 1), :]) * nrs[pl.ds(head, 1), :]
        return offset, value

    take("maps")

    def forward_pair(p, state):
        lanes = pl.ds(pl.multiple_of(p * 2 * head_width, 2 * head_width), 2 * head_width)
        keys = ks[:, lanes]
        vals = vs[:, lanes]
        queries = qs[:, lanes] * jnp.asarray(scale, BF16)
        mem_vals = mvs[:, lanes] * flag.astype(BF16)
        for e in range(2):
            head = 2 * p + e
            masked_q = queries * half[e]
            masked_v = vals * half[e]
            for r in range(blocks):
                cols = (r + 1) * blk
                s_s[:, :cols] = mm_nt(masked_q[r * blk : (r + 1) * blk], keys[:cols])
                for t in range(0, blk, sub):
                    scores = s_s[t : t + sub, :cols] + mask[r * blk + t : r * blk + t + sub, :cols]
                    shifted = jnp.exp(scores - jnp.max(scores, axis=-1, keepdims=True))
                    inverse = 1.0 / jnp.sum(shifted, axis=-1, keepdims=True)
                    probs[r][head, t : t + sub, :] = (shifted * inverse).astype(BF16)
            for t in range(0, basis, n_tile):
                _, value = recall_tile(head, t)
                rt_s[t : t + n_tile, :] = value.astype(BF16)
            part = mm_tn(rt_s[...], mem_vals * half[e])
            for r in range(blocks):
                cols = (r + 1) * blk
                span = slice(r * blk, (r + 1) * blk)
                value = mm(probs[r][head], masked_v[:cols]) + part[span]
                if e == 0:
                    u_s[span, 0 : 2 * head_width] = value
                else:
                    ctx[span, lanes] = (value + u_s[span, 0 : 2 * head_width]).astype(BF16)
        take_at(p, pairs, "fwd")
        return state

    lax.fori_loop(0, pairs, forward_pair, 0)

    take("needO")

    for n in range(0, width, tile_n):
        hid[:, n : n + tile_n] = mm(ctx[...], wa[3, :, n : n + tile_n])

    take("out")

    def second_norm(span, state):
        hidden = xs[span, :].astype(F32) + (hid[span, :] + nrm[2:3, :])
        hid[span, :] = hidden
        normed, _ = norm_rows(hidden)
        x2[span, :] = (normed * nrm[3:4, :] + nrm[4:5, :]).astype(BF16)
        acc[span, :] = jnp.zeros((ROW_TILE, width), F32)
        dx2[span, :] = jnp.zeros((ROW_TILE, width), F32)
        return state

    each_tile(second_norm)
    take("ln2")

    def units(k, state):
        g = pick(k, net.groups)
        take_at(k, n_head, "needU")
        for n in range(0, width, tile_n):
            cols = slice(n, n + tile_n)
            u_s[:, cols] = mm(x2[...], wm[g, 0, :, cols])
        take_at(k, n_head, "mlp0")
        take_at(k, n_head, "needD")
        for n in range(0, width, tile_n):
            cols = slice(n, n + tile_n)
            g_s[:, cols] = mm_nt(gos[...], wm[g, 1, cols, :])
        bias = aux[g, 2:3, :]

        def activate(span, total):
            pre = u_s[span, :] + bias
            square = pre * pre
            tanh = jnp.tanh(ROOT * pre * (1.0 + CUBE * square))
            outer = 0.5 + 0.5 * tanh
            act_s[span, :] = (pre * outer).astype(BF16)
            slope = outer + (0.5 * ROOT) * pre * (1.0 - tanh * tanh) * (1.0 + (3 * CUBE) * square)
            low = (g_s[span, :] * slope).astype(BF16)
            du_s[span, :] = low
            return total + fold8(low.astype(F32))

        total = each_tile(activate, zero_sum)
        take_at(k, n_head, "mlp1")
        early[pl.ds(4 + g, 1), :] = row_sum(total)
        for n in range(0, width, tile_n):
            cols = slice(n, n + tile_n)
            acc[:, cols] += mm(act_s[...], wm[g, 1, :, cols])
            dx2[:, cols] += mm_nt(du_s[...], wm[g, 0, cols, :])
        take_at(k, n_head, "mlp2")

        def each_group(*calls):
            for value in range(n_head):
                @pl.when(k == value)
                def _():
                    for call, kind, *rest in calls:
                        call(kind, value, *rest)

        each_group((net.gather_sent, UP), (net.gather_sent, DOWN))
        for n in range(0, width, tile_n):
            cols = slice(n, n + tile_n)
            wm[g, 1, :, cols] = mm_tn(act_s[...], gos[:, cols]).astype(BF16)
        each_group((net.reduce_pass, DOWN, 0))
        take_at(k, n_head, "mlpD")
        for n in range(0, width, tile_n):
            cols = slice(n, n + tile_n)
            wm[g, 0, :, cols] = mm_tn(x2[...], du_s[:, cols]).astype(BF16)
        each_group((net.reduce_pass, UP, 0))
        take_at(k, n_head, "mlpU")
        return state

    lax.fori_loop(0, n_head, units, 0)

    def second_back(span, sums):
        hidden = hid[span, :]
        normed, factor = norm_rows(hidden)
        grad = dx2[span, :]
        grad_out = gos[span, :].astype(F32)
        xl2 = hidden + (acc[span, :] + nrm[5:6, :])
        du_s[span, :] = xl2.astype(BF16)
        scaled = grad * nrm[3:4, :]
        total = grad_out + factor * (
            scaled - lane_mean(scaled) - normed * lane_mean(scaled * normed)
        )
        hid[span, :] = total
        low = total.astype(BF16)
        act_s[span, :] = low
        return (
            sums[0] + fold8(grad * normed),
            sums[1] + fold8(grad),
            sums[2] + fold8(low.astype(F32)),
            sums[3] + fold8(grad_out),
        )

    sums = each_tile(second_back, (zero_sum,) * 4)
    y_copy = load(du_s, y_out, 0)
    early[1:2, :] = row_sum(sums[0])
    early[2:3, :] = row_sum(sums[1])
    early[0:1, :] = row_sum(sums[2])
    early[3:4, :] = row_sum(sums[3])
    event("s", 0, 0)
    take("sb")
    for n in range(0, width, tile_n):
        cols = slice(n, n + tile_n)
        gcs[:, cols] = mm_nt(act_s[...], wa[3, cols, :]).astype(BF16)
    take("gctx")
    for k in range(n_head):
        net.gather_sent(OUT, k)
    for n in range(0, width, tile_n):
        cols = slice(n, n + tile_n)
        wa[3, :, cols] = mm_tn(ctx[...], act_s[:, cols]).astype(BF16)
    for k in range(n_head):
        net.reduce_pass(OUT, k, 0)
    take("dwo")

    def backward_pair(p, state):
        lanes = pl.ds(pl.multiple_of(p * 2 * head_width, 2 * head_width), 2 * head_width)
        keys = ks[:, lanes]
        vals = vs[:, lanes]
        queries = qs[:, lanes] * jnp.asarray(scale, BF16)
        grads = gcs[:, lanes]
        mem_vals = mvs[:, lanes] * flag.astype(BF16)
        for e in range(2):
            head = 2 * p + e
            masked_g = grads * half[e]
            masked_q = queries * half[e]
            masked_k = keys * half[e]
            for r in range(blocks):
                cols = (r + 1) * blk
                span = slice(r * blk, (r + 1) * blk)
                s_s[:, :cols] = mm_nt(masked_g[span], vals[:cols])
                for t in range(0, blk, sub):
                    inner = slice(r * blk + t, r * blk + t + sub)
                    grad = s_s[t : t + sub, :cols]
                    prob = probs[r][head, t : t + sub, :].astype(F32)
                    total = jnp.sum(prob * grad, axis=-1, keepdims=True)
                    ds_s[inner, :cols] = (prob * (grad - total)).astype(BF16)
                value = mm(ds_s[span, :cols], masked_k[:cols])
                if e == 0:
                    dqs[span, lanes] = value
                else:
                    dqs[span, lanes] += value
            for c in range(blocks):
                span = slice(c * blk, (c + 1) * blk)
                key_part = mm_tn(ds_s[c * blk :, span], masked_q[c * blk :])
                val_part = mm_tn(prob_low[head, :, span], masked_g[blk:])
                if c == 0:
                    val_part = val_part + mm_tn(prob_top[head], masked_g[:blk])
                if e == 0:
                    u_s[span, 0:128] = key_part
                    u_s[span, 128:256] = val_part
                else:
                    dks[span, lanes] = (key_part + u_s[span, 0:128]).astype(BF16)
                    dvs[span, lanes] = (val_part + u_s[span, 128:256]).astype(BF16)
            g_s[0:basis, 0:rows] = mm_nt(mem_vals * half[e], grads)
            sum0 = jnp.zeros((8, rows), F32)
            sum1 = sum0
            sum2 = sum0
            for t in range(0, basis, n_tile):
                offset, value = recall_tile(head, t)
                rt_s[t : t + n_tile, :] = value.astype(BF16)
                weighted = g_s[t : t + n_tile, 0:rows] * value
                moment = weighted * offset
                sum0 = sum0 + fold8(weighted)
                sum1 = sum1 + fold8(moment)
                sum2 = sum2 + fold8(moment * offset)
            part = mm(rt_s[...], masked_g * flag.astype(BF16))
            if e == 0:
                u_s[0:basis, 256:384] = part
            else:
                gmv[:, lanes] = (part + u_s[0:basis, 256:384]).astype(BF16)
            one = pl.ds(head, 1)
            centre = cen[one, :]
            inverse = 1.0 / spr[one, :]
            grad_centre = -row_sum(sum1) * inverse
            grad_spread = (row_sum(sum2) * inverse - row_sum(sum0)) * (0.5 * inverse)
            pg[one, :] = grad_centre * centre * (1.0 - centre)
            pg[pl.ds(16 + head, 1), :] = 0.02 * grad_spread * wsg[one, :]
            take_at(p, pairs, ("bwd0", "bwd1")[e])
        return state

    lax.fori_loop(0, pairs, backward_pair, 0)
    y_copy.wait()

    slopes = three_parts(pg[...])
    moments = sum(mm(part, qs[...]) for part in reversed(slopes))
    moments = jnp.where(own_lanes, moments * scale, 0.0)
    pieces = three_parts(moments)
    weight_grads = sum(mm_nt(piece, mks[...]) for piece in reversed(pieces))
    for h in range(heads):
        g, k = divmod(h, per_group)
        middle[2 + g : 3 + g, k * basis : (k + 1) * basis] = weight_grads[h : h + 1, :]
        middle[6 + g : 7 + g, k * basis : (k + 1) * basis] = weight_grads[16 + h : 17 + h, :]
    gmk[...] = (
        (mm_tn(parts[1], pieces[0]) + mm_tn(parts[0], pieces[1])) + mm_tn(parts[0], pieces[0])
    ).astype(BF16)
    for n in range(0, width, tile_n):
        cols = slice(n, n + tile_n)
        high = um[0:32, cols]
        value = (mm_tn(slopes[1], high) + mm_tn(slopes[0], um[32:64, cols])) + mm_tn(
            slopes[0], high
        )
        act_s[:, cols] = (dqs[:, cols] * scale + value).astype(BF16)
    take("mem")

    def bias_sums(span, sums):
        return (
            sums[0] + fold8(act_s[span, :].astype(F32)),
            sums[1] + fold8(dvs[span, :].astype(F32)),
        )

    sums = each_tile(bias_sums, (zero_sum,) * 2)
    middle[0:1, :] = row_sum(sums[0])
    middle[1:2, :] = row_sum(sums[1]) + row_sum(gmv[...].astype(F32))
    event("s", 1, 0)
    take("bias")

    for n in range(0, width, tile_n):
        cols = slice(n, n + tile_n)
        dx2[:, cols] = (
            mm(act_s[...], wa[0, :, cols])
            + mm(dks[...], wa[1, :, cols])
            + mm(dvs[...], wa[2, :, cols])
        )
    take("dx")
    for k in range(n_head):
        net.gather_sent(ATT, k)
    for n in range(0, width, tile_n):
        cols = slice(n, n + tile_n)
        wa[0, :, cols] = mm_tn(act_s[...], xl[:, cols]).astype(BF16)
        wa[1, :, cols] = (
            mm_tn(dks[...], xl[:, cols]) + mm_tn(gmk[...], mcs[:, cols])
        ).astype(BF16)
        wa[2, :, cols] = (
            mm_tn(dvs[...], xl[:, cols]) + mm_tn(gmv[...], mcs[:, cols])
        ).astype(BF16)

    for k in range(n_head):
        net.reduce_pass(ATT, k, 0)
    take("dwa")

    def first_back(span, sums):
        normed, factor = norm_rows(xs[span, :].astype(F32))
        grad = dx2[span, :]
        scaled = grad * nrm[0:1, :]
        total = hid[span, :] + factor * (
            scaled - lane_mean(scaled) - normed * lane_mean(scaled * normed)
        )
        du_s[span, :] = total.astype(BF16)
        return (sums[0] + fold8(grad * normed), sums[1] + fold8(grad))

    sums = each_tile(first_back, (zero_sum,) * 2)
    late[0:1, :] = row_sum(sums[0])
    late[1:2, :] = row_sum(sums[1])
    event("s", 2, 0)
    outs = [load(du_s, dx_out, 0)]
    take("fb")
    finished = {
        ("f", ATT, 3): (fin[ATT], dqkv_out, 1),
        ("f", OUT, 3): (fin[OUT], dout_out, 2),
        ("f", UP, 3): (fin[UP], dmlp_out.at[pl.ds(0, 1)], 3),
        ("f", DOWN, 3): (fin[DOWN], dmlp_out.at[pl.ds(1, 1)], 4),
    }
    for item in SCHEDULE["tail"]:
        event(*item)
        if item in finished:
            outs.append(load(*finished[item]))
    small[0:2, :] = late[0:2, :]
    small[2:6, :] = early[0:4, :]
    small[6:7, :] = early[pl.ds(4 + me, 1), :]
    for row in range(2):
        own = middle[row : row + 1, :]
        for g in range(1, n_head):
            own = jnp.where(me == g, pltpu.roll(middle[row : row + 1, :], width - g * gcols, 1), own)
        small[7 + row : 8 + row, :] = own
    for row in range(2):
        own = middle[pl.ds(2 + 4 * row + me, 1), :]
        for k in range(per_group):
            maps_s[row, k : k + 1, :] = own[:, k * basis : (k + 1) * basis]
    outs.append(load(maps_s, maps_out, 6))
    outs.append(load(small, small_out, 5))
    net.all_sent()
    for j in range(1, n_head):
        net.aux_copy(aux, j).wait_send()
    for copy in outs:
        copy.wait()


def per_device(
    n_batch, n_head,
    layer_input, memory_flags, document_start, memory_coefficients,
    first_gain, first_shift, query_weight, query_bias, key_matrix, value_matrix,
    value_offset_bias, out_weight, out_bias, second_gain, second_shift,
    up_weight, up_bias, down_weight, down_bias, centre_weight, width_weight, grad_output,
):
    rows, width = layer_input.shape
    basis = memory_coefficients.shape[1]
    gcols = query_weight.shape[1]
    heads = centre_weight.shape[0] * n_head
    att = jnp.stack([query_weight.T, key_matrix.T, value_matrix.T, out_weight])

    extra = 0
    while SUB << extra < n_batch:
        extra += 1

    def vm(*shape, dtype=BF16):
        return pltpu.VMEM(shape, dtype)

    any_spec = pl.BlockSpec(memory_space=pl.ANY)
    smem = pl.BlockSpec(memory_space=pltpu.SMEM)
    vec = pl.BlockSpec(memory_space=pltpu.VMEM)
    dma = pltpu.SemaphoreType.DMA
    halves = ((3, gcols), (1, gcols), (1, width), (1, width))
    recv = tuple(
        tuple(vm(n_head, t, r // pieces, width // 2) for t, r in halves) for pieces in (1, 2, 4, 4)
    )
    y, dx, dqkv, dout, dmlp, small, maps = pl.pallas_call(
        lambda *refs: layer_kernel(n_batch, n_head, *refs),
        out_shape=(
            jax.ShapeDtypeStruct((rows, width), BF16),
            jax.ShapeDtypeStruct((rows, width), BF16),
            jax.ShapeDtypeStruct((3, gcols, width), BF16),
            jax.ShapeDtypeStruct((1, gcols, width), BF16),
            jax.ShapeDtypeStruct((2, width, width), BF16),
            jax.ShapeDtypeStruct((16, width), F32),
            jax.ShapeDtypeStruct((2, heads // n_head, basis), F32),
        ),
        in_specs=[smem, smem, (vec,) * 6, (vec,) * 3, (vec,) * 2] + [any_spec] * 6,
        out_specs=[any_spec] * 7,
        scratch_shapes=[
            vm(rows, width), vm(rows, width), vm(basis, width),
            vm(4, width, width), vm(n_head, 2, width, width),
            vm(n_head, 8, width, dtype=F32), vm(8, width, dtype=F32),
            vm(rows, width), vm(rows, width), vm(rows, width), vm(rows, width),
            vm(basis, width), vm(basis, width), vm(rows, width),
            vm(heads, rows // 2, rows // 2), vm(heads, rows // 2, rows),
            vm(rows, width, dtype=F32), vm(rows, width),
            vm(rows, width, dtype=F32), vm(rows, width, dtype=F32),
            vm(rows, width, dtype=F32), vm(rows, width, dtype=F32),
            vm(rows, width), vm(rows, width), vm(basis, rows),
            vm(32, basis, dtype=F32), vm(96, width),
            vm(16, rows, dtype=F32), vm(16, rows, dtype=F32), vm(16, rows, dtype=F32),
            vm(16, rows, dtype=F32), vm(16, rows, dtype=F32), vm(32, rows, dtype=F32),
            vm(16, width, dtype=F32),
            vm(2, heads // n_head, basis, dtype=F32),
            tuple(
                (vm(r, width, dtype=F32), vm(3 + extra, r, width, dtype=F32),
                 vm(n_head, r, width, dtype=F32)) for r in (8, 16, 8)
            ),
            recv,
            tuple(vm(t, r, width) for t, r in halves),
            tuple(vm(extra, t, r // 4, width // 2) for t, r in halves) if extra else (),
            (dma((4, n_head, 4)), dma((4, n_head, 4)), dma((4, n_head)), dma((4, n_head, 4)), dma((4, n_head, 4)),
             dma((4, 3)), dma((4, 3)), dma((4, max(extra, 1))), dma((4, max(extra, 1))),
             dma((3, 3 + extra + n_head)),
             dma((3, 3 + extra + n_head)), dma((n_head,)), dma((n_head,))),
            dma((8,)),
        ],
        compiler_params=pltpu.CompilerParams(
            collective_id=0, has_side_effects=True, vmem_limit_bytes=67043328
        ),
    )(memory_flags, document_start,
      (first_gain, first_shift, out_bias, second_gain, second_shift, down_bias),
      (query_bias, value_offset_bias, up_bias), (centre_weight, width_weight),
      layer_input, grad_output, memory_coefficients, att, up_weight, down_weight)
    return (
        y, dx, small[0], small[1],
        dqkv[0].T.astype(F32), small[7, :gcols], dqkv[1].T.astype(F32), dqkv[2].T.astype(F32), small[8, :gcols],
        dout[0].astype(F32),
        small[2], small[3], small[4],
        dmlp[0].astype(F32), small[6], dmlp[1].astype(F32), small[5],
        maps[0], maps[1],
    )


def solution(mesh):
    n_batch, n_head = mesh.shape["batch"], mesh.shape["head"]
    tokens = P(("batch", "head"), None)
    cols, rows, split, whole = P(None, "head"), P("head", None), P("head"), P()
    placed = (
        tokens, P("batch"), P("batch"), P("batch", None, None), whole, whole, cols, split, cols,
        cols, split, rows, whole, whole, whole, cols, split, rows, whole, rows, rows, tokens,
    )
    outs = (
        tokens, tokens, whole, whole, cols, split, cols, cols, split, rows, whole, whole, whole,
        cols, split, rows, whole, rows, rows,
    )
    return jax.shard_map(
        lambda *args: per_device(n_batch, n_head, *args),
        mesh=mesh, in_specs=placed, out_specs=outs, check_vma=False,
    )
```

```python
import math

import jax
import jax.numpy as jnp
from jax import lax
from jax.experimental import pallas as pl
from jax.experimental.pallas import tpu as pltpu
from jax.sharding import PartitionSpec as P

F32 = jnp.float32
BF16 = jnp.bfloat16
EPS = 1e-05
ROOT = math.sqrt(2.0 / math.pi)
CUBE = 0.044715
ROW_TILE = 128


def mm(left, right):
    return lax.dot_general(left, right, (((1,), (0,)), ((), ())), preferred_element_type=F32)


def mm_nt(left, right):
    return lax.dot_general(left, right, (((1,), (1,)), ((), ())), preferred_element_type=F32)


def mm_tn(left, right):
    return lax.dot_general(left, right, (((0,), (0,)), ((), ())), preferred_element_type=F32)


def three_parts(value):
    high = value.astype(BF16)
    rest = value - high.astype(F32)
    middle = rest.astype(BF16)
    low = (rest - middle.astype(F32)).astype(BF16)
    return high, middle, low


def lane_mean(value):
    return jnp.mean(value, axis=-1, keepdims=True)


def norm_rows(value):
    center = value - lane_mean(value)
    factor = lax.rsqrt(lane_mean(center * center) + EPS)
    return center * factor, factor


def fold8(value):
    return jnp.sum(value.reshape(value.shape[0] // 8, 8, value.shape[1]), axis=0)


def row_sum(value):
    return jnp.sum(value, axis=0, keepdims=True)


ATT, OUT, UP, DOWN, QUERY, KEY, VALUE = range(7)
SUMMED = (OUT, UP, DOWN, QUERY, KEY, VALUE)
ALL_GROUPS = (OUT, QUERY, KEY, VALUE)
DIRECT = (ATT, OUT)
SPANS = {ATT: (0, 3), OUT: (3, 1), QUERY: (0, 1), KEY: (1, 1), VALUE: (2, 1)}
EARLY = (DOWN, 1)
MESH = pl.DeviceIdType.MESH
SUB = 8


def nearest_first(place, count):
    pair = place + 1 - 2 * (place % 2)
    return sorted(range(count), key=lambda other: (abs(other - place), other != pair))


def pick(index, values):
    chosen = values[0]
    for at, value in enumerate(values[1:], 1):
        chosen = jnp.where(index == at, value, chosen)
    return chosen


class Exchange:
    def __init__(self, n_batch, n_head, wa, wm, recv, early, fin, more, smalls, sems):
        self.n_head, self.smalls, self.early = n_head, smalls, early
        self.wa, self.wm = wa, wm
        self.recv, self.fin, self.more = recv, fin, more
        (self.ag_s, self.ag_r, self.ag_o, self.early_s, self.early_r, self.rs_s, self.rs_r, self.fin_s, self.fin_r, self.ex_s, self.ex_r,
         self.sm_s, self.sm_r, self.ax_s, self.ax_r) = sems
        b, h = lax.axis_index("batch"), lax.axis_index("head")
        self.b, self.h = b, h
        core, x, y = lax.rem(b, 2), lax.rem(lax.div(b, 2), 2), lax.rem(lax.div(b, 4), 2)
        self.core = core
        across_x, across_y = b + 2 - 4 * x, b + 4 - 8 * y
        self.mate = b + 1 - 2 * core
        self.near = across_x + core * (across_y - across_x)
        self.far = across_y + core * (across_x - across_y)
        self.high = y + core * (x - y)
        self.low = x + core * (y - x)
        self.quarter = 2 * self.high + self.low
        self.other_quarter = 2 * self.high + 1 - self.low
        self.extra = []
        step = SUB
        while step < n_batch:
            bit = lax.rem(lax.div(b, step), 2)
            self.extra.append(b + step - 2 * step * bit)
            step *= 2
        orders = [nearest_first(place, n_head) for place in range(n_head)]
        self.groups = [
            h if k == 0 else pick(h, [order[k] for order in orders]) for k in range(n_head)
        ]
        self.places = [
            pick(h, [orders[orders[place][k]].index(place) for place in range(n_head)])
            for k in range(n_head)
        ]
        self.half_width = wm.shape[-1] // 2
        self.rows = [wm.shape[2] if k in (UP, DOWN) else wa.shape[1] // n_head for k in range(7)]
        self.pending = []

    def barrier(self):
        signal = pltpu.get_barrier_semaphore()
        peers = [(p, self.h) for p in [self.mate, self.near, self.far] + self.extra]
        peers += [(self.b, self.turn(k)) for k in range(1, self.n_head)]
        for peer in peers:
            pl.semaphore_signal(signal, inc=1, device_id=peer, device_id_type=MESH)
        pl.semaphore_wait(signal, len(peers))

    def group(self, k):
        return self.groups[k]

    def turn(self, j):
        return lax.rem(self.h + j, self.n_head)

    def cols(self, which):
        return pl.ds(pl.multiple_of(which * self.half_width, 128), self.half_width)

    def view(self, kind, k, start, count, cols):
        g = self.group(k)
        if kind in (UP, DOWN):
            return self.wm.at[g, pl.ds(kind - UP, 1), pl.ds(pl.multiple_of(start, 16), count), cols]
        first, many = SPANS[kind]
        offset = pl.multiple_of(g * self.rows[kind] + start, 16)
        return self.wa.at[pl.ds(first, many), pl.ds(offset, count), cols]

    def part(self, kind, k, pieces, index, cols):
        count = self.rows[kind] // pieces
        return self.view(kind, k, index * count, count, cols)

    def copy(self, src, dst, send, recv, peer):
        return pltpu.make_async_remote_copy(
            src_ref=src, dst_ref=dst, send_sem=send, recv_sem=recv,
            device_id=peer, device_id_type=MESH,
        )

    def own_sends(self, kind):
        own = self.part(kind, 0, 4, self.quarter, self.cols(self.core))
        if kind in DIRECT:
            targets = [(self.group(k), None) for k in range(1, self.n_head)]
        else:
            targets = [(self.h + 1, self.h < self.n_head - 1), (self.h - 1, self.h > 0)]
        for at, (target, allowed) in enumerate(targets):
            copy = self.copy(
                own, own, self.ag_s.at[kind, at, 0], self.ag_r.at[kind, self.h, 0],
                (self.b, target),
            )
            yield copy, allowed

    def gather_start(self, kind):
        for copy, allowed in self.own_sends(kind):
            if allowed is None:
                copy.start()
            else:
                pl.when(allowed)(copy.start)

    def onward(self, kind, k):
        g = self.group(k)
        ref = self.part(kind, k, 4, self.quarter, self.cols(self.core))
        target = jnp.where(g < self.h, self.h + 1, self.h - 1)
        copy = self.copy(
            ref, ref, self.ag_o.at[kind, k], self.ag_r.at[kind, g, 0], (self.b, target)
        )
        return copy, (target >= 0) & (target < self.n_head)

    def pass_on(self, kind, k):
        copy, allowed = self.onward(kind, k)

        @pl.when(allowed)
        def _():
            self.gather_step(kind, k, 0, receive=True).wait_recv()
            copy.start()

    def gather_step(self, kind, k, stage, receive=False):
        mine = self.cols(self.core)
        if stage == 0:
            ref = self.part(kind, k, 4, self.quarter, mine)
            peer = (self.b, self.group(k))
        elif stage == 1:
            which = self.other_quarter if receive else self.quarter
            ref = self.part(kind, k, 4, which, mine)
            peer = (self.near, self.h)
        elif stage == 2:
            ref = self.part(kind, k, 2, 1 - self.high if receive else self.high, mine)
            peer = (self.far, self.h)
        else:
            ref = self.part(kind, k, 1, 0, self.cols(1 - self.core) if receive else mine)
            peer = (self.mate, self.h)
        at = self.group(k) if stage == 0 else k
        return self.copy(
            ref, ref, self.ag_s.at[kind, k, stage], self.ag_r.at[kind, at, stage], peer
        )

    def gather_pass(self, kind, k, stage):
        arrived = self.gather_step(kind, k, stage - 1, receive=True)
        if stage == 1 and kind not in DIRECT:
            for other in range(1, self.n_head):
                if max(other - 1, 1) == k:
                    self.pass_on(kind, other)
            pl.when(jnp.logical_not(self.onward(kind, k)[1]))(arrived.wait_recv)
        else:
            arrived.wait_recv()
        if stage < 4:
            self.gather_step(kind, k, stage).start()

    def gather_sent(self, kind, k):
        if k == 0:
            for copy, allowed in self.own_sends(kind):
                if allowed is None:
                    copy.wait_send()
                else:
                    pl.when(allowed)(copy.wait_send)
            return
        for stage in (1, 2, 3):
            self.gather_step(kind, k, stage).wait_send()
        if kind not in DIRECT:
            copy, allowed = self.onward(kind, k)
            pl.when(allowed)(copy.wait_send)

    def reduce_step(self, kind, k, stage, receive=False):
        mine = self.cols(self.core)
        if stage == 0:
            src, peer = self.part(kind, k, 1, 0, self.cols(1 - self.core)), (self.mate, self.h)
        elif stage == 1:
            src, peer = self.part(kind, k, 2, 1 - self.high, mine), (self.far, self.h)
        elif stage == 2:
            src, peer = self.part(kind, k, 4, self.other_quarter, mine), (self.near, self.h)
        else:
            src, peer = self.part(kind, k, 4, self.quarter, mine), (self.b, self.group(k))
        at = k
        if stage == 3 and not receive:
            at = self.places[k]
        return self.copy(
            src, self.recv[stage][kind - 1].at[at], self.rs_s.at[kind, k, stage],
            self.rs_r.at[kind, at, stage], peer,
        )

    def add_rows(self, kind, k, start, count, received, out=None):
        mine = self.cols(self.core)
        own = self.view(kind, k, start, count, mine)
        target = own if out is None else out
        sources = [buf.at[:, pl.ds(pl.multiple_of(start - base, 16), count), :] for buf, base in received]
        kinds = own.shape[0]
        tile = min(count, 192)

        for t in range(kinds):
            def step(i, state):
                span = pl.ds(pl.multiple_of(i * tile, 16), tile)
                if len(sources) == 1:
                    target[t, span, :] = own[t, span, :] + sources[0][t, span, :]
                    return state
                total = own[t, span, :].astype(F32)
                for source in sources:
                    total = total + source[t, span, :].astype(F32)
                target[t, span, :] = total.astype(BF16)
                return state

            lax.fori_loop(0, count // tile, step, 0)

    def early_copy(self):
        kind, k = EARLY
        src = self.part(kind, k, 1, 0, self.cols(self.core))
        return self.copy(
            src, self.early.at[0], self.early_s, self.early_r, (self.b, self.group(k))
        )

    def reduce_pass(self, kind, k, stage):
        rows = self.rows[kind]
        half, quarter = rows // 2, rows // 4
        first, second, third = (self.recv[s][kind - 1].at[k] for s in range(3))
        if stage > 0:
            self.reduce_step(kind, k, stage - 1).wait_recv()
        if (kind, k) == EARLY and stage == 1:
            self.add_rows(kind, k, 0, rows, [(first, 0)])
            self.early_copy().start()
            return
        kept = self.high * half
        parts = [(first, 0)]
        if kind == EARLY[0] and k == 0:
            parts.append((self.early.at[0], 0))
            if stage == 1:
                self.early_copy().wait_recv()
        if stage == 1:
            self.add_rows(kind, k, (1 - self.high) * half, half, parts)
        elif stage == 2:
            self.add_rows(
                kind, k, self.other_quarter * quarter, quarter, parts + [(second, kept)]
            )
        elif stage == 3:
            own = self.quarter * quarter
            self.add_rows(kind, k, own, quarter, parts + [(second, kept), (third, own)])
        if stage < 3 or k > 0:
            self.reduce_step(kind, k, stage).start()

    def late(self, kind):
        return [k for k in range(1, self.n_head) if (kind, k) != EARLY]

    def fin_part(self, kind, pieces, index, cols):
        count = self.rows[kind] // pieces
        return self.fin[kind - 1].at[:, pl.ds(pl.multiple_of(index * count, 16), count), cols]

    def final_step(self, kind, stage, receive=False):
        mine = self.cols(self.core)
        if stage == 0:
            which = self.other_quarter if receive else self.quarter
            ref, peer = self.fin_part(kind, 4, which, mine), (self.near, self.h)
        elif stage == 1:
            which = 1 - self.high if receive else self.high
            ref, peer = self.fin_part(kind, 2, which, mine), (self.far, self.h)
        else:
            ref = self.fin_part(kind, 1, 0, self.cols(1 - self.core) if receive else mine)
            peer = (self.mate, self.h)
        return self.copy(ref, ref, self.fin_s.at[kind, stage], self.fin_r.at[kind, stage], peer)

    def final_pass(self, kind, stage):
        if stage == 0:
            for k in self.late(kind):
                self.reduce_step(kind, k, 3, receive=True).wait_recv()
            quarter = self.rows[kind] // 4
            last = self.recv[3][kind - 1]
            mine = self.cols(self.core)
            own = self.view(kind, 0, self.quarter * quarter, quarter, mine)
            target = self.fin_part(kind, 4, self.quarter, mine)
            tile = min(quarter, 192)
            for t in range(own.shape[0]):
                def step(i, state):
                    span = pl.ds(pl.multiple_of(i * tile, 16), tile)
                    total = own[t, span, :].astype(F32)
                    for k in self.late(kind):
                        total = total + last[k, t, span, :].astype(F32)
                    target[t, span, :] = total.astype(BF16)
                    return state

                lax.fori_loop(0, quarter // tile, step, 0)
            for e, peer in enumerate(self.extra):
                copy = self.copy(
                    target, self.more[kind - 1].at[e], self.ex_s.at[kind, e], self.ex_r.at[kind, e],
                    (peer, self.h),
                )
                copy.start()
                copy.wait()
                for t in range(own.shape[0]):
                    total = target[t].astype(F32) + self.more[kind - 1][e, t].astype(F32)
                    target[t] = total.astype(BF16)
        else:
            self.final_step(kind, stage - 1, receive=True).wait_recv()
        if stage < 3:
            self.final_step(kind, stage).start()

    def all_sent(self):
        self.early_copy().wait_send()
        for kind in SUMMED:
            for k in range(self.n_head):
                stages = range(1) if (kind, k) == EARLY else range(4 if k > 0 else 3)
                for stage in stages:
                    self.reduce_step(kind, k, stage).wait_send()
            for stage in range(3):
                self.final_step(kind, stage).wait_send()

    def aux_copy(self, aux, j):
        own = aux.at[self.h]
        return self.copy(
            own, own, self.ax_s.at[j], self.ax_r.at[self.n_head - j], (self.b, self.turn(j))
        )

    def aux_wait(self, aux, k):
        own = aux.at[self.turn(k)]
        self.copy(own, own, self.ax_s.at[k], self.ax_r.at[k], (self.b, self.turn(k))).wait_recv()

    def small_step(self, which, stage, j=0):
        value, got, all_heads = self.smalls[which]
        peers = [self.mate, self.near, self.far]
        if stage < 3:
            src, dst, peer, at = value, got.at[stage], (peers[stage], self.h), stage
        else:
            src, dst, peer, at = value, all_heads.at[self.h], (self.b, self.turn(j)), 2 + j
        return self.copy(src, dst, self.sm_s.at[which, at], self.sm_r.at[which, at], peer)

    def small_pass(self, which, stage):
        value, got, all_heads = self.smalls[which]
        if stage == 0:
            self.small_step(which, 0).start()
        elif stage <= 3:
            self.small_step(which, stage - 1).wait()
            value[...] = value[...] + got[stage - 1]
            if stage < 3:
                self.small_step(which, stage).start()
                return
            first = 2 + self.n_head
            for e, peer in enumerate(self.extra):
                copy = self.copy(
                    value, got.at[3 + e], self.sm_s.at[which, first + e],
                    self.sm_r.at[which, first + e], (peer, self.h),
                )
                copy.start()
                copy.wait()
                value[...] = value[...] + got[3 + e]
            for j in range(1, self.n_head):
                self.small_step(which, 3, j).start()
            all_heads[self.h] = value[...]
        else:
            for j in range(1, self.n_head):
                self.small_step(which, 3, j).wait()
            total = all_heads[0]
            for g in range(1, self.n_head):
                total = total + all_heads[g]
            value[...] = total


SCHEDULE = {
    "needA": (("g", 0, 1, 1), ("g", 0, 1, 2), ("g", 0, 2, 1), ("g", 1, 2, 1), ("g", 0, 3, 1), ("g", 1, 1, 1), ("g", 0, 1, 3), ("g", 0, 2, 2), ("g", 1, 2, 2), ("g", 0, 1, 4), ("g", 1, 3, 1), ("g", 0, 3, 2), ("g", 1, 1, 2), ("g", 0, 2, 3), ("g", 1, 3, 2), ("g", 2, 1, 1), ("g", 1, 2, 3), ("g", 0, 2, 4), ("g", 3, 1, 1), ("g", 2, 2, 1), ("g", 0, 3, 3), ("g", 2, 1, 2), ("g", 1, 1, 3), ("g", 0, 3, 4),),
    ("proj", 0): (("g", 3, 2, 1),),
    ("proj", 1): (("g", 1, 3, 3),),
    ("proj", 2): (("g", 3, 1, 2),),
    ("fwd", 1): (("g", 2, 2, 2), ("g", 2, 3, 1),),
    ("fwd", 3): (("g", 2, 1, 3), ("g", 3, 2, 2), ("g", 3, 3, 1),),
    "needO": (("g", 1, 2, 4), ("g", 1, 1, 4), ("g", 1, 3, 4),),
    "out": (("g", 2, 3, 2),),
    ("mlp0", 0): (("g", 3, 1, 3),),
    ("mlp1", 0): (("g", 3, 3, 2),),
    ("mlp2", 0): (("g", 2, 2, 3),),
    ("needU", 1): (("g", 2, 1, 4),),
    ("mlp0", 1): (("g", 3, 2, 3),),
    ("needD", 1): (("g", 3, 1, 4),),
    ("mlp1", 1): (("r", 2, 0, 1),),
    ("mlp2", 1): (("g", 2, 3, 3),),
    ("needU", 2): (("g", 2, 2, 4),),
    ("mlp0", 2): (("g", 3, 3, 3), ("r", 3, 1, 1),),
    ("needD", 2): (("g", 3, 2, 4),),
    ("mlp1", 2): (("r", 2, 0, 2), ("r", 2, 1, 1),),
    ("needU", 3): (("g", 2, 3, 4),),
    ("mlp0", 3): (("r", 3, 2, 1), ("r", 2, 2, 1), ("r", 2, 0, 3),),
    ("needD", 3): (("g", 3, 3, 4),),
    ("mlp1", 3): (("r", 2, 1, 2),),
    ("mlpD", 3): (("r", 3, 2, 2),),
    "sb": (("r", 2, 3, 1), ("r", 2, 1, 3), ("r", 3, 0, 1), ("r", 3, 3, 1),),
    "dwo": (("r", 2, 2, 2), ("s", 0, 1), ("r", 3, 2, 3),),
    ("bwd0", 0): (("r", 1, 0, 1),),
    ("bwd0", 1): (("r", 2, 3, 2),),
    ("bwd1", 1): (("r", 2, 2, 3), ("s", 0, 2),),
    ("bwd1", 3): (("r", 3, 0, 2), ("r", 2, 3, 3),),
    ("bwd0", 5): (("r", 3, 3, 2),),
    "dwv": (("r", 3, 0, 3), ("r", 6, 0, 1),),
    "mem": (("s", 0, 3), ("r", 1, 0, 2), ("r", 3, 3, 3),),
    "dwk": (("s", 1, 1), ("f", 2, 0), ("r", 5, 0, 1),),
    "dwq": (("s", 1, 2), ("r", 6, 0, 2), ("r", 4, 0, 1), ("r", 1, 0, 3),),
    "fb": (("s", 2, 1),),
    "tail": (("s", 0, 4), ("f", 2, 1), ("r", 5, 0, 2), ("r", 6, 0, 3), ("f", 3, 0), ("s", 2, 2), ("s", 1, 3), ("f", 1, 0), ("r", 5, 0, 3), ("r", 4, 0, 2), ("f", 6, 0), ("f", 3, 1), ("f", 1, 1), ("r", 4, 0, 3), ("s", 1, 4), ("f", 2, 2), ("f", 6, 1), ("s", 2, 3), ("f", 2, 3), ("f", 5, 0), ("f", 3, 2), ("f", 1, 2), ("f", 5, 1), ("f", 3, 3), ("f", 6, 2), ("f", 1, 3), ("f", 4, 0), ("f", 6, 3), ("f", 5, 2), ("s", 2, 4), ("f", 4, 1), ("f", 5, 3), ("f", 4, 2), ("f", 4, 3),),
}

def layer_kernel(
    n_batch, n_head,
    flags, bounds, norm_in, bias_in, map_in, x_in, go_in, mc_in, att_in, up_in, down_in,
    y_out, dx_out, dqkv_out, dout_out, dmlp_out, small_out, maps_out,
    xs, gos, mcs, wa, wm, aux, nrm,
    xl, qs, ks, vs, mks, mvs, ctx, prob_top, prob_low, hid, x2, acc, dx2,
    u_s, g_s, act_s, du_s, rt_s,
    cwm, um, cen, spr, wsg, isp, nrs, pg, small,
    maps_s, smalls, recv, ahead, fin, more, links, sems,
):
    gcs, dqs, dks, dvs, gmk, gmv = x2, acc, ks, vs, mks, mvs
    me = lax.axis_index("head")
    rows, width = xs.shape
    heads = prob_low.shape[0]
    blocks = 2
    blk = rows // blocks
    probs = (prob_top, prob_low)
    mask = dx2.at[:, 0:rows]
    s_s = g_s.at[blk:rows, 0:rows]
    ds_s = act_s.at[:, 0:rows]
    pairs = heads // 2
    basis = mcs.shape[0]
    gcols = width // n_head
    tiles = rows // ROW_TILE

    def load(src, dst, index):
        copy = pltpu.make_async_copy(src, dst, sems.at[index])
        copy.start()
        return copy

    others = range(1, n_head)
    net = Exchange(n_batch, n_head, wa, wm, recv, ahead, fin, more, smalls, links)
    att_copies = [load(att_in, wa.at[:, pl.ds(pl.multiple_of(me * gcols, 16), gcols), :], 5)]
    copies = [
        load(x_in, xs, 0),
        load(mc_in.at[me], mcs, 2),
        load(go_in, gos, 4),
    ]
    mlp_copies = [load(up_in, wm.at[me, 0], 6), load(down_in, wm.at[me, 1], 7)]
    for row, ref in enumerate(norm_in):
        nrm[row : row + 1, :] = ref[...].astype(F32).reshape(1, width)
    aux[me] = jnp.zeros((8, width), F32)
    for row, ref in enumerate(bias_in[:2]):
        aux[me, row : row + 1, 0:gcols] = ref[...].astype(F32).reshape(1, gcols)
    aux[me, 2:3, :] = bias_in[2][...].astype(F32).reshape(1, width)
    for row, ref in enumerate(map_in):
        for k in range(ref.shape[0]):
            aux[me, 3 + row : 4 + row, k * basis : (k + 1) * basis] = ref[k : k + 1, :]
    net.barrier()
    for copy in att_copies:
        copy.wait()
    net.gather_start(ATT)
    for j in range(1, n_head):
        net.aux_copy(aux, j).start()
    net.gather_start(OUT)
    for copy in mlp_copies:
        copy.wait()
    net.gather_start(UP)
    net.gather_start(DOWN)

    def event(op, first, *rest):
        if op == "g":
            net.gather_pass(first, *rest)
        elif op == "r":
            group, stage = rest
            for k in range(n_head) if first in ALL_GROUPS else (group,):
                net.reduce_pass(first, k, stage)
        elif op == "f":
            net.final_pass(first, *rest)
        else:
            net.small_pass(first, *rest)

    def take(slot):
        for item in SCHEDULE.get(slot, ()):
            event(*item)

    def take_at(index, count, slot):
        for value in range(count):
            if (slot, value) in SCHEDULE:
                @pl.when(index == value)
                def _():
                    take((slot, value))


    flag = flags[me].astype(F32)
    bound = bounds[me]

    def each_tile(body, carry=0):
        def step(i, state):
            return body(pl.ds(pl.multiple_of(i * ROW_TILE, ROW_TILE), ROW_TILE), state)

        return lax.fori_loop(0, tiles, step, carry)

    early, middle, late = (group[0] for group in smalls)
    for ref in (middle, late):
        ref[...] = jnp.zeros_like(ref)
    zero_sum = jnp.zeros((8, width), F32)

    def mask_rows(span, state):
        row_ids = lax.broadcasted_iota(jnp.int32, (ROW_TILE, rows), 0) + span.start
        col_ids = lax.broadcasted_iota(jnp.int32, (ROW_TILE, rows), 1)
        least = jnp.where(row_ids < bound, 0, bound)
        allowed = (col_ids <= row_ids) & (col_ids >= least)
        mask[span, :] = jnp.where(allowed, 0.0, -jnp.inf).astype(F32)
        return state

    each_tile(mask_rows)
    for copy in copies:
        copy.wait()

    def first_norm(span, state):
        normed, _ = norm_rows(xs[span, :].astype(F32))
        xl[span, :] = (normed * nrm[0:1, :] + nrm[1:2, :]).astype(BF16)
        return state

    each_tile(first_norm)
    take("ln1")
    take("needA")
    for k in others:
        net.aux_wait(aux, k)

    column = lax.broadcasted_iota(jnp.int32, (1, width), 1)
    biases = []
    for row in range(2):
        bias = jnp.zeros((1, width), F32)
        for g in range(n_head):
            moved = aux[g, row : row + 1, :]
            shift = g * gcols
            if shift:
                moved = pltpu.roll(moved, shift, 1)
            bias = bias + jnp.where(column // gcols == g, moved, 0.0)
        biases.append(bias)

    tile_n = 256
    for kind, out, mem_out, bias_row in ((0, qs, None, 0), (1, ks, mks, None), (2, vs, mvs, 1)):
        for n in range(0, width, tile_n):
            cols = slice(n, n + tile_n)
            weight = wa[kind, cols, :]
            value = mm_nt(xl[...], weight)
            if bias_row is not None:
                value = value + biases[bias_row][:, cols]
            out[:, cols] = value.astype(BF16)
            if mem_out is not None:
                value = mm_nt(mcs[...], weight)
                if bias_row is not None:
                    value = value + biases[bias_row][:, cols]
                mem_out[:, cols] = value.astype(BF16)
        take(("proj", kind))

    cwm[...] = jnp.zeros_like(cwm)
    per_group = heads // n_head
    for h in range(heads):
        g, k = divmod(h, per_group)
        cwm[h : h + 1, :] = aux[g, 3:4, k * basis : (k + 1) * basis]
        cwm[16 + h : 17 + h, :] = aux[g, 4:5, k * basis : (k + 1) * basis]
    head_width = width // heads
    own_lanes = (
        lax.broadcasted_iota(jnp.int32, (32, width), 0) % 16
        == lax.broadcasted_iota(jnp.int32, (32, width), 1) // head_width
    )
    scale = head_width ** (-0.5)
    parts = three_parts(cwm[...])
    maps = sum(mm(part, mks[...]) for part in reversed(parts))
    maps = jnp.where(own_lanes, maps * scale, 0.0)
    for index, part in enumerate(three_parts(maps)):
        um[32 * index : 32 * index + 32, :] = part
    pre = mm_nt(um[...], qs[...])
    pre = (pre[64:96] + pre[32:64]) + pre[0:32]
    centre = jax.nn.sigmoid(pre[0:16])
    width_pre = pre[16:32]
    spread = 0.02 * (jnp.maximum(width_pre, 0.0) + jnp.log1p(jnp.exp(-jnp.abs(width_pre)))) + 0.01
    cen[...] = centre
    spr[...] = spread
    wsg[...] = jax.nn.sigmoid(width_pre)
    isp[...] = -0.5 / spread
    nrs[...] = lax.rsqrt((2.0 * math.pi) * spread) / basis
    pg[...] = jnp.zeros_like(pg)

    lane = lax.broadcasted_iota(jnp.int32, (1, 2 * head_width), 1)
    half = [
        jnp.where((lane >= head_width) == bool(e), 1.0, 0.0).astype(BF16) for e in range(2)
    ]
    n_tile = 64
    sub = 64

    def recall_tile(head, start):
        ids = lax.broadcasted_iota(jnp.int32, (n_tile, rows), 0).astype(F32)
        offset = cen[pl.ds(head, 1), :] - (ids + (start + 0.5)) / basis
        value = jnp.exp(offset * offset * isp[pl.ds(head, 1), :]) * nrs[pl.ds(head, 1), :]
        return offset, value

    take("maps")

    def forward_pair(p, state):
        lanes = pl.ds(pl.multiple_of(p * 2 * head_width, 2 * head_width), 2 * head_width)
        keys = ks[:, lanes]
        vals = vs[:, lanes]
        queries = qs[:, lanes] * jnp.asarray(scale, BF16)
        mem_vals = mvs[:, lanes] * flag.astype(BF16)
        for e in range(2):
            head = 2 * p + e
            masked_q = queries * half[e]
            masked_v = vals * half[e]
            for r in range(blocks):
                cols = (r + 1) * blk
                s_s[:, :cols] = mm_nt(masked_q[r * blk : (r + 1) * blk], keys[:cols])
                for t in range(0, blk, sub):
                    scores = s_s[t : t + sub, :cols] + mask[r * blk + t : r * blk + t + sub, :cols]
                    shifted = jnp.exp(scores - jnp.max(scores, axis=-1, keepdims=True))
                    inverse = 1.0 / jnp.sum(shifted, axis=-1, keepdims=True)
                    probs[r][head, t : t + sub, :] = (shifted * inverse).astype(BF16)
            for t in range(0, basis, n_tile):
                _, value = recall_tile(head, t)
                rt_s[t : t + n_tile, :] = value.astype(BF16)
            part = mm_tn(rt_s[...], mem_vals * half[e])
            for r in range(blocks):
                cols = (r + 1) * blk
                span = slice(r * blk, (r + 1) * blk)
                value = mm(probs[r][head], masked_v[:cols]) + part[span]
                if e == 0:
                    u_s[span, 0 : 2 * head_width] = value
                else:
                    ctx[span, lanes] = (value + u_s[span, 0 : 2 * head_width]).astype(BF16)
        take_at(p, pairs, "fwd")
        return state

    lax.fori_loop(0, pairs, forward_pair, 0)

    take("needO")

    for n in range(0, width, tile_n):
        hid[:, n : n + tile_n] = mm(ctx[...], wa[3, :, n : n + tile_n])

    take("out")

    def second_norm(span, state):
        hidden = xs[span, :].astype(F32) + (hid[span, :] + nrm[2:3, :])
        hid[span, :] = hidden
        normed, _ = norm_rows(hidden)
        x2[span, :] = (normed * nrm[3:4, :] + nrm[4:5, :]).astype(BF16)
        acc[span, :] = jnp.zeros((ROW_TILE, width), F32)
        dx2[span, :] = jnp.zeros((ROW_TILE, width), F32)
        return state

    each_tile(second_norm)
    take("ln2")

    def units(k, state):
        g = pick(k, net.groups)
        take_at(k, n_head, "needU")
        for n in range(0, width, tile_n):
            cols = slice(n, n + tile_n)
            u_s[:, cols] = mm(x2[...], wm[g, 0, :, cols])
        take_at(k, n_head, "mlp0")
        take_at(k, n_head, "needD")
        for n in range(0, width, tile_n):
            cols = slice(n, n + tile_n)
            g_s[:, cols] = mm_nt(gos[...], wm[g, 1, cols, :])
        bias = aux[g, 2:3, :]

        def activate(span, total):
            pre = u_s[span, :] + bias
            square = pre * pre
            tanh = jnp.tanh(ROOT * pre * (1.0 + CUBE * square))
            outer = 0.5 + 0.5 * tanh
            act_s[span, :] = (pre * outer).astype(BF16)
            slope = outer + (0.5 * ROOT) * pre * (1.0 - tanh * tanh) * (1.0 + (3 * CUBE) * square)
            low = (g_s[span, :] * slope).astype(BF16)
            du_s[span, :] = low
            return total + fold8(low.astype(F32))

        total = each_tile(activate, zero_sum)
        take_at(k, n_head, "mlp1")
        early[pl.ds(4 + g, 1), :] = row_sum(total)
        for n in range(0, width, tile_n):
            cols = slice(n, n + tile_n)
            acc[:, cols] += mm(act_s[...], wm[g, 1, :, cols])
            dx2[:, cols] += mm_nt(du_s[...], wm[g, 0, cols, :])
        take_at(k, n_head, "mlp2")

        def each_group(*calls):
            for value in range(n_head):
                @pl.when(k == value)
                def _():
                    for call, kind, *rest in calls:
                        call(kind, value, *rest)

        each_group((net.gather_sent, UP), (net.gather_sent, DOWN))
        for n in range(0, width, tile_n):
            cols = slice(n, n + tile_n)
            wm[g, 1, :, cols] = mm_tn(act_s[...], gos[:, cols]).astype(BF16)
        each_group((net.reduce_pass, DOWN, 0))
        take_at(k, n_head, "mlpD")
        for n in range(0, width, tile_n):
            cols = slice(n, n + tile_n)
            wm[g, 0, :, cols] = mm_tn(x2[...], du_s[:, cols]).astype(BF16)
        each_group((net.reduce_pass, UP, 0))
        take_at(k, n_head, "mlpU")
        return state

    lax.fori_loop(0, n_head, units, 0)

    def second_back(span, sums):
        hidden = hid[span, :]
        normed, factor = norm_rows(hidden)
        grad = dx2[span, :]
        grad_out = gos[span, :].astype(F32)
        xl2 = hidden + (acc[span, :] + nrm[5:6, :])
        du_s[span, :] = xl2.astype(BF16)
        scaled = grad * nrm[3:4, :]
        total = grad_out + factor * (
            scaled - lane_mean(scaled) - normed * lane_mean(scaled * normed)
        )
        hid[span, :] = total
        low = total.astype(BF16)
        act_s[span, :] = low
        return (
            sums[0] + fold8(grad * normed),
            sums[1] + fold8(grad),
            sums[2] + fold8(low.astype(F32)),
            sums[3] + fold8(grad_out),
        )

    sums = each_tile(second_back, (zero_sum,) * 4)
    y_copy = load(du_s, y_out, 0)
    early[1:2, :] = row_sum(sums[0])
    early[2:3, :] = row_sum(sums[1])
    early[0:1, :] = row_sum(sums[2])
    early[3:4, :] = row_sum(sums[3])
    event("s", 0, 0)
    take("sb")
    for n in range(0, width, tile_n):
        cols = slice(n, n + tile_n)
        gcs[:, cols] = mm_nt(act_s[...], wa[3, cols, :]).astype(BF16)
    take("gctx")
    for k in range(n_head):
        net.gather_sent(OUT, k)
    for n in range(0, width, tile_n):
        cols = slice(n, n + tile_n)
        wa[3, :, cols] = mm_tn(ctx[...], act_s[:, cols]).astype(BF16)
    event("r", OUT, 0, 0)
    take("dwo")

    def backward_pair(p, state):
        lanes = pl.ds(pl.multiple_of(p * 2 * head_width, 2 * head_width), 2 * head_width)
        keys = ks[:, lanes]
        vals = vs[:, lanes]
        queries = qs[:, lanes] * jnp.asarray(scale, BF16)
        grads = gcs[:, lanes]
        mem_vals = mvs[:, lanes] * flag.astype(BF16)
        for e in range(2):
            head = 2 * p + e
            masked_g = grads * half[e]
            masked_q = queries * half[e]
            masked_k = keys * half[e]
            for r in range(blocks):
                cols = (r + 1) * blk
                span = slice(r * blk, (r + 1) * blk)
                s_s[:, :cols] = mm_nt(masked_g[span], vals[:cols])
                for t in range(0, blk, sub):
                    inner = slice(r * blk + t, r * blk + t + sub)
                    grad = s_s[t : t + sub, :cols]
                    prob = probs[r][head, t : t + sub, :].astype(F32)
                    total = jnp.sum(prob * grad, axis=-1, keepdims=True)
                    ds_s[inner, :cols] = (prob * (grad - total)).astype(BF16)
                value = mm(ds_s[span, :cols], masked_k[:cols])
                if e == 0:
                    dqs[span, lanes] = value
                else:
                    dqs[span, lanes] += value
            for c in range(blocks):
                span = slice(c * blk, (c + 1) * blk)
                key_part = mm_tn(ds_s[c * blk :, span], masked_q[c * blk :])
                val_part = mm_tn(prob_low[head, :, span], masked_g[blk:])
                if c == 0:
                    val_part = val_part + mm_tn(prob_top[head], masked_g[:blk])
                if e == 0:
                    u_s[span, 0:128] = key_part
                    u_s[span, 128:256] = val_part
                else:
                    dks[span, lanes] = (key_part + u_s[span, 0:128]).astype(BF16)
                    dvs[span, lanes] = (val_part + u_s[span, 128:256]).astype(BF16)
            g_s[0:basis, 0:rows] = mm_nt(mem_vals * half[e], grads)
            sum0 = jnp.zeros((8, rows), F32)
            sum1 = sum0
            sum2 = sum0
            for t in range(0, basis, n_tile):
                offset, value = recall_tile(head, t)
                rt_s[t : t + n_tile, :] = value.astype(BF16)
                weighted = g_s[t : t + n_tile, 0:rows] * value
                moment = weighted * offset
                sum0 = sum0 + fold8(weighted)
                sum1 = sum1 + fold8(moment)
                sum2 = sum2 + fold8(moment * offset)
            part = mm(rt_s[...], masked_g * flag.astype(BF16))
            if e == 0:
                u_s[0:basis, 256:384] = part
            else:
                gmv[:, lanes] = (part + u_s[0:basis, 256:384]).astype(BF16)
            one = pl.ds(head, 1)
            centre = cen[one, :]
            inverse = 1.0 / spr[one, :]
            grad_centre = -row_sum(sum1) * inverse
            grad_spread = (row_sum(sum2) * inverse - row_sum(sum0)) * (0.5 * inverse)
            pg[one, :] = grad_centre * centre * (1.0 - centre)
            pg[pl.ds(16 + head, 1), :] = 0.02 * grad_spread * wsg[one, :]
            take_at(p, pairs, ("bwd0", "bwd1")[e])
        return state

    lax.fori_loop(0, pairs, backward_pair, 0)
    y_copy.wait()

    def input_share(kind, grads, first):
        for n in range(0, width, tile_n):
            cols = slice(n, n + tile_n)
            value = mm(grads[...], wa[kind, :, cols])
            dx2[:, cols] = value if first else dx2[:, cols] + value

    def weight_share(kind, grads, memory):
        for n in range(0, width, tile_n):
            cols = slice(n, n + tile_n)
            value = mm_tn(grads[...], xl[:, cols])
            if memory is not None:
                value = value + mm_tn(memory[...], mcs[:, cols])
            wa[kind, :, cols] = value.astype(BF16)

    for k in range(n_head):
        net.gather_sent(ATT, k)
    input_share(2, dvs, True)
    weight_share(2, dvs, gmv)
    event("r", VALUE, 0, 0)
    take("dwv")

    slopes = three_parts(pg[...])
    moments = sum(mm(part, qs[...]) for part in reversed(slopes))
    moments = jnp.where(own_lanes, moments * scale, 0.0)
    pieces = three_parts(moments)
    weight_grads = sum(mm_nt(piece, mks[...]) for piece in reversed(pieces))
    for h in range(heads):
        g, k = divmod(h, per_group)
        middle[2 + g : 3 + g, k * basis : (k + 1) * basis] = weight_grads[h : h + 1, :]
        middle[6 + g : 7 + g, k * basis : (k + 1) * basis] = weight_grads[16 + h : 17 + h, :]
    gmk[...] = (
        (mm_tn(parts[1], pieces[0]) + mm_tn(parts[0], pieces[1])) + mm_tn(parts[0], pieces[0])
    ).astype(BF16)
    for n in range(0, width, tile_n):
        cols = slice(n, n + tile_n)
        high = um[0:32, cols]
        value = (mm_tn(slopes[1], high) + mm_tn(slopes[0], um[32:64, cols])) + mm_tn(
            slopes[0], high
        )
        act_s[:, cols] = (dqs[:, cols] * scale + value).astype(BF16)
    take("mem")

    def bias_sums(span, sums):
        return (
            sums[0] + fold8(act_s[span, :].astype(F32)),
            sums[1] + fold8(dvs[span, :].astype(F32)),
        )

    sums = each_tile(bias_sums, (zero_sum,) * 2)
    middle[0:1, :] = row_sum(sums[0])
    middle[1:2, :] = row_sum(sums[1]) + row_sum(gmv[...].astype(F32))
    event("s", 1, 0)
    take("bias")

    input_share(1, dks, False)
    weight_share(1, dks, gmk)
    event("r", KEY, 0, 0)
    take("dwk")
    input_share(0, act_s, False)
    weight_share(0, act_s, None)
    event("r", QUERY, 0, 0)
    take("dwq")

    def first_back(span, sums):
        normed, factor = norm_rows(xs[span, :].astype(F32))
        grad = dx2[span, :]
        scaled = grad * nrm[0:1, :]
        total = hid[span, :] + factor * (
            scaled - lane_mean(scaled) - normed * lane_mean(scaled * normed)
        )
        du_s[span, :] = total.astype(BF16)
        return (sums[0] + fold8(grad * normed), sums[1] + fold8(grad))

    sums = each_tile(first_back, (zero_sum,) * 2)
    late[0:1, :] = row_sum(sums[0])
    late[1:2, :] = row_sum(sums[1])
    event("s", 2, 0)
    outs = [load(du_s, dx_out, 0)]
    take("fb")
    finished = {
        ("f", QUERY, 3): (QUERY, dqkv_out.at[pl.ds(0, 1)], 1),
        ("f", KEY, 3): (KEY, dqkv_out.at[pl.ds(1, 1)], 2),
        ("f", VALUE, 3): (VALUE, dqkv_out.at[pl.ds(2, 1)], 3),
        ("f", OUT, 3): (OUT, dout_out, 4),
        ("f", UP, 3): (UP, dmlp_out.at[pl.ds(0, 1)], 7),
        ("f", DOWN, 3): (DOWN, dmlp_out.at[pl.ds(1, 1)], 8),
    }
    for item in SCHEDULE["tail"]:
        event(*item)
        if item in finished:
            kind, target, at = finished[item]
            outs.append(load(fin[kind - 1], target, at))
    small[0:2, :] = late[0:2, :]
    small[2:6, :] = early[0:4, :]
    small[6:7, :] = early[pl.ds(4 + me, 1), :]
    for row in range(2):
        own = middle[row : row + 1, :]
        for g in range(1, n_head):
            own = jnp.where(me == g, pltpu.roll(middle[row : row + 1, :], width - g * gcols, 1), own)
        small[7 + row : 8 + row, :] = own
    for row in range(2):
        own = middle[pl.ds(2 + 4 * row + me, 1), :]
        for k in range(per_group):
            maps_s[row, k : k + 1, :] = own[:, k * basis : (k + 1) * basis]
    outs.append(load(maps_s, maps_out, 6))
    outs.append(load(small, small_out, 5))
    net.all_sent()
    for j in range(1, n_head):
        net.aux_copy(aux, j).wait_send()
    for copy in outs:
        copy.wait()


def per_device(
    n_batch, n_head,
    layer_input, memory_flags, document_start, memory_coefficients,
    first_gain, first_shift, query_weight, query_bias, key_matrix, value_matrix,
    value_offset_bias, out_weight, out_bias, second_gain, second_shift,
    up_weight, up_bias, down_weight, down_bias, centre_weight, width_weight, grad_output,
):
    rows, width = layer_input.shape
    basis = memory_coefficients.shape[1]
    gcols = query_weight.shape[1]
    heads = centre_weight.shape[0] * n_head
    att = jnp.stack([query_weight.T, key_matrix.T, value_matrix.T, out_weight])

    extra = 0
    while SUB << extra < n_batch:
        extra += 1

    def vm(*shape, dtype=BF16):
        return pltpu.VMEM(shape, dtype)

    any_spec = pl.BlockSpec(memory_space=pl.ANY)
    smem = pl.BlockSpec(memory_space=pltpu.SMEM)
    vec = pl.BlockSpec(memory_space=pltpu.VMEM)
    dma = pltpu.SemaphoreType.DMA
    halves = ((1, gcols), (1, width), (1, width)) + ((1, gcols),) * 3
    recv = tuple(
        tuple(vm(n_head, t, r // pieces, width // 2) for t, r in halves) for pieces in (1, 2, 4, 4)
    )
    y, dx, dqkv, dout, dmlp, small, maps = pl.pallas_call(
        lambda *refs: layer_kernel(n_batch, n_head, *refs),
        out_shape=(
            jax.ShapeDtypeStruct((rows, width), BF16),
            jax.ShapeDtypeStruct((rows, width), BF16),
            jax.ShapeDtypeStruct((3, gcols, width), BF16),
            jax.ShapeDtypeStruct((1, gcols, width), BF16),
            jax.ShapeDtypeStruct((2, width, width), BF16),
            jax.ShapeDtypeStruct((16, width), F32),
            jax.ShapeDtypeStruct((2, heads // n_head, basis), F32),
        ),
        in_specs=[smem, smem, (vec,) * 6, (vec,) * 3, (vec,) * 2] + [any_spec] * 6,
        out_specs=[any_spec] * 7,
        scratch_shapes=[
            vm(rows, width), vm(rows, width), vm(basis, width),
            vm(4, width, width), vm(n_head, 2, width, width),
            vm(n_head, 8, width, dtype=F32), vm(8, width, dtype=F32),
            vm(rows, width), vm(rows, width), vm(rows, width), vm(rows, width),
            vm(basis, width), vm(basis, width), vm(rows, width),
            vm(heads, rows // 2, rows // 2), vm(heads, rows // 2, rows),
            vm(rows, width, dtype=F32), vm(rows, width),
            vm(rows, width, dtype=F32), vm(rows, width, dtype=F32),
            vm(rows, width, dtype=F32), vm(rows, width, dtype=F32),
            vm(rows, width), vm(rows, width), vm(basis, rows),
            vm(32, basis, dtype=F32), vm(96, width),
            vm(16, rows, dtype=F32), vm(16, rows, dtype=F32), vm(16, rows, dtype=F32),
            vm(16, rows, dtype=F32), vm(16, rows, dtype=F32), vm(32, rows, dtype=F32),
            vm(16, width, dtype=F32),
            vm(2, heads // n_head, basis, dtype=F32),
            tuple(
                (vm(r, width, dtype=F32), vm(3 + extra, r, width, dtype=F32),
                 vm(n_head, r, width, dtype=F32)) for r in (8, 16, 8)
            ),
            recv, vm(1, 1, width, width // 2),
            tuple(vm(t, r, width) for t, r in halves),
            tuple(vm(extra, t, r // 4, width // 2) for t, r in halves) if extra else (),
            (dma((4, n_head, 4)), dma((4, n_head, 4)), dma((4, n_head)), dma, dma, dma((7, n_head, 4)), dma((7, n_head, 4)),
             dma((7, 3)), dma((7, 3)), dma((7, max(extra, 1))), dma((7, max(extra, 1))),
             dma((3, 3 + extra + n_head)),
             dma((3, 3 + extra + n_head)), dma((n_head,)), dma((n_head,))),
            dma((10,)),
        ],
        compiler_params=pltpu.CompilerParams(
            collective_id=0, has_side_effects=True, vmem_limit_bytes=67043328
        ),
    )(memory_flags, document_start,
      (first_gain, first_shift, out_bias, second_gain, second_shift, down_bias),
      (query_bias, value_offset_bias, up_bias), (centre_weight, width_weight),
      layer_input, grad_output, memory_coefficients, att, up_weight, down_weight)
    return (
        y, dx, small[0], small[1],
        dqkv[0].T.astype(F32), small[7, :gcols], dqkv[1].T.astype(F32), dqkv[2].T.astype(F32), small[8, :gcols],
        dout[0].astype(F32),
        small[2], small[3], small[4],
        dmlp[0].astype(F32), small[6], dmlp[1].astype(F32), small[5],
        maps[0], maps[1],
    )


def solution(mesh):
    n_batch, n_head = mesh.shape["batch"], mesh.shape["head"]
    tokens = P(("batch", "head"), None)
    cols, rows, split, whole = P(None, "head"), P("head", None), P("head"), P()
    placed = (
        tokens, P("batch"), P("batch"), P("batch", None, None), whole, whole, cols, split, cols,
        cols, split, rows, whole, whole, whole, cols, split, rows, whole, rows, rows, tokens,
    )
    outs = (
        tokens, tokens, whole, whole, cols, split, cols, cols, split, rows, whole, whole, whole,
        cols, split, rows, whole, rows, rows,
    )
    return jax.shard_map(
        lambda *args: per_device(n_batch, n_head, *args),
        mesh=mesh, in_specs=placed, out_specs=outs, check_vma=False,
    )
```

```python
import math

import jax
import jax.numpy as jnp
from jax import lax
from jax.experimental import pallas as pl
from jax.experimental.pallas import tpu as pltpu
from jax.sharding import PartitionSpec as P

F32 = jnp.float32
BF16 = jnp.bfloat16
EPS = 1e-05
ROOT = math.sqrt(2.0 / math.pi)
CUBE = 0.044715
ROW_TILE = 256


def mm(left, right):
    return lax.dot_general(left, right, (((1,), (0,)), ((), ())), preferred_element_type=F32)


def mm_nt(left, right):
    return lax.dot_general(left, right, (((1,), (1,)), ((), ())), preferred_element_type=F32)


def mm_tn(left, right):
    return lax.dot_general(left, right, (((0,), (0,)), ((), ())), preferred_element_type=F32)


def three_parts(value):
    high = value.astype(BF16)
    rest = value - high.astype(F32)
    middle = rest.astype(BF16)
    low = (rest - middle.astype(F32)).astype(BF16)
    return high, middle, low


def lane_mean(value):
    return jnp.mean(value, axis=-1, keepdims=True)


def norm_rows(value):
    center = value - lane_mean(value)
    factor = lax.rsqrt(lane_mean(center * center) + EPS)
    return center * factor, factor


def fold8(value):
    return jnp.sum(value.reshape(value.shape[0] // 8, 8, value.shape[1]), axis=0)


def row_sum(value):
    return jnp.sum(value, axis=0, keepdims=True)


ATT, OUT, UP, DOWN, QUERY, KEY, VALUE = range(7)
SUMMED = (OUT, UP, DOWN, QUERY, KEY, VALUE)
ALL_GROUPS = (OUT, QUERY, KEY, VALUE)
DIRECT = (ATT, OUT)
SPANS = {ATT: (0, 3), OUT: (3, 1), QUERY: (0, 1), KEY: (1, 1), VALUE: (2, 1)}
EARLY = (DOWN, 1)
MESH = pl.DeviceIdType.MESH
SUB = 8


def nearest_first(place, count):
    pair = place + 1 - 2 * (place % 2)
    return sorted(range(count), key=lambda other: (abs(other - place), other != pair))


def pick(index, values):
    chosen = values[0]
    for at, value in enumerate(values[1:], 1):
        chosen = jnp.where(index == at, value, chosen)
    return chosen


class Exchange:
    def __init__(self, n_batch, n_head, wa, wm, recv, early, fin, more, smalls, sems):
        self.n_head, self.smalls, self.early = n_head, smalls, early
        self.wa, self.wm = wa, wm
        self.recv, self.fin, self.more = recv, fin, more
        (self.ag_s, self.ag_r, self.ag_o, self.early_s, self.early_r, self.rs_s, self.rs_r, self.fin_s, self.fin_r, self.ex_s, self.ex_r,
         self.sm_s, self.sm_r, self.ax_s, self.ax_r) = sems
        b, h = lax.axis_index("batch"), lax.axis_index("head")
        self.b, self.h = b, h
        core, x, y = lax.rem(b, 2), lax.rem(lax.div(b, 2), 2), lax.rem(lax.div(b, 4), 2)
        self.core = core
        across_x, across_y = b + 2 - 4 * x, b + 4 - 8 * y
        self.mate = b + 1 - 2 * core
        self.near = across_x + core * (across_y - across_x)
        self.far = across_y + core * (across_x - across_y)
        self.high = y + core * (x - y)
        self.low = x + core * (y - x)
        self.quarter = 2 * self.high + self.low
        self.other_quarter = 2 * self.high + 1 - self.low
        self.extra = []
        step = SUB
        while step < n_batch:
            bit = lax.rem(lax.div(b, step), 2)
            self.extra.append(b + step - 2 * step * bit)
            step *= 2
        orders = [nearest_first(place, n_head) for place in range(n_head)]
        self.groups = [
            h if k == 0 else pick(h, [order[k] for order in orders]) for k in range(n_head)
        ]
        self.places = [
            pick(h, [orders[orders[place][k]].index(place) for place in range(n_head)])
            for k in range(n_head)
        ]
        self.half_width = wm.shape[-1] // 2
        self.rows = [wm.shape[2] if k in (UP, DOWN) else wa.shape[1] // n_head for k in range(7)]
        self.pending = []

    def barrier(self):
        signal = pltpu.get_barrier_semaphore()
        peers = [(p, self.h) for p in [self.mate, self.near, self.far] + self.extra]
        peers += [(self.b, self.turn(k)) for k in range(1, self.n_head)]
        for peer in peers:
            pl.semaphore_signal(signal, inc=1, device_id=peer, device_id_type=MESH)
        pl.semaphore_wait(signal, len(peers))

    def group(self, k):
        return self.groups[k]

    def turn(self, j):
        return lax.rem(self.h + j, self.n_head)

    def cols(self, which):
        return pl.ds(pl.multiple_of(which * self.half_width, 128), self.half_width)

    def view(self, kind, k, start, count, cols):
        g = self.group(k)
        if kind in (UP, DOWN):
            return self.wm.at[g, pl.ds(kind - UP, 1), pl.ds(pl.multiple_of(start, 16), count), cols]
        first, many = SPANS[kind]
        offset = pl.multiple_of(g * self.rows[kind] + start, 16)
        return self.wa.at[pl.ds(first, many), pl.ds(offset, count), cols]

    def part(self, kind, k, pieces, index, cols):
        count = self.rows[kind] // pieces
        return self.view(kind, k, index * count, count, cols)

    def copy(self, src, dst, send, recv, peer):
        return pltpu.make_async_remote_copy(
            src_ref=src, dst_ref=dst, send_sem=send, recv_sem=recv,
            device_id=peer, device_id_type=MESH,
        )

    def own_sends(self, kind):
        own = self.part(kind, 0, 4, self.quarter, self.cols(self.core))
        if kind in DIRECT:
            targets = [(self.group(k), None) for k in range(1, self.n_head)]
        else:
            targets = [(self.h + 1, self.h < self.n_head - 1), (self.h - 1, self.h > 0)]
        for at, (target, allowed) in enumerate(targets):
            copy = self.copy(
                own, own, self.ag_s.at[kind, at, 0], self.ag_r.at[kind, self.h, 0],
                (self.b, target),
            )
            yield copy, allowed

    def gather_start(self, kind):
        for copy, allowed in self.own_sends(kind):
            if allowed is None:
                copy.start()
            else:
                pl.when(allowed)(copy.start)

    def onward(self, kind, k):
        g = self.group(k)
        ref = self.part(kind, k, 4, self.quarter, self.cols(self.core))
        target = jnp.where(g < self.h, self.h + 1, self.h - 1)
        copy = self.copy(
            ref, ref, self.ag_o.at[kind, k], self.ag_r.at[kind, g, 0], (self.b, target)
        )
        return copy, (target >= 0) & (target < self.n_head)

    def pass_on(self, kind, k):
        copy, allowed = self.onward(kind, k)

        @pl.when(allowed)
        def _():
            self.gather_step(kind, k, 0, receive=True).wait_recv()
            copy.start()

    def gather_step(self, kind, k, stage, receive=False):
        mine = self.cols(self.core)
        if stage == 0:
            ref = self.part(kind, k, 4, self.quarter, mine)
            peer = (self.b, self.group(k))
        elif stage == 1:
            which = self.other_quarter if receive else self.quarter
            ref = self.part(kind, k, 4, which, mine)
            peer = (self.near, self.h)
        elif stage == 2:
            ref = self.part(kind, k, 2, 1 - self.high if receive else self.high, mine)
            peer = (self.far, self.h)
        else:
            ref = self.part(kind, k, 1, 0, self.cols(1 - self.core) if receive else mine)
            peer = (self.mate, self.h)
        at = self.group(k) if stage == 0 else k
        return self.copy(
            ref, ref, self.ag_s.at[kind, k, stage], self.ag_r.at[kind, at, stage], peer
        )

    def gather_pass(self, kind, k, stage):
        arrived = self.gather_step(kind, k, stage - 1, receive=True)
        if stage == 1 and kind not in DIRECT:
            for other in range(1, self.n_head):
                if max(other - 1, 1) == k:
                    self.pass_on(kind, other)
            pl.when(jnp.logical_not(self.onward(kind, k)[1]))(arrived.wait_recv)
        else:
            arrived.wait_recv()
        if stage < 4:
            self.gather_step(kind, k, stage).start()

    def gather_sent(self, kind, k):
        if k == 0:
            for copy, allowed in self.own_sends(kind):
                if allowed is None:
                    copy.wait_send()
                else:
                    pl.when(allowed)(copy.wait_send)
            return
        for stage in (1, 2, 3):
            self.gather_step(kind, k, stage).wait_send()
        if kind not in DIRECT:
            copy, allowed = self.onward(kind, k)
            pl.when(allowed)(copy.wait_send)

    def reduce_step(self, kind, k, stage, receive=False):
        mine = self.cols(self.core)
        if stage == 0:
            src, peer = self.part(kind, k, 1, 0, self.cols(1 - self.core)), (self.mate, self.h)
        elif stage == 1:
            src, peer = self.part(kind, k, 2, 1 - self.high, mine), (self.far, self.h)
        elif stage == 2:
            src, peer = self.part(kind, k, 4, self.other_quarter, mine), (self.near, self.h)
        else:
            src, peer = self.part(kind, k, 4, self.quarter, mine), (self.b, self.group(k))
        at = k
        if stage == 3 and not receive:
            at = self.places[k]
        return self.copy(
            src, self.recv[stage][kind - 1].at[at], self.rs_s.at[kind, k, stage],
            self.rs_r.at[kind, at, stage], peer,
        )

    def add_rows(self, kind, k, start, count, received, out=None):
        mine = self.cols(self.core)
        own = self.view(kind, k, start, count, mine)
        target = own if out is None else out
        sources = [buf.at[:, pl.ds(pl.multiple_of(start - base, 16), count), :] for buf, base in received]
        kinds = own.shape[0]
        tile = min(count, 192)

        for t in range(kinds):
            def step(i, state):
                span = pl.ds(pl.multiple_of(i * tile, 16), tile)
                if len(sources) == 1:
                    target[t, span, :] = own[t, span, :] + sources[0][t, span, :]
                    return state
                total = own[t, span, :].astype(F32)
                for source in sources:
                    total = total + source[t, span, :].astype(F32)
                target[t, span, :] = total.astype(BF16)
                return state

            lax.fori_loop(0, count // tile, step, 0)

    def early_copy(self):
        kind, k = EARLY
        src = self.part(kind, k, 1, 0, self.cols(self.core))
        return self.copy(
            src, self.early.at[0], self.early_s, self.early_r, (self.b, self.group(k))
        )

    def reduce_pass(self, kind, k, stage):
        rows = self.rows[kind]
        half, quarter = rows // 2, rows // 4
        first, second, third = (self.recv[s][kind - 1].at[k] for s in range(3))
        if stage > 0:
            self.reduce_step(kind, k, stage - 1).wait_recv()
        if (kind, k) == EARLY and stage == 1:
            self.add_rows(kind, k, 0, rows, [(first, 0)])
            self.early_copy().start()
            return
        kept = self.high * half
        parts = [(first, 0)]
        if kind == EARLY[0] and k == 0:
            parts.append((self.early.at[0], 0))
            if stage == 1:
                self.early_copy().wait_recv()
        if stage == 1:
            self.add_rows(kind, k, (1 - self.high) * half, half, parts)
        elif stage == 2:
            self.add_rows(
                kind, k, self.other_quarter * quarter, quarter, parts + [(second, kept)]
            )
        elif stage == 3:
            own = self.quarter * quarter
            self.add_rows(kind, k, own, quarter, parts + [(second, kept), (third, own)])
        if stage < 3 or k > 0:
            self.reduce_step(kind, k, stage).start()

    def late(self, kind):
        return [k for k in range(1, self.n_head) if (kind, k) != EARLY]

    def fin_part(self, kind, pieces, index, cols):
        count = self.rows[kind] // pieces
        return self.fin[kind - 1].at[:, pl.ds(pl.multiple_of(index * count, 16), count), cols]

    def final_step(self, kind, stage, receive=False):
        mine = self.cols(self.core)
        if stage == 0:
            which = self.other_quarter if receive else self.quarter
            ref, peer = self.fin_part(kind, 4, which, mine), (self.near, self.h)
        elif stage == 1:
            which = 1 - self.high if receive else self.high
            ref, peer = self.fin_part(kind, 2, which, mine), (self.far, self.h)
        else:
            ref = self.fin_part(kind, 1, 0, self.cols(1 - self.core) if receive else mine)
            peer = (self.mate, self.h)
        return self.copy(ref, ref, self.fin_s.at[kind, stage], self.fin_r.at[kind, stage], peer)

    def final_pass(self, kind, stage):
        if stage == 0:
            for k in self.late(kind):
                self.reduce_step(kind, k, 3, receive=True).wait_recv()
            quarter = self.rows[kind] // 4
            last = self.recv[3][kind - 1]
            mine = self.cols(self.core)
            own = self.view(kind, 0, self.quarter * quarter, quarter, mine)
            target = self.fin_part(kind, 4, self.quarter, mine)
            tile = min(quarter, 192)
            for t in range(own.shape[0]):
                def step(i, state):
                    span = pl.ds(pl.multiple_of(i * tile, 16), tile)
                    total = own[t, span, :].astype(F32)
                    for k in self.late(kind):
                        total = total + last[k, t, span, :].astype(F32)
                    target[t, span, :] = total.astype(BF16)
                    return state

                lax.fori_loop(0, quarter // tile, step, 0)
            for e, peer in enumerate(self.extra):
                copy = self.copy(
                    target, self.more[kind - 1].at[e], self.ex_s.at[kind, e], self.ex_r.at[kind, e],
                    (peer, self.h),
                )
                copy.start()
                copy.wait()
                for t in range(own.shape[0]):
                    total = target[t].astype(F32) + self.more[kind - 1][e, t].astype(F32)
                    target[t] = total.astype(BF16)
        else:
            self.final_step(kind, stage - 1, receive=True).wait_recv()
        if stage < 3:
            self.final_step(kind, stage).start()

    def all_sent(self):
        self.early_copy().wait_send()
        for kind in SUMMED:
            for k in range(self.n_head):
                stages = range(1) if (kind, k) == EARLY else range(4 if k > 0 else 3)
                for stage in stages:
                    self.reduce_step(kind, k, stage).wait_send()
            for stage in range(3):
                self.final_step(kind, stage).wait_send()

    def aux_copy(self, aux, j):
        own = aux.at[self.h]
        return self.copy(
            own, own, self.ax_s.at[j], self.ax_r.at[self.n_head - j], (self.b, self.turn(j))
        )

    def aux_wait(self, aux, k):
        own = aux.at[self.turn(k)]
        self.copy(own, own, self.ax_s.at[k], self.ax_r.at[k], (self.b, self.turn(k))).wait_recv()

    def small_step(self, which, stage, j=0):
        value, got, all_heads = self.smalls[which]
        peers = [self.mate, self.near, self.far]
        if stage < 3:
            src, dst, peer, at = value, got.at[stage], (peers[stage], self.h), stage
        else:
            src, dst, peer, at = value, all_heads.at[self.h], (self.b, self.turn(j)), 2 + j
        return self.copy(src, dst, self.sm_s.at[which, at], self.sm_r.at[which, at], peer)

    def small_pass(self, which, stage):
        value, got, all_heads = self.smalls[which]
        if stage == 0:
            self.small_step(which, 0).start()
        elif stage <= 3:
            self.small_step(which, stage - 1).wait()
            value[...] = value[...] + got[stage - 1]
            if stage < 3:
                self.small_step(which, stage).start()
                return
            first = 2 + self.n_head
            for e, peer in enumerate(self.extra):
                copy = self.copy(
                    value, got.at[3 + e], self.sm_s.at[which, first + e],
                    self.sm_r.at[which, first + e], (peer, self.h),
                )
                copy.start()
                copy.wait()
                value[...] = value[...] + got[3 + e]
            for j in range(1, self.n_head):
                self.small_step(which, 3, j).start()
            all_heads[self.h] = value[...]
        else:
            for j in range(1, self.n_head):
                self.small_step(which, 3, j).wait()
            total = all_heads[0]
            for g in range(1, self.n_head):
                total = total + all_heads[g]
            value[...] = total


SCHEDULE = {
    "needA": (("g", 0, 1, 1), ("g", 0, 1, 2), ("g", 0, 2, 1), ("g", 1, 2, 1), ("g", 0, 3, 1), ("g", 1, 1, 1), ("g", 0, 1, 3), ("g", 0, 2, 2), ("g", 1, 2, 2), ("g", 0, 1, 4), ("g", 0, 3, 2), ("g", 1, 3, 1), ("g", 1, 1, 2), ("g", 2, 1, 1), ("g", 0, 2, 3), ("g", 1, 3, 2), ("g", 1, 2, 3), ("g", 0, 2, 4), ("g", 3, 1, 1), ("g", 2, 2, 1), ("g", 0, 3, 3), ("g", 2, 1, 2), ("g", 1, 1, 3), ("g", 0, 3, 4),),
    ("proj", 0): (("g", 3, 2, 1),),
    ("proj", 1): (("g", 1, 3, 3), ("g", 3, 1, 2),),
    ("fwd", 0): (("g", 2, 3, 1),),
    ("fwd", 1): (("g", 2, 2, 2),),
    ("fwd", 2): (("g", 2, 1, 3),),
    ("fwd", 3): (("g", 3, 2, 2), ("g", 3, 3, 1),),
    ("fwd", 5): (("g", 2, 3, 2),),
    "needO": (("g", 1, 2, 4), ("g", 1, 1, 4), ("g", 1, 3, 4),),
    ("mlp0", 0): (("g", 3, 1, 3), ("g", 3, 3, 2),),
    ("mlp2", 0): (("g", 2, 2, 3),),
    ("needU", 1): (("g", 2, 1, 4),),
    ("mlp0", 1): (("g", 3, 2, 3),),
    ("needD", 1): (("g", 3, 1, 4),),
    ("mlp1", 1): (("r", 2, 0, 1), ("g", 2, 3, 3),),
    ("mlpU", 1): (("g", 3, 3, 3),),
    ("needU", 2): (("g", 2, 2, 4),),
    ("mlp0", 2): (("r", 3, 1, 1), ("r", 2, 1, 1),),
    ("needD", 2): (("g", 3, 2, 4),),
    ("mlp1", 2): (("r", 2, 0, 2),),
    ("needU", 3): (("g", 2, 3, 4),),
    ("mlp0", 3): (("r", 2, 1, 2), ("r", 2, 0, 3), ("r", 2, 2, 1), ("r", 3, 2, 1),),
    ("needD", 3): (("g", 3, 3, 4),),
    ("mlpD", 3): (("r", 2, 1, 3),),
    "sb": (("r", 2, 2, 2), ("r", 2, 3, 1), ("r", 3, 0, 1), ("r", 3, 3, 1),),
    "gctx": (("r", 3, 2, 2),),
    "dwo": (("s", 0, 1),),
    ("bwd1", 0): (("r", 2, 2, 3), ("r", 1, 0, 1),),
    ("bwd0", 2): (("r", 2, 3, 2), ("s", 0, 2), ("r", 3, 2, 3),),
    ("bwd1", 3): (("r", 3, 0, 2),),
    ("bwd1", 4): (("r", 2, 3, 3),),
    "dwv": (("r", 3, 3, 2), ("r", 3, 0, 3), ("r", 6, 0, 1),),
    "mem": (("s", 0, 3), ("r", 1, 0, 2),),
    "dwk": (("s", 1, 1), ("r", 3, 3, 3), ("r", 5, 0, 1),),
    "dwq": (("r", 1, 0, 3), ("f", 2, 0), ("r", 4, 0, 1), ("r", 6, 0, 2),),
    "fb": (("s", 1, 2), ("s", 2, 1),),
    "tail": (("s", 0, 4), ("r", 5, 0, 2), ("f", 2, 1), ("r", 6, 0, 3), ("s", 2, 2), ("f", 3, 0), ("r", 4, 0, 2), ("r", 5, 0, 3), ("s", 1, 3), ("f", 1, 0), ("f", 3, 1), ("f", 6, 0), ("r", 4, 0, 3), ("f", 2, 2), ("f", 1, 1), ("s", 2, 3), ("f", 5, 0), ("f", 6, 1), ("f", 2, 3), ("f", 5, 1), ("f", 3, 2), ("f", 1, 2), ("s", 1, 4), ("f", 6, 2), ("f", 3, 3), ("f", 5, 2), ("f", 1, 3), ("f", 6, 3), ("f", 4, 0), ("f", 5, 3), ("s", 2, 4), ("f", 4, 1), ("f", 4, 2), ("f", 4, 3),),
}

def layer_kernel(
    n_batch, n_head,
    flags, bounds, norm_in, bias_in, map_in, x_in, go_in, mc_in, att_in, up_in, down_in,
    y_out, dx_out, dqkv_out, dout_out, dmlp_out, small_out, maps_out,
    xs, gos, mcs, wa, wm, aux, nrm,
    xl, qs, ks, vs, mks, mvs, ctx, prob_top, prob_low, hid, x2, acc, dx2,
    u_s, g_s, act_s, du_s, rt_s,
    cwm, um, cen, spr, wsg, isp, nrs, pg, small,
    maps_s, smalls, recv, ahead, fin, more, links, sems,
):
    gcs, dqs, dks, dvs, gmk, gmv = x2, acc, ks, vs, mks, mvs
    me = lax.axis_index("head")
    rows, width = xs.shape
    heads = prob_low.shape[0]
    blocks = 2
    blk = rows // blocks
    probs = (prob_top, prob_low)
    mask = dx2.at[:, 0:rows]
    s_s = g_s.at[blk:rows, 0:rows]
    ds_s = act_s.at[:, 0:rows]
    pairs = heads // 2
    basis = mcs.shape[0]
    gcols = width // n_head
    tiles = rows // ROW_TILE

    def load(src, dst, index):
        copy = pltpu.make_async_copy(src, dst, sems.at[index])
        copy.start()
        return copy

    others = range(1, n_head)
    net = Exchange(n_batch, n_head, wa, wm, recv, ahead, fin, more, smalls, links)
    att_copies = [load(att_in, wa.at[:, pl.ds(pl.multiple_of(me * gcols, 16), gcols), :], 5)]
    copies = [
        load(x_in, xs, 0),
        load(mc_in.at[me], mcs, 2),
        load(go_in, gos, 4),
    ]
    mlp_copies = [load(up_in, wm.at[me, 0], 6), load(down_in, wm.at[me, 1], 7)]
    for row, ref in enumerate(norm_in):
        nrm[row : row + 1, :] = ref[...].astype(F32).reshape(1, width)
    aux[me] = jnp.zeros((8, width), F32)
    for row, ref in enumerate(bias_in[:2]):
        aux[me, row : row + 1, 0:gcols] = ref[...].astype(F32).reshape(1, gcols)
    aux[me, 2:3, :] = bias_in[2][...].astype(F32).reshape(1, width)
    for row, ref in enumerate(map_in):
        for k in range(ref.shape[0]):
            aux[me, 3 + row : 4 + row, k * basis : (k + 1) * basis] = ref[k : k + 1, :]
    net.barrier()
    for copy in att_copies:
        copy.wait()
    net.gather_start(ATT)
    for j in range(1, n_head):
        net.aux_copy(aux, j).start()
    net.gather_start(OUT)
    for copy in mlp_copies:
        copy.wait()
    net.gather_start(UP)
    net.gather_start(DOWN)

    def event(op, first, *rest):
        if op == "g":
            net.gather_pass(first, *rest)
        elif op == "r":
            group, stage = rest
            for k in range(n_head) if first in ALL_GROUPS else (group,):
                net.reduce_pass(first, k, stage)
        elif op == "f":
            net.final_pass(first, *rest)
        else:
            net.small_pass(first, *rest)

    def take(slot):
        for item in SCHEDULE.get(slot, ()):
            event(*item)

    def take_at(index, count, slot):
        for value in range(count):
            if (slot, value) in SCHEDULE:
                @pl.when(index == value)
                def _():
                    take((slot, value))


    flag = flags[me].astype(F32)
    bound = bounds[me]

    def each_tile(body, carry=0):
        def step(i, state):
            return body(pl.ds(pl.multiple_of(i * ROW_TILE, ROW_TILE), ROW_TILE), state)

        return lax.fori_loop(0, tiles, step, carry)

    early, middle, late = (group[0] for group in smalls)
    for ref in (middle, late):
        ref[...] = jnp.zeros_like(ref)
    zero_sum = jnp.zeros((8, width), F32)

    def mask_rows(span, state):
        row_ids = lax.broadcasted_iota(jnp.int32, (ROW_TILE, rows), 0) + span.start
        col_ids = lax.broadcasted_iota(jnp.int32, (ROW_TILE, rows), 1)
        least = jnp.where(row_ids < bound, 0, bound)
        allowed = (col_ids <= row_ids) & (col_ids >= least)
        mask[span, :] = jnp.where(allowed, 0.0, -jnp.inf).astype(F32)
        return state

    each_tile(mask_rows)
    for copy in copies:
        copy.wait()

    def first_norm(span, state):
        normed, _ = norm_rows(xs[span, :].astype(F32))
        xl[span, :] = (normed * nrm[0:1, :] + nrm[1:2, :]).astype(BF16)
        return state

    each_tile(first_norm)
    take("ln1")
    take("needA")
    for k in others:
        net.aux_wait(aux, k)

    column = lax.broadcasted_iota(jnp.int32, (1, width), 1)
    biases = []
    for row in range(2):
        bias = jnp.zeros((1, width), F32)
        for g in range(n_head):
            moved = aux[g, row : row + 1, :]
            shift = g * gcols
            if shift:
                moved = pltpu.roll(moved, shift, 1)
            bias = bias + jnp.where(column // gcols == g, moved, 0.0)
        biases.append(bias)

    tile_n = 256
    for kind, out, mem_out, bias_row in ((0, qs, None, 0), (1, ks, mks, None), (2, vs, mvs, 1)):
        for n in range(0, width, tile_n):
            cols = slice(n, n + tile_n)
            weight = wa[kind, cols, :]
            value = mm_nt(xl[...], weight)
            if bias_row is not None:
                value = value + biases[bias_row][:, cols]
            out[:, cols] = value.astype(BF16)
            if mem_out is not None:
                value = mm_nt(mcs[...], weight)
                if bias_row is not None:
                    value = value + biases[bias_row][:, cols]
                mem_out[:, cols] = value.astype(BF16)
        take(("proj", kind))

    cwm[...] = jnp.zeros_like(cwm)
    per_group = heads // n_head
    for h in range(heads):
        g, k = divmod(h, per_group)
        cwm[h : h + 1, :] = aux[g, 3:4, k * basis : (k + 1) * basis]
        cwm[16 + h : 17 + h, :] = aux[g, 4:5, k * basis : (k + 1) * basis]
    head_width = width // heads
    own_lanes = (
        lax.broadcasted_iota(jnp.int32, (32, width), 0) % 16
        == lax.broadcasted_iota(jnp.int32, (32, width), 1) // head_width
    )
    scale = head_width ** (-0.5)
    parts = three_parts(cwm[...])
    maps = sum(mm(part, mks[...]) for part in reversed(parts))
    maps = jnp.where(own_lanes, maps * scale, 0.0)
    for index, part in enumerate(three_parts(maps)):
        um[32 * index : 32 * index + 32, :] = part
    pre = mm_nt(um[...], qs[...])
    pre = (pre[64:96] + pre[32:64]) + pre[0:32]
    centre = jax.nn.sigmoid(pre[0:16])
    width_pre = pre[16:32]
    spread = 0.02 * (jnp.maximum(width_pre, 0.0) + jnp.log1p(jnp.exp(-jnp.abs(width_pre)))) + 0.01
    cen[...] = centre
    spr[...] = spread
    wsg[...] = jax.nn.sigmoid(width_pre)
    isp[...] = -0.5 / spread
    nrs[...] = lax.rsqrt((2.0 * math.pi) * spread) / basis
    pg[...] = jnp.zeros_like(pg)

    lane = lax.broadcasted_iota(jnp.int32, (1, 2 * head_width), 1)
    half = [
        jnp.where((lane >= head_width) == bool(e), 1.0, 0.0).astype(BF16) for e in range(2)
    ]
    n_tile = 64
    sub = 64

    def recall_tile(head, start):
        ids = lax.broadcasted_iota(jnp.int32, (n_tile, rows), 0).astype(F32)
        offset = cen[pl.ds(head, 1), :] - (ids + (start + 0.5)) / basis
        value = jnp.exp(offset * offset * isp[pl.ds(head, 1), :]) * nrs[pl.ds(head, 1), :]
        return offset, value

    take("maps")

    def forward_pair(p, state):
        lanes = pl.ds(pl.multiple_of(p * 2 * head_width, 2 * head_width), 2 * head_width)
        keys = ks[:, lanes]
        vals = vs[:, lanes]
        queries = qs[:, lanes] * jnp.asarray(scale, BF16)
        mem_vals = mvs[:, lanes] * flag.astype(BF16)
        for e in range(2):
            head = 2 * p + e
            masked_q = queries * half[e]
            masked_v = vals * half[e]
            for r in range(blocks):
                cols = (r + 1) * blk
                s_s[:, :cols] = mm_nt(masked_q[r * blk : (r + 1) * blk], keys[:cols])
                for t in range(0, blk, sub):
                    scores = s_s[t : t + sub, :cols] + mask[r * blk + t : r * blk + t + sub, :cols]
                    shifted = jnp.exp(scores - jnp.max(scores, axis=-1, keepdims=True))
                    inverse = 1.0 / jnp.sum(shifted, axis=-1, keepdims=True)
                    probs[r][head, t : t + sub, :] = (shifted * inverse).astype(BF16)
            for t in range(0, basis, n_tile):
                _, value = recall_tile(head, t)
                rt_s[t : t + n_tile, :] = value.astype(BF16)
            part = mm_tn(rt_s[...], mem_vals * half[e])
            for r in range(blocks):
                cols = (r + 1) * blk
                span = slice(r * blk, (r + 1) * blk)
                value = mm(probs[r][head], masked_v[:cols]) + part[span]
                if e == 0:
                    u_s[span, 0 : 2 * head_width] = value
                else:
                    ctx[span, lanes] = (value + u_s[span, 0 : 2 * head_width]).astype(BF16)
        take_at(p, pairs, "fwd")
        return state

    lax.fori_loop(0, pairs, forward_pair, 0)

    take("needO")

    for n in range(0, width, tile_n):
        hid[:, n : n + tile_n] = mm(ctx[...], wa[3, :, n : n + tile_n])

    take("out")

    def second_norm(span, state):
        hidden = xs[span, :].astype(F32) + (hid[span, :] + nrm[2:3, :])
        hid[span, :] = hidden
        normed, _ = norm_rows(hidden)
        x2[span, :] = (normed * nrm[3:4, :] + nrm[4:5, :]).astype(BF16)
        acc[span, :] = jnp.zeros((ROW_TILE, width), F32)
        dx2[span, :] = jnp.zeros((ROW_TILE, width), F32)
        return state

    each_tile(second_norm)
    take("ln2")

    def units(k, state):
        g = pick(k, net.groups)
        take_at(k, n_head, "needU")
        for n in range(0, width, tile_n):
            cols = slice(n, n + tile_n)
            u_s[:, cols] = mm(x2[...], wm[g, 0, :, cols])
        take_at(k, n_head, "mlp0")
        take_at(k, n_head, "needD")
        for n in range(0, width, tile_n):
            cols = slice(n, n + tile_n)
            g_s[:, cols] = mm_nt(gos[...], wm[g, 1, cols, :])
        bias = aux[g, 2:3, :]

        def activate(span, total):
            pre = u_s[span, :] + bias
            square = pre * pre
            tanh = jnp.tanh(ROOT * pre * (1.0 + CUBE * square))
            outer = 0.5 + 0.5 * tanh
            act_s[span, :] = (pre * outer).astype(BF16)
            slope = outer + (0.5 * ROOT) * pre * (1.0 - tanh * tanh) * (1.0 + (3 * CUBE) * square)
            low = (g_s[span, :] * slope).astype(BF16)
            du_s[span, :] = low
            return total + fold8(low.astype(F32))

        total = each_tile(activate, zero_sum)
        take_at(k, n_head, "mlp1")
        early[pl.ds(4 + g, 1), :] = row_sum(total)
        for n in range(0, width, tile_n):
            cols = slice(n, n + tile_n)
            acc[:, cols] += mm(act_s[...], wm[g, 1, :, cols])
            dx2[:, cols] += mm_nt(du_s[...], wm[g, 0, cols, :])
        take_at(k, n_head, "mlp2")

        def each_group(*calls):
            for value in range(n_head):
                @pl.when(k == value)
                def _():
                    for call, kind, *rest in calls:
                        call(kind, value, *rest)

        each_group((net.gather_sent, UP), (net.gather_sent, DOWN))
        for n in range(0, width, tile_n):
            cols = slice(n, n + tile_n)
            wm[g, 1, :, cols] = mm_tn(act_s[...], gos[:, cols]).astype(BF16)
        each_group((net.reduce_pass, DOWN, 0))
        take_at(k, n_head, "mlpD")
        for n in range(0, width, tile_n):
            cols = slice(n, n + tile_n)
            wm[g, 0, :, cols] = mm_tn(x2[...], du_s[:, cols]).astype(BF16)
        each_group((net.reduce_pass, UP, 0))
        take_at(k, n_head, "mlpU")
        return state

    lax.fori_loop(0, n_head, units, 0)

    def second_back(span, sums):
        hidden = hid[span, :]
        normed, factor = norm_rows(hidden)
        grad = dx2[span, :]
        grad_out = gos[span, :].astype(F32)
        xl2 = hidden + (acc[span, :] + nrm[5:6, :])
        du_s[span, :] = xl2.astype(BF16)
        scaled = grad * nrm[3:4, :]
        total = grad_out + factor * (
            scaled - lane_mean(scaled) - normed * lane_mean(scaled * normed)
        )
        hid[span, :] = total
        low = total.astype(BF16)
        act_s[span, :] = low
        return (
            sums[0] + fold8(grad * normed),
            sums[1] + fold8(grad),
            sums[2] + fold8(low.astype(F32)),
            sums[3] + fold8(grad_out),
        )

    sums = each_tile(second_back, (zero_sum,) * 4)
    y_copy = load(du_s, y_out, 0)
    early[1:2, :] = row_sum(sums[0])
    early[2:3, :] = row_sum(sums[1])
    early[0:1, :] = row_sum(sums[2])
    early[3:4, :] = row_sum(sums[3])
    event("s", 0, 0)
    take("sb")
    for n in range(0, width, tile_n):
        cols = slice(n, n + tile_n)
        gcs[:, cols] = mm_nt(act_s[...], wa[3, cols, :]).astype(BF16)
    take("gctx")
    for k in range(n_head):
        net.gather_sent(OUT, k)
    for n in range(0, width, tile_n):
        cols = slice(n, n + tile_n)
        wa[3, :, cols] = mm_tn(ctx[...], act_s[:, cols]).astype(BF16)
    event("r", OUT, 0, 0)
    take("dwo")

    def backward_pair(p, state):
        lanes = pl.ds(pl.multiple_of(p * 2 * head_width, 2 * head_width), 2 * head_width)
        keys = ks[:, lanes]
        vals = vs[:, lanes]
        queries = qs[:, lanes] * jnp.asarray(scale, BF16)
        grads = gcs[:, lanes]
        mem_vals = mvs[:, lanes] * flag.astype(BF16)
        for e in range(2):
            head = 2 * p + e
            masked_g = grads * half[e]
            masked_q = queries * half[e]
            masked_k = keys * half[e]
            for r in range(blocks):
                cols = (r + 1) * blk
                span = slice(r * blk, (r + 1) * blk)
                s_s[:, :cols] = mm_nt(masked_g[span], vals[:cols])
                for t in range(0, blk, sub):
                    inner = slice(r * blk + t, r * blk + t + sub)
                    grad = s_s[t : t + sub, :cols]
                    prob = probs[r][head, t : t + sub, :].astype(F32)
                    total = jnp.sum(prob * grad, axis=-1, keepdims=True)
                    ds_s[inner, :cols] = (prob * (grad - total)).astype(BF16)
                value = mm(ds_s[span, :cols], masked_k[:cols])
                if e == 0:
                    dqs[span, lanes] = value
                else:
                    dqs[span, lanes] += value
            for c in range(blocks):
                span = slice(c * blk, (c + 1) * blk)
                key_part = mm_tn(ds_s[c * blk :, span], masked_q[c * blk :])
                val_part = mm_tn(prob_low[head, :, span], masked_g[blk:])
                if c == 0:
                    val_part = val_part + mm_tn(prob_top[head], masked_g[:blk])
                if e == 0:
                    u_s[span, 0:128] = key_part
                    u_s[span, 128:256] = val_part
                else:
                    dks[span, lanes] = (key_part + u_s[span, 0:128]).astype(BF16)
                    dvs[span, lanes] = (val_part + u_s[span, 128:256]).astype(BF16)
            g_s[0:basis, 0:rows] = mm_nt(mem_vals * half[e], grads)
            sum0 = jnp.zeros((8, rows), F32)
            sum1 = sum0
            sum2 = sum0
            for t in range(0, basis, n_tile):
                offset, value = recall_tile(head, t)
                rt_s[t : t + n_tile, :] = value.astype(BF16)
                weighted = g_s[t : t + n_tile, 0:rows] * value
                moment = weighted * offset
                sum0 = sum0 + fold8(weighted)
                sum1 = sum1 + fold8(moment)
                sum2 = sum2 + fold8(moment * offset)
            part = mm(rt_s[...], masked_g * flag.astype(BF16))
            if e == 0:
                u_s[0:basis, 256:384] = part
            else:
                gmv[:, lanes] = (part + u_s[0:basis, 256:384]).astype(BF16)
            one = pl.ds(head, 1)
            centre = cen[one, :]
            inverse = 1.0 / spr[one, :]
            grad_centre = -row_sum(sum1) * inverse
            grad_spread = (row_sum(sum2) * inverse - row_sum(sum0)) * (0.5 * inverse)
            pg[one, :] = grad_centre * centre * (1.0 - centre)
            pg[pl.ds(16 + head, 1), :] = 0.02 * grad_spread * wsg[one, :]
            take_at(p, pairs, ("bwd0", "bwd1")[e])
        return state

    lax.fori_loop(0, pairs, backward_pair, 0)
    y_copy.wait()

    def input_share(kind, grads, first):
        for n in range(0, width, tile_n):
            cols = slice(n, n + tile_n)
            value = mm(grads[...], wa[kind, :, cols])
            dx2[:, cols] = value if first else dx2[:, cols] + value

    def weight_share(kind, grads, memory):
        for n in range(0, width, tile_n):
            cols = slice(n, n + tile_n)
            value = mm_tn(grads[...], xl[:, cols])
            if memory is not None:
                value = value + mm_tn(memory[...], mcs[:, cols])
            wa[kind, :, cols] = value.astype(BF16)

    for k in range(n_head):
        net.gather_sent(ATT, k)
    input_share(2, dvs, True)
    weight_share(2, dvs, gmv)
    event("r", VALUE, 0, 0)
    take("dwv")

    slopes = three_parts(pg[...])
    moments = sum(mm(part, qs[...]) for part in reversed(slopes))
    moments = jnp.where(own_lanes, moments * scale, 0.0)
    pieces = three_parts(moments)
    weight_grads = sum(mm_nt(piece, mks[...]) for piece in reversed(pieces))
    for h in range(heads):
        g, k = divmod(h, per_group)
        middle[2 + g : 3 + g, k * basis : (k + 1) * basis] = weight_grads[h : h + 1, :]
        middle[6 + g : 7 + g, k * basis : (k + 1) * basis] = weight_grads[16 + h : 17 + h, :]
    gmk[...] = (
        (mm_tn(parts[1], pieces[0]) + mm_tn(parts[0], pieces[1])) + mm_tn(parts[0], pieces[0])
    ).astype(BF16)
    for n in range(0, width, tile_n):
        cols = slice(n, n + tile_n)
        high = um[0:32, cols]
        value = (mm_tn(slopes[1], high) + mm_tn(slopes[0], um[32:64, cols])) + mm_tn(
            slopes[0], high
        )
        act_s[:, cols] = (dqs[:, cols] * scale + value).astype(BF16)
    take("mem")

    def bias_sums(span, sums):
        return (
            sums[0] + fold8(act_s[span, :].astype(F32)),
            sums[1] + fold8(dvs[span, :].astype(F32)),
        )

    sums = each_tile(bias_sums, (zero_sum,) * 2)
    middle[0:1, :] = row_sum(sums[0])
    middle[1:2, :] = row_sum(sums[1]) + row_sum(gmv[...].astype(F32))
    event("s", 1, 0)
    take("bias")

    input_share(1, dks, False)
    weight_share(1, dks, gmk)
    event("r", KEY, 0, 0)
    take("dwk")
    input_share(0, act_s, False)
    weight_share(0, act_s, None)
    event("r", QUERY, 0, 0)
    take("dwq")

    def first_back(span, sums):
        normed, factor = norm_rows(xs[span, :].astype(F32))
        grad = dx2[span, :]
        scaled = grad * nrm[0:1, :]
        total = hid[span, :] + factor * (
            scaled - lane_mean(scaled) - normed * lane_mean(scaled * normed)
        )
        du_s[span, :] = total.astype(BF16)
        return (sums[0] + fold8(grad * normed), sums[1] + fold8(grad))

    sums = each_tile(first_back, (zero_sum,) * 2)
    late[0:1, :] = row_sum(sums[0])
    late[1:2, :] = row_sum(sums[1])
    event("s", 2, 0)
    outs = [load(du_s, dx_out, 0)]
    take("fb")
    finished = {
        ("f", QUERY, 3): (QUERY, dqkv_out.at[pl.ds(0, 1)], 1),
        ("f", KEY, 3): (KEY, dqkv_out.at[pl.ds(1, 1)], 2),
        ("f", VALUE, 3): (VALUE, dqkv_out.at[pl.ds(2, 1)], 3),
        ("f", OUT, 3): (OUT, dout_out, 4),
        ("f", UP, 3): (UP, dmlp_out.at[pl.ds(0, 1)], 7),
        ("f", DOWN, 3): (DOWN, dmlp_out.at[pl.ds(1, 1)], 8),
    }
    for item in SCHEDULE["tail"]:
        event(*item)
        if item in finished:
            kind, target, at = finished[item]
            outs.append(load(fin[kind - 1], target, at))
    small[0:2, :] = late[0:2, :]
    small[2:6, :] = early[0:4, :]
    small[6:7, :] = early[pl.ds(4 + me, 1), :]
    for row in range(2):
        own = middle[row : row + 1, :]
        for g in range(1, n_head):
            own = jnp.where(me == g, pltpu.roll(middle[row : row + 1, :], width - g * gcols, 1), own)
        small[7 + row : 8 + row, :] = own
    for row in range(2):
        own = middle[pl.ds(2 + 4 * row + me, 1), :]
        for k in range(per_group):
            maps_s[row, k : k + 1, :] = own[:, k * basis : (k + 1) * basis]
    outs.append(load(maps_s, maps_out, 6))
    outs.append(load(small, small_out, 5))
    net.all_sent()
    for j in range(1, n_head):
        net.aux_copy(aux, j).wait_send()
    for copy in outs:
        copy.wait()


def per_device(
    n_batch, n_head,
    layer_input, memory_flags, document_start, memory_coefficients,
    first_gain, first_shift, query_weight, query_bias, key_matrix, value_matrix,
    value_offset_bias, out_weight, out_bias, second_gain, second_shift,
    up_weight, up_bias, down_weight, down_bias, centre_weight, width_weight, grad_output,
):
    rows, width = layer_input.shape
    basis = memory_coefficients.shape[1]
    gcols = query_weight.shape[1]
    heads = centre_weight.shape[0] * n_head
    att = jnp.stack([query_weight.T, key_matrix.T, value_matrix.T, out_weight])

    extra = 0
    while SUB << extra < n_batch:
        extra += 1

    def vm(*shape, dtype=BF16):
        return pltpu.VMEM(shape, dtype)

    any_spec = pl.BlockSpec(memory_space=pl.ANY)
    smem = pl.BlockSpec(memory_space=pltpu.SMEM)
    vec = pl.BlockSpec(memory_space=pltpu.VMEM)
    dma = pltpu.SemaphoreType.DMA
    halves = ((1, gcols), (1, width), (1, width)) + ((1, gcols),) * 3
    recv = tuple(
        tuple(vm(n_head, t, r // pieces, width // 2) for t, r in halves) for pieces in (1, 2, 4, 4)
    )
    y, dx, dqkv, dout, dmlp, small, maps = pl.pallas_call(
        lambda *refs: layer_kernel(n_batch, n_head, *refs),
        out_shape=(
            jax.ShapeDtypeStruct((rows, width), BF16),
            jax.ShapeDtypeStruct((rows, width), BF16),
            jax.ShapeDtypeStruct((3, gcols, width), BF16),
            jax.ShapeDtypeStruct((1, gcols, width), BF16),
            jax.ShapeDtypeStruct((2, width, width), BF16),
            jax.ShapeDtypeStruct((16, width), F32),
            jax.ShapeDtypeStruct((2, heads // n_head, basis), F32),
        ),
        in_specs=[smem, smem, (vec,) * 6, (vec,) * 3, (vec,) * 2] + [any_spec] * 6,
        out_specs=[any_spec] * 7,
        scratch_shapes=[
            vm(rows, width), vm(rows, width), vm(basis, width),
            vm(4, width, width), vm(n_head, 2, width, width),
            vm(n_head, 8, width, dtype=F32), vm(8, width, dtype=F32),
            vm(rows, width), vm(rows, width), vm(rows, width), vm(rows, width),
            vm(basis, width), vm(basis, width), vm(rows, width),
            vm(heads, rows // 2, rows // 2), vm(heads, rows // 2, rows),
            vm(rows, width, dtype=F32), vm(rows, width),
            vm(rows, width, dtype=F32), vm(rows, width, dtype=F32),
            vm(rows, width, dtype=F32), vm(rows, width, dtype=F32),
            vm(rows, width), vm(rows, width), vm(basis, rows),
            vm(32, basis, dtype=F32), vm(96, width),
            vm(16, rows, dtype=F32), vm(16, rows, dtype=F32), vm(16, rows, dtype=F32),
            vm(16, rows, dtype=F32), vm(16, rows, dtype=F32), vm(32, rows, dtype=F32),
            vm(16, width, dtype=F32),
            vm(2, heads // n_head, basis, dtype=F32),
            tuple(
                (vm(r, width, dtype=F32), vm(3 + extra, r, width, dtype=F32),
                 vm(n_head, r, width, dtype=F32)) for r in (8, 16, 8)
            ),
            recv, vm(1, 1, width, width // 2),
            tuple(vm(t, r, width) for t, r in halves),
            tuple(vm(extra, t, r // 4, width // 2) for t, r in halves) if extra else (),
            (dma((4, n_head, 4)), dma((4, n_head, 4)), dma((4, n_head)), dma, dma, dma((7, n_head, 4)), dma((7, n_head, 4)),
             dma((7, 3)), dma((7, 3)), dma((7, max(extra, 1))), dma((7, max(extra, 1))),
             dma((3, 3 + extra + n_head)),
             dma((3, 3 + extra + n_head)), dma((n_head,)), dma((n_head,))),
            dma((10,)),
        ],
        compiler_params=pltpu.CompilerParams(
            collective_id=0, has_side_effects=True, vmem_limit_bytes=67043328
        ),
    )(memory_flags, document_start,
      (first_gain, first_shift, out_bias, second_gain, second_shift, down_bias),
      (query_bias, value_offset_bias, up_bias), (centre_weight, width_weight),
      layer_input, grad_output, memory_coefficients, att, up_weight, down_weight)
    return (
        y, dx, small[0], small[1],
        dqkv[0].T.astype(F32), small[7, :gcols], dqkv[1].T.astype(F32), dqkv[2].T.astype(F32), small[8, :gcols],
        dout[0].astype(F32),
        small[2], small[3], small[4],
        dmlp[0].astype(F32), small[6], dmlp[1].astype(F32), small[5],
        maps[0], maps[1],
    )


def solution(mesh):
    n_batch, n_head = mesh.shape["batch"], mesh.shape["head"]
    tokens = P(("batch", "head"), None)
    cols, rows, split, whole = P(None, "head"), P("head", None), P("head"), P()
    placed = (
        tokens, P("batch"), P("batch"), P("batch", None, None), whole, whole, cols, split, cols,
        cols, split, rows, whole, whole, whole, cols, split, rows, whole, rows, rows, tokens,
    )
    outs = (
        tokens, tokens, whole, whole, cols, split, cols, cols, split, rows, whole, whole, whole,
        cols, split, rows, whole, rows, rows,
    )
    return jax.shard_map(
        lambda *args: per_device(n_batch, n_head, *args),
        mesh=mesh, in_specs=placed, out_specs=outs, check_vma=False,
    )
```
